32 devices in a mesh: grp: 2 (over y), row: 8 (over z, x), tile: 2 (over core).
Axes of the slice: x: 2, y: 2, z: 4, core: 2. Of those that a mesh axis runs over, the one named last changes fastest.
Arguments:
- right_side: bfloat16 [16, 4096, 384], P(('grp', 'row'), 'tile'), parts along dimension 0, may hold values from -6 to 6
- diag_inverse: bfloat16 [3, 4096, 4096], P(None, ('row', 'tile')), may hold values from -0.09375 to 0.09375
- u_factor: bfloat16 [8, 3, 4096, 384], P('row', None, 'tile'), may hold values from -0.5 to 0.5
- v_factor: bfloat16 [8, 3, 4096, 384], P('row', None, 'tile'), may hold values from -0.09375 to 0.09375
- ranks: int32 [8, 3], P('row'), may hold values from 64 to 384, as said below
- pivots: int32 [3], replicated, may hold values from 0 to 7, as said below
Outputs:
- solution: bfloat16 [3, 8192, 384], P(None, ('grp', 'row', 'tile')), parts along dimension 1
- residual_out: float32 [16, 4096, 384], P(('grp', 'row'), 'tile'), parts along dimension 0
The draws below stay inside these ranges and needn't reach their ends.
There are 2 independent parts, one for each index of `grp`. The reference program is written for one: setup_inputs(seed, part) draws one part's arguments, and reference() takes and returns one part's arrays. A program takes and returns all parts, laid end to end along the dimension named above; an argument that names none is the same for every part. Nothing has to cross between parts.
Inputs may be any that keep to these rules, and one draw needn't show every extreme that they name: `ranks`: each entry is 384 // 6 times one of 1, 2, 3, 4, 6; in every draw some block row has rank 384 in every pivot column. `pivots`: distinct block rows of the strip; the first and the last block row are always among them, in an order drawn from the seed.
All inputs are finite; a program needn't handle non-finite values.
Results may differ from the reference program's by a relative error of at most 0.0085.
Values may be sent and summed in bfloat16 or wider, within the bound.
No kernel may reach another device: no remote copies, remote signals or barrier semaphores. Data moves between devices by JAX's collectives and lax.ppermute only.
A program may use at most 64 MiB of HBM per device.

```python
import jax
import jax.numpy as jnp
from jax import lax

BS = 4096
RMAX = 384
RHS = 384
PIVOTS = 3
BLOCKS = 8


def draw_ranks(key, part):
    draws = jax.random.randint(key, (BLOCKS, PIVOTS), 0, 20)
    levels = jnp.where(draws < 8, 1, jnp.where(draws < 15, 2, jnp.where(draws < 17, 3, jnp.where(draws < 19, 4, 6))))
    chosen = jax.random.randint(jax.random.fold_in(key, 7), (), 0, BLOCKS)
    levels = levels.at[chosen].set(6)
    return (levels * (RMAX // 6)).astype(jnp.int32)


def draw_pivots(key, part):
    middle = jax.random.permutation(jax.random.fold_in(key, 11), BLOCKS - 2)[:PIVOTS - 2].astype(jnp.int32) + 1
    ends = jnp.array([0, BLOCKS - 1], dtype=jnp.int32)
    chosen = jnp.concatenate([ends, middle])
    order = jax.random.permutation(jax.random.fold_in(key, 13), PIVOTS)
    return chosen[order].astype(jnp.int32)


def shard_levels(own_key, shape, split, least, top_value):
    def one(axis_at, parts):
        steps = jax.random.uniform(jax.random.fold_in(jax.random.fold_in(own_key, 6), axis_at), (parts,), jnp.float32, least / len(split), top_value / len(split))
        return jnp.repeat(jnp.exp(steps), shape[axis_at] // parts).reshape((-1,) + (1,) * (len(shape) - axis_at - 1))

    level = one(*split[0])
    for cut in split[1:]:
        level = level * one(*cut)
    return level


def noise(own_key, extent, width, bound, split=(), kind=jnp.bfloat16):
    factor_of = shard_levels(own_key, extent, split, -0.22, 0.18) if split else 1.0
    values = jax.random.normal(own_key, extent, jnp.float32) * width * factor_of
    return jnp.minimum(jnp.maximum(values, -bound), bound).astype(kind)


def setup_inputs(seed: int = 0, part: int = 0) -> dict:
    splits = jax.random.split(jax.random.key(seed), 7)
    own_keys = jax.random.split(jax.random.fold_in(splits[6], part), 7)
    right_side = noise(own_keys[0], (BLOCKS, BS, RHS), 1.0, 6.0, ((0, 8), (1, 2)))
    diag_inverse = noise(splits[1], (PIVOTS, BS, BS), BS ** -0.5, 0.09375, ((1, 16),))
    u_factor = noise(splits[2], (BLOCKS, PIVOTS, BS, RMAX), (RMAX // 3) ** -0.5, 0.5, ((0, 8), (2, 2)))
    v_factor = noise(splits[3], (BLOCKS, PIVOTS, BS, RMAX), BS ** -0.5, 0.09375, ((0, 8), (2, 2)))
    ranks = draw_ranks(jax.random.fold_in(splits[6], 71), part)
    pivots = draw_pivots(jax.random.fold_in(splits[6], 71), part)
    return dict(right_side=right_side, diag_inverse=diag_inverse, u_factor=u_factor, v_factor=v_factor, ranks=ranks, pivots=pivots)


def product(left, right):
    return jnp.dot(left.astype(jnp.float32), right.astype(jnp.float32), precision=lax.Precision.HIGHEST, preferred_element_type=jnp.float32)


def reference(right_side, diag_inverse, u_factor, v_factor, ranks, pivots):
    residual = right_side.astype(jnp.float32)
    columns = jnp.arange(RMAX, dtype=jnp.int32)[:, None]
    block_ids = jnp.arange(BLOCKS, dtype=jnp.int32)
    solved_list = []
    for step in range(PIVOTS):
        pivot_rhs = lax.dynamic_index_in_dim(residual, pivots[step].astype(jnp.int32), 0, keepdims=False).astype(jnp.bfloat16)
        unknowns = product(diag_inverse[step], pivot_rhs).astype(jnp.bfloat16)
        solved_list.append(unknowns)

        def per_block(item):
            v_block, u_block, rank_now = item
            coef = product(v_block.T, unknowns)
            coef = jnp.where(columns < rank_now, coef, jnp.float32(0.0)).astype(jnp.bfloat16)
            return product(u_block, coef)

        updates = lax.map(per_block, (v_factor[:, step], u_factor[:, step], ranks[:, step]))
        finished = jnp.any(block_ids[:, None] == pivots[None, :step + 1], axis=1)
        residual = residual - jnp.where(finished[:, None, None], jnp.float32(0.0), updates)
    return jnp.stack(solved_list), residual
```

```python
import jax
import jax.numpy as jnp
from jax import lax
from jax.sharding import PartitionSpec as P


SMALL_ROWS = 8
SWAP = [(0, 1), (1, 0)]
BF16 = jnp.bfloat16
F32 = jnp.float32


def ring_order(rows):
    return list(range(0, rows, 2)) + list(range(rows - 1, 0, -2))


def dot(a, b):
    return jnp.dot(a, b, preferred_element_type=F32)


def dot_t(a, b):
    return lax.dot_general(a, b, (((0,), (0,)), ((), ())), preferred_element_type=F32)


def gather_rows(piece, rows, place):
    if rows > SMALL_ROWS:
        return lax.all_gather(piece, "row", axis=0, tiled=True)
    ring = ring_order(rows)
    forward = [(ring[i], ring[(i + 1) % rows]) for i in range(rows)]
    backward = [(b, a) for a, b in forward]
    by_distance = [None] * rows
    by_distance[0] = piece
    down, up = piece, piece
    for hop in range(1, rows // 2 + 1):
        down = lax.ppermute(down, "row", forward)
        by_distance[hop] = down
        if hop < rows - hop:
            up = lax.ppermute(up, "row", backward)
            by_distance[rows - hop] = up
    stacked = jnp.stack(by_distance)
    places = jnp.array([ring.index(i) for i in range(rows)], jnp.int32)
    return jnp.concatenate(
        [lax.dynamic_index_in_dim(stacked, (place - places[i]) % rows, 0, keepdims=False) for i in range(rows)]
    )


def scatter_pieces(payload, rows, me, place, pivots):
    ring = ring_order(rows)
    ring_at = jnp.array(ring, jnp.int32)
    parts = [
        lax.dynamic_index_in_dim(payload, ring_at[(place + k) % rows], 1, keepdims=False) for k in range(rows)
    ]

    def send(holders, *values):
        return tuple(
            lax.ppermute(values[k - 1], "row", [(h, ring[(ring.index(h) + k) % rows]) for h in holders])
            for k in range(1, rows)
        )

    if rows <= SMALL_ROWS and pivots.shape[0] == 3:
        middle = jnp.sum(pivots) - (rows - 1)
        branches = [lambda *v, h=h: send((0, h, rows - 1), *v) for h in range(1, rows - 1)]
        got = lax.switch(middle - 1, branches, *parts[1:])
    else:
        got = send(tuple(range(rows)), *parts[1:])
    stacked = jnp.stack([parts[0], *got])
    places = jnp.array([ring.index(i) for i in range(rows)], jnp.int32)
    return [
        lax.dynamic_index_in_dim(stacked, (place - places[pivots[p]]) % rows, 0, keepdims=False)
        for p in range(pivots.shape[0])
    ]


def sum_all(value, rows, tile):
    half = value.shape[0] // 2
    mine = lax.dynamic_slice_in_dim(value, tile * half, half, 0)
    other = lax.dynamic_slice_in_dim(value, (1 - tile) * half, half, 0)
    mine = mine + lax.ppermute(other, "tile", SWAP)
    bit = 1
    while bit < rows:
        sent = lax.ppermute(mine.astype(BF16), "row", [(i, i ^ bit) for i in range(rows)])
        mine = mine + sent.astype(F32)
        bit *= 2
    mine = mine.astype(BF16)
    other = lax.ppermute(mine, "tile", SWAP)
    return jnp.where(tile == 0, jnp.concatenate([mine, other]), jnp.concatenate([other, mine]))


def solution(mesh):
    rows, groups = mesh.shape["row"], mesh.shape["grp"]

    def local(right_side, diag_inverse, u_factor, v_factor, ranks, pivots):
        steps = pivots.shape[0]
        me, tile, group = lax.axis_index("row"), lax.axis_index("tile"), lax.axis_index("grp")
        block = right_side[0]
        half, cols = block.shape
        width = u_factor.shape[3]
        n = half // rows
        ring = ring_order(rows)
        place = jnp.array([ring.index(i) for i in range(rows)], jnp.int32)[me]
        lanes = lax.broadcasted_iota(jnp.int32, (1, width), 1)

        v_pairs = v_factor[0].reshape(steps, rows // 2, 2, n, width)
        v_keep = lax.dynamic_index_in_dim(v_pairs, tile, 2, keepdims=False)
        v_give = lax.dynamic_index_in_dim(v_pairs, 1 - tile, 2, keepdims=False)
        v_take = lax.ppermute(v_give, "tile", SWAP)
        v_rows = jnp.where(
            tile == 0, jnp.concatenate([v_keep, v_take], 1), jnp.concatenate([v_take, v_keep], 1)
        )
        in_rank = lanes < ranks[0][:, None]
        v_rows = jnp.where(in_rank[:, None, None, :], v_rows, jnp.zeros_like(v_rows))

        d_keep = lax.dynamic_slice_in_dim(diag_inverse, tile * half, half, 2)
        d_give = lax.dynamic_slice_in_dim(diag_inverse, (1 - tile) * half, half, 2)
        d_take = lax.ppermute(d_give, "tile", SWAP)

        u_rows = u_factor[0, : steps - 1].reshape(steps - 1, rows, n, width)
        b_rows = block.reshape(1, rows, n, cols)
        v_sent = v_rows[: steps - 1]
        if groups == 2:
            payload = jnp.concatenate([b_rows, jnp.where(group == 0, v_sent, u_rows)])
        else:
            payload = jnp.concatenate([b_rows, v_sent, u_rows])
        held = scatter_pieces(payload, rows, me, place, pivots)
        pairs = [(p, q) for p in range(steps) for q in range(p)]
        if groups == 2:
            mine = jnp.stack([held[p][1 + q] for p, q in pairs])
            other = lax.ppermute(mine, "grp", SWAP)
            v_slice = jnp.where(group == 0, mine, other)
            u_slice = jnp.where(group == 0, other, mine)
        else:
            v_slice = jnp.stack([held[p][1 + q] for p, q in pairs])
            u_slice = jnp.stack([held[p][steps + q] for p, q in pairs])

        remaining = [held[p][0].astype(F32) for p in range(steps)]
        residual = block.astype(F32)
        solved = []
        for step in range(steps):
            pivot_half = gather_rows(remaining[step].astype(BF16), rows, place)
            mine = dot(d_keep[step], pivot_half)
            other = dot(d_take[step], pivot_half)
            x = (mine + lax.ppermute(other, "tile", SWAP)).astype(BF16)
            solved.append(x)
            x_all = lax.all_gather(x, "row", axis=0, tiled=True)
            for later in range(step + 1, steps):
                at = pairs.index((later, step))
                coef = sum_all(dot_t(v_slice[at], x), rows, tile)
                remaining[later] = remaining[later] - dot(u_slice[at], coef)
            part = dot_t(v_rows[step].reshape(half, width), x_all)
            coef = part + lax.ppermute(part, "tile", SWAP)
            finished = jnp.any(pivots[: step + 1] == me)
            coef = jnp.where(finished, F32(0.0), coef).astype(BF16)
            residual = residual - dot(u_factor[0, step], coef)
        return jnp.stack(solved), residual[None]

    in_specs = (
        P(("grp", "row"), "tile", None),
        P(None, ("row", "tile"), None),
        P("row", None, "tile", None),
        P("row", None, "tile", None),
        P("row", None),
        P(),
    )
    out_specs = (P(None, ("grp", "row", "tile"), None), P(("grp", "row"), "tile", None))
    return jax.shard_map(local, mesh=mesh, in_specs=in_specs, out_specs=out_specs, check_vma=False)
```

```python
import jax
import jax.numpy as jnp
from jax import lax
from jax.experimental import pallas as pl
from jax.experimental.pallas import tpu as pltpu
from jax.sharding import PartitionSpec as P


MOST_HOPS = 8
LANES = 128
SWAP = [(0, 1), (1, 0)]
BF16 = jnp.bfloat16
F32 = jnp.float32
VMEM_GRANT = 48 * 1024 * 1024


def ring_order(rows):
    return list(range(0, rows, 2)) + list(range(rows - 1, 0, -2))


def ring_place(index, rows):
    return jnp.where(index % 2 == 0, index // 2, rows - (index + 1) // 2)


def whole_specs(count):
    return [pl.BlockSpec(memory_space=pltpu.VMEM)] * count


def diag_product(where, own, take, pieces):
    rows = len(pieces)
    n, cols = pieces[0].shape
    half = rows * n

    def kernel(where_ref, own_ref, take_ref, *refs):
        piece_refs, (mine_ref, other_ref) = refs[:rows], refs[rows:]
        base, distance = where_ref[0] * half, where_ref[1]
        for k in range(rows):
            at = lax.rem(distance - k + rows, rows) * n
            piece = piece_refs[k][...]
            mine = jnp.dot(
                own_ref[:, pl.ds(pl.multiple_of(base + at, n), n)], piece, preferred_element_type=F32
            )
            other = jnp.dot(take_ref[:, pl.ds(pl.multiple_of(at, n), n)], piece, preferred_element_type=F32)
            if k == 0:
                mine_ref[...] = mine
                other_ref[...] = other
            else:
                mine_ref[...] += mine
                other_ref[...] += other

    out = jax.ShapeDtypeStruct((n, cols), F32)
    return pl.pallas_call(
        kernel,
        out_shape=(out, out),
        in_specs=[pl.BlockSpec(memory_space=pltpu.SMEM)] + whole_specs(2 + rows),
        out_specs=tuple(whole_specs(2)),
        compiler_params=pltpu.CompilerParams(vmem_limit_bytes=VMEM_GRANT),
        cost_estimate=pl.CostEstimate(flops=4 * n * half * cols, bytes_accessed=8 * n * half, transcendentals=0),
        name="diag_product",
    )(where, own, take, *pieces)


def coef_product(order, v_pieces, pieces):
    rows, n, width = v_pieces.shape
    cols = pieces[0].shape[1]

    def kernel(order_ref, v_ref, *refs):
        piece_refs, out_ref = refs[:rows], refs[rows]
        for k in range(rows):
            part = lax.dot_general(
                v_ref[order_ref[k]], piece_refs[k][...], (((0,), (0,)), ((), ())), preferred_element_type=F32
            )
            if k == 0:
                out_ref[...] = part
            else:
                out_ref[...] += part

    return pl.pallas_call(
        kernel,
        out_shape=jax.ShapeDtypeStruct((width, cols), F32),
        in_specs=[pl.BlockSpec(memory_space=pltpu.SMEM)] + whole_specs(1 + rows),
        out_specs=whole_specs(1)[0],
        compiler_params=pltpu.CompilerParams(vmem_limit_bytes=VMEM_GRANT),
        cost_estimate=pl.CostEstimate(
            flops=2 * rows * n * width * cols, bytes_accessed=4 * rows * n * width, transcendentals=0
        ),
        name="coef_product",
    )(order, v_pieces, *pieces)


def ring_steps(rows, half, n):
    ring = ring_order(rows)
    forward = [(ring[i], ring[(i + 1) % rows]) for i in range(rows)]
    backward = [(b, a) for a, b in forward]
    reach = rows // 2

    def gather(piece):
        got = [None] * rows
        got[0] = down = up = piece
        for hop in range(1, reach + 1):
            got[hop] = down = lax.ppermute(down, "row", forward)
            if hop < rows - hop:
                got[rows - hop] = up = lax.ppermute(up, "row", backward)
        return got

    def scatter(block, is_holder, distance):
        pieces = [block[d * n : (d + 1) * n] for d in range(rows)]
        down = up = None
        for far in range(reach, 0, -1):
            give = pieces[far] if down is None else jnp.where(is_holder, pieces[far], down)
            down = lax.ppermute(give, "row", forward)
            if far < rows - far:
                give = pieces[rows - far] if up is None else jnp.where(is_holder, pieces[rows - far], up)
                up = lax.ppermute(give, "row", backward)
        away = down if up is None else jnp.where(distance <= reach, down, up)
        return jnp.where(is_holder, pieces[0], away)

    def local(right_side, diag_inverse, u_factor, v_factor, ranks, pivots):
        steps = pivots.shape[0]
        me, tile = lax.axis_index("row"), lax.axis_index("tile")
        block = right_side[0]
        width = u_factor.shape[3]
        place = ring_place(me, rows)
        distances = lax.rem(place - ring_place(pivots, rows) + rows, rows)
        heights = lax.broadcasted_iota(jnp.int32, (width, 1), 0)

        orders = [
            [[(ring[(ring.index(j) - k) % rows] + t * reach) % rows for k in range(rows)] for j in range(rows)]
            for t in range(2)
        ]
        order = lax.dynamic_slice(
            jnp.array(orders, jnp.int32).reshape(2 * rows, rows), (tile * rows + me, 0), (1, rows)
        )[0]

        d_give = lax.dynamic_slice_in_dim(diag_inverse, (1 - tile) * half, half, 2)
        v_pairs = v_factor[0].reshape(steps, reach, 2, n, width)
        v_keep = lax.dynamic_index_in_dim(v_pairs, tile, 2, keepdims=False)
        v_give = lax.dynamic_index_in_dim(v_pairs, 1 - tile, 2, keepdims=False)
        d_take = [lax.ppermute(d_give[p], "tile", SWAP) for p in range(steps)]
        v_take = lax.ppermute(v_give, "tile", SWAP)
        v_pieces = jnp.concatenate([v_keep, v_take], 1)

        residual = block.astype(F32)
        finished = jnp.bool_(False)
        solved = []
        for step in range(steps):
            is_holder = pivots[step] == me
            piece = scatter(residual.astype(BF16), is_holder, distances[step])
            pieces = gather(piece)
            where = jnp.stack([tile, distances[step]])
            mine, other = diag_product(where, diag_inverse[step], d_take[step], pieces)
            x = (mine + lax.ppermute(other, "tile", SWAP)).astype(BF16)
            solved.append(x)
            part = coef_product(order, v_pieces[step], gather(x))
            coef = part + lax.ppermute(part, "tile", SWAP)
            finished = finished | is_holder
            kept = jnp.where(finished, 0, ranks[0, step])
            coef = jnp.where(heights < kept, coef, F32(0.0)).astype(BF16)
            residual = residual - jnp.dot(u_factor[0, step], coef, preferred_element_type=F32)
        return jnp.stack(solved), residual[None]

    return local


def gathered_steps(right_side, diag_inverse, u_factor, v_factor, ranks, pivots):
    residual = right_side[0].astype(F32)
    half = residual.shape[0]
    heights = lax.broadcasted_iota(jnp.int32, (u_factor.shape[3], 1), 0)
    me, tile = lax.axis_index("row"), lax.axis_index("tile")
    solved = []
    for step in range(pivots.shape[0]):
        current = residual.astype(BF16)
        held = lax.psum(jnp.where(me == pivots[step], current, jnp.zeros_like(current)), "row")
        other = lax.ppermute(held, "tile", SWAP)
        pivot = jnp.where(tile == 0, jnp.concatenate([held, other]), jnp.concatenate([other, held]))
        x = jnp.dot(diag_inverse[step], pivot, preferred_element_type=F32).astype(BF16)
        solved.append(x)
        x_all = lax.all_gather(x, ("row", "tile"), axis=0, tiled=True)
        x_mine = lax.dynamic_slice_in_dim(x_all, tile * half, half, 0)
        part = lax.dot_general(
            v_factor[0, step], x_mine, (((0,), (0,)), ((), ())), preferred_element_type=F32
        )
        coef = part + lax.ppermute(part, "tile", SWAP)
        finished = jnp.any(pivots[: step + 1] == me)
        kept = jnp.where(finished, 0, ranks[0, step])
        coef = jnp.where(heights < kept, coef, F32(0.0)).astype(BF16)
        residual = residual - jnp.dot(u_factor[0, step], coef, preferred_element_type=F32)
    return jnp.stack(solved), residual[None]


def solution(mesh):
    rows = mesh.shape["row"]

    def local(right_side, diag_inverse, *others):
        half, n = right_side.shape[1], diag_inverse.shape[1]
        short = rows % 2 == 0 and rows <= MOST_HOPS and n % LANES == 0 and half == rows * n
        run = ring_steps(rows, half, n) if short else gathered_steps
        return run(right_side, diag_inverse, *others)

    in_specs = (
        P(("grp", "row"), "tile", None),
        P(None, ("row", "tile"), None),
        P("row", None, "tile", None),
        P("row", None, "tile", None),
        P("row", None),
        P(),
    )
    out_specs = (P(None, ("grp", "row", "tile"), None), P(("grp", "row"), "tile", None))
    return jax.shard_map(local, mesh=mesh, in_specs=in_specs, out_specs=out_specs, check_vma=False)
```

```python
import jax
import jax.numpy as jnp
from jax import lax
from jax.experimental import pallas as pl
from jax.experimental.pallas import tpu as pltpu
from jax.sharding import PartitionSpec as P


MOST_HOPS = 8
LANES = 128
SWAP = [(0, 1), (1, 0)]
BF16 = jnp.bfloat16
F32 = jnp.float32
VMEM_GRANT = 16 * 1024 * 1024


def ring_order(rows):
    return list(range(0, rows, 2)) + list(range(rows - 1, 0, -2))


def ring_place(index, rows):
    return jnp.where(index % 2 == 0, index // 2, rows - (index + 1) // 2)


def whole_specs(count):
    return [pl.BlockSpec(memory_space=pltpu.VMEM)] * count


def diag_product(where, own, take, pieces):
    rows = len(pieces)
    n, cols = pieces[0].shape
    half = rows * n

    def kernel(where_ref, own_ref, take_ref, *refs):
        piece_refs, (mine_ref, other_ref) = refs[:rows], refs[rows:]
        base, distance = where_ref[0] * half, where_ref[1]
        for k in range(rows):
            at = lax.rem(distance - k + rows, rows) * n
            piece = piece_refs[k][...]
            mine = jnp.dot(
                own_ref[:, pl.ds(pl.multiple_of(base + at, n), n)], piece, preferred_element_type=F32
            )
            other = jnp.dot(take_ref[:, pl.ds(pl.multiple_of(at, n), n)], piece, preferred_element_type=F32)
            if k == 0:
                mine_ref[...] = mine
                other_ref[...] = other
            else:
                mine_ref[...] += mine
                other_ref[...] += other

    out = jax.ShapeDtypeStruct((n, cols), F32)
    return pl.pallas_call(
        kernel,
        out_shape=(out, out),
        in_specs=[pl.BlockSpec(memory_space=pltpu.SMEM)] + whole_specs(2 + rows),
        out_specs=tuple(whole_specs(2)),
        compiler_params=pltpu.CompilerParams(vmem_limit_bytes=VMEM_GRANT),
        cost_estimate=pl.CostEstimate(flops=4 * n * half * cols, bytes_accessed=8 * n * half, transcendentals=0),
        name="diag_product",
    )(where, own, take, *pieces)


def coef_product(order, v_pieces, pieces):
    rows, n, width = v_pieces.shape
    cols = pieces[0].shape[1]

    def kernel(order_ref, v_ref, *refs):
        piece_refs, out_ref = refs[:rows], refs[rows]
        for k in range(rows):
            part = lax.dot_general(
                v_ref[order_ref[k]], piece_refs[k][...], (((0,), (0,)), ((), ())), preferred_element_type=F32
            )
            if k == 0:
                out_ref[...] = part
            else:
                out_ref[...] += part

    return pl.pallas_call(
        kernel,
        out_shape=jax.ShapeDtypeStruct((width, cols), F32),
        in_specs=[pl.BlockSpec(memory_space=pltpu.SMEM)] + whole_specs(1 + rows),
        out_specs=whole_specs(1)[0],
        compiler_params=pltpu.CompilerParams(vmem_limit_bytes=VMEM_GRANT),
        cost_estimate=pl.CostEstimate(
            flops=2 * rows * n * width * cols, bytes_accessed=4 * rows * n * width, transcendentals=0
        ),
        name="coef_product",
    )(order, v_pieces, *pieces)


def pick(is_holder, own, received):
    count = len(own)
    shape = jax.ShapeDtypeStruct(own[0].shape, own[0].dtype)

    def kernel(holder_ref, *refs):
        own_refs, got_refs, out_refs = refs[:count], refs[count : 2 * count], refs[2 * count :]
        held = holder_ref[0] == 1

        @pl.when(held)
        def _():
            for i in range(count):
                out_refs[i][...] = own_refs[i][...]

        @pl.when(jnp.logical_not(held))
        def _():
            for i in range(count):
                out_refs[i][...] = got_refs[i][...]

    return pl.pallas_call(
        kernel,
        out_shape=(shape,) * count,
        in_specs=[pl.BlockSpec(memory_space=pltpu.SMEM)] + whole_specs(2 * count),
        out_specs=tuple(whole_specs(count)),
        compiler_params=pltpu.CompilerParams(vmem_limit_bytes=VMEM_GRANT),
        name="pick",
    )(is_holder, *own, *received)


def arrive(where, reach, own, down, up):
    def kernel(where_ref, own_ref, down_ref, up_ref, out_ref):
        distance = where_ref[1]
        for near, ref in ((distance == 0, own_ref), (distance > reach, up_ref)):

            @pl.when(near)
            def _(ref=ref):
                out_ref[...] = ref[...]

        @pl.when(jnp.logical_and(distance > 0, distance <= reach))
        def _():
            out_ref[...] = down_ref[...]

    return pl.pallas_call(
        kernel,
        out_shape=jax.ShapeDtypeStruct(own.shape, own.dtype),
        in_specs=[pl.BlockSpec(memory_space=pltpu.SMEM)] + whole_specs(3),
        out_specs=whole_specs(1)[0],
        compiler_params=pltpu.CompilerParams(vmem_limit_bytes=VMEM_GRANT),
        name="arrive",
    )(where, own, down, up)


def update(step, kept, part, taken, block, factors, coefs, n, last):
    half, cols = block.shape
    width = part.shape[0]
    rows = half // n
    before = len(coefs)

    def kernel(kept_ref, part_ref, taken_ref, block_ref, *refs):
        u_refs, c_refs, out_refs = refs[: before + 1], refs[before + 1 : 2 * before + 1], refs[2 * before + 1 :]
        heights = lax.broadcasted_iota(jnp.int32, (width, cols), 0)
        total = part_ref[...] + taken_ref[...]
        coef = jnp.where(heights < kept_ref[step], total, 0.0).astype(BF16)
        if not last:
            out_refs[-1][...] = coef
        for i in range(rows):
            span = slice(i * n, (i + 1) * n)
            value = block_ref[span, :].astype(F32)
            for u_ref, c_ref in zip(u_refs, c_refs):
                value -= jnp.dot(u_ref[span, :], c_ref[...], preferred_element_type=F32)
            value -= jnp.dot(u_refs[before][span, :], coef, preferred_element_type=F32)
            if last:
                out_refs[0][span, :] = value
            else:
                out_refs[i][...] = value.astype(BF16)

    piece = jax.ShapeDtypeStruct((n, cols), BF16)
    if last:
        out_shape = (jax.ShapeDtypeStruct((half, cols), F32),)
    else:
        out_shape = (piece,) * rows + (jax.ShapeDtypeStruct((width, cols), BF16),)
    return pl.pallas_call(
        kernel,
        out_shape=out_shape,
        in_specs=[pl.BlockSpec(memory_space=pltpu.SMEM)] + whole_specs(4 + 2 * before),
        out_specs=tuple(whole_specs(len(out_shape))),
        compiler_params=pltpu.CompilerParams(vmem_limit_bytes=VMEM_GRANT),
        cost_estimate=pl.CostEstimate(
            flops=2 * (before + 1) * half * width * cols,
            bytes_accessed=2 * (before + 2) * half * cols,
            transcendentals=0,
        ),
        name="update",
    )(kept, part, taken, block, *factors, *coefs)


def ring_steps(rows, half, n):
    ring = ring_order(rows)
    forward = [(ring[i], ring[(i + 1) % rows]) for i in range(rows)]
    backward = [(b, a) for a, b in forward]
    reach = rows // 2

    def gather(piece):
        got = [None] * rows
        got[0] = down = up = piece
        for hop in range(1, reach + 1):
            got[hop] = down = lax.ppermute(down, "row", forward)
            if hop < rows - hop:
                got[rows - hop] = up = lax.ppermute(up, "row", backward)
        return got

    def scatter(pieces, is_holder, where):
        down, up = pieces[reach], None
        for far in range(reach, 0, -1):
            if far == reach - 1:
                (down,), up = pick(is_holder, [pieces[far]], [down]), pieces[rows - far]
            elif far < reach - 1:
                down, up = pick(is_holder, [pieces[far], pieces[rows - far]], [down, up])
            down = lax.ppermute(down, "row", forward)
            if up is not None:
                up = lax.ppermute(up, "row", backward)
        return arrive(where, reach, pieces[0], down, down if up is None else up)

    def local(right_side, diag_inverse, u_factor, v_factor, ranks, pivots):
        steps = pivots.shape[0]
        me, tile = lax.axis_index("row"), lax.axis_index("tile")
        block = right_side[0]
        distances = lax.rem(ring_place(me, rows) - ring_place(pivots, rows) + rows, rows)
        wheres = jnp.stack([jnp.full_like(distances, tile), distances], 1)
        holders = (pivots == me).astype(jnp.int32)
        kept = jnp.where(jnp.cumsum(holders) > 0, 0, ranks[0])

        orders = [
            [[(ring[(ring.index(j) - k) % rows] + t * reach) % rows for k in range(rows)] for j in range(rows)]
            for t in range(2)
        ]
        order = lax.dynamic_slice(
            jnp.array(orders, jnp.int32).reshape(2 * rows, rows), (tile * rows + me, 0), (1, rows)
        )[0]

        width = u_factor.shape[3]
        d_give = lax.dynamic_slice_in_dim(diag_inverse, (1 - tile) * half, half, 2)
        v_pairs = v_factor[0].reshape(steps, reach, 2, n, width)
        v_keep = lax.dynamic_index_in_dim(v_pairs, tile, 2, keepdims=False)
        v_give = lax.dynamic_index_in_dim(v_pairs, 1 - tile, 2, keepdims=False)
        d_take = [lax.ppermute(d_give[p], "tile", SWAP) for p in range(steps)]
        v_take = lax.ppermute(v_give, "tile", SWAP)
        v_pieces = jnp.concatenate([v_keep, v_take], 1)

        pieces = [block[d * n : (d + 1) * n] for d in range(rows)]
        factors, coefs, solved = [], [], []
        for step in range(steps):
            got = gather(scatter(pieces, holders[step : step + 1], wheres[step]))
            mine, other = diag_product(wheres[step], diag_inverse[step], d_take[step], got)
            x = (mine + lax.ppermute(other, "tile", SWAP)).astype(BF16)
            solved.append(x)
            part = coef_product(order, v_pieces[step], gather(x))
            taken = lax.ppermute(part, "tile", SWAP)
            factors.append(u_factor[0, step])
            *pieces, coef = update(step, kept, part, taken, block, factors, coefs, n, step == steps - 1)
            coefs.append(coef)
        return jnp.stack(solved), coefs[-1][None]

    return local


def gathered_steps(right_side, diag_inverse, u_factor, v_factor, ranks, pivots):
    residual = right_side[0].astype(F32)
    half = residual.shape[0]
    heights = lax.broadcasted_iota(jnp.int32, (u_factor.shape[3], 1), 0)
    me, tile = lax.axis_index("row"), lax.axis_index("tile")
    solved = []
    for step in range(pivots.shape[0]):
        current = residual.astype(BF16)
        held = lax.psum(jnp.where(me == pivots[step], current, jnp.zeros_like(current)), "row")
        other = lax.ppermute(held, "tile", SWAP)
        pivot = jnp.where(tile == 0, jnp.concatenate([held, other]), jnp.concatenate([other, held]))
        x = jnp.dot(diag_inverse[step], pivot, preferred_element_type=F32).astype(BF16)
        solved.append(x)
        x_all = lax.all_gather(x, ("row", "tile"), axis=0, tiled=True)
        x_mine = lax.dynamic_slice_in_dim(x_all, tile * half, half, 0)
        part = lax.dot_general(
            v_factor[0, step], x_mine, (((0,), (0,)), ((), ())), preferred_element_type=F32
        )
        coef = part + lax.ppermute(part, "tile", SWAP)
        finished = jnp.any(pivots[: step + 1] == me)
        kept = jnp.where(finished, 0, ranks[0, step])
        coef = jnp.where(heights < kept, coef, F32(0.0)).astype(BF16)
        residual = residual - jnp.dot(u_factor[0, step], coef, preferred_element_type=F32)
    return jnp.stack(solved), residual[None]


def solution(mesh):
    rows = mesh.shape["row"]

    def local(right_side, diag_inverse, *others):
        half, n = right_side.shape[1], diag_inverse.shape[1]
        short = rows % 2 == 0 and rows <= MOST_HOPS and n % LANES == 0 and half == rows * n
        run = ring_steps(rows, half, n) if short else gathered_steps
        return run(right_side, diag_inverse, *others)

    in_specs = (
        P(("grp", "row"), "tile", None),
        P(None, ("row", "tile"), None),
        P("row", None, "tile", None),
        P("row", None, "tile", None),
        P("row", None),
        P(),
    )
    out_specs = (P(None, ("grp", "row", "tile"), None), P(("grp", "row"), "tile", None))
    return jax.shard_map(local, mesh=mesh, in_specs=in_specs, out_specs=out_specs, check_vma=False)
```

```python
import jax
import jax.numpy as jnp
from jax import lax
from jax.experimental import pallas as pl
from jax.experimental.pallas import tpu as pltpu
from jax.sharding import PartitionSpec as P


MOST_HOPS = 8
LANES = 128
SWAP = [(0, 1), (1, 0)]
BF16 = jnp.bfloat16
F32 = jnp.float32
VMEM_GRANT = 16 * 1024 * 1024


def ring_order(rows):
    return list(range(0, rows, 2)) + list(range(rows - 1, 0, -2))


def ring_place(index, rows):
    return jnp.where(index % 2 == 0, index // 2, rows - (index + 1) // 2)


def whole_specs(count):
    return [pl.BlockSpec(memory_space=pltpu.VMEM)] * count


def diag_product(where, own, take, pieces, downs, ups):
    rows, hops = len(pieces), len(downs)
    n, cols = pieces[0].shape
    half = rows * n

    def kernel(where_ref, own_ref, take_ref, *refs):
        piece_refs, refs = refs[:rows], refs[rows:]
        down_refs, up_refs, (mine_ref, other_ref, whole_ref) = refs[:hops], refs[hops : 2 * hops], refs[2 * hops :]
        distance = where_ref[1]

        @pl.when(distance == 0)
        def _():
            for i in range(rows):
                whole_ref[i * n : (i + 1) * n, :] = piece_refs[i][...]

        for hop in range(1, hops + 1):

            @pl.when(jnp.logical_and(distance > 0, distance <= hop))
            def _(hop=hop):
                at = pl.multiple_of((hop - distance) * n, n)
                whole_ref[pl.ds(at, n), :] = down_refs[hop - 1][...]

            @pl.when(jnp.logical_and(distance > 0, distance >= rows - hop))
            def _(hop=hop):
                at = pl.multiple_of((2 * rows - 1 - hop - distance) * n, n)
                whole_ref[pl.ds(at, n), :] = up_refs[hop - 1][...]

        base = pl.multiple_of(where_ref[0] * half, half)
        whole = whole_ref[...]
        mine_ref[...] = jnp.dot(own_ref[:, pl.ds(base, half)], whole, preferred_element_type=F32)
        other_ref[...] = jnp.dot(take_ref[...], whole, preferred_element_type=F32)

    out = jax.ShapeDtypeStruct((n, cols), F32)
    return pl.pallas_call(
        kernel,
        out_shape=(out, out),
        in_specs=[pl.BlockSpec(memory_space=pltpu.SMEM)] + whole_specs(2 + rows + 2 * hops),
        out_specs=tuple(whole_specs(2)),
        scratch_shapes=[pltpu.VMEM((half, cols), BF16)],
        compiler_params=pltpu.CompilerParams(vmem_limit_bytes=VMEM_GRANT),
        cost_estimate=pl.CostEstimate(flops=4 * n * half * cols, bytes_accessed=8 * n * half, transcendentals=0),
        name="diag_product",
    )(where, own, take, *pieces, *downs, *ups)


def coef_product(order, v_pieces, pieces):
    rows, n, width = v_pieces.shape
    cols = pieces[0].shape[1]

    def kernel(order_ref, v_ref, *refs):
        piece_refs, out_ref = refs[:rows], refs[rows]
        for k in range(rows):
            part = lax.dot_general(
                v_ref[order_ref[k]], piece_refs[k][...], (((0,), (0,)), ((), ())), preferred_element_type=F32
            )
            if k == 0:
                out_ref[...] = part
            else:
                out_ref[...] += part

    return pl.pallas_call(
        kernel,
        out_shape=jax.ShapeDtypeStruct((width, cols), F32),
        in_specs=[pl.BlockSpec(memory_space=pltpu.SMEM)] + whole_specs(1 + rows),
        out_specs=whole_specs(1)[0],
        compiler_params=pltpu.CompilerParams(vmem_limit_bytes=VMEM_GRANT),
        cost_estimate=pl.CostEstimate(
            flops=2 * rows * n * width * cols, bytes_accessed=4 * rows * n * width, transcendentals=0
        ),
        name="coef_product",
    )(order, v_pieces, *pieces)


def pick(is_holder, own, received):
    count = len(own)
    shape = jax.ShapeDtypeStruct(own[0].shape, own[0].dtype)

    def kernel(holder_ref, *refs):
        own_refs, got_refs, out_refs = refs[:count], refs[count : 2 * count], refs[2 * count :]
        held = holder_ref[0] == 1

        @pl.when(held)
        def _():
            for i in range(count):
                out_refs[i][...] = own_refs[i][...]

        @pl.when(jnp.logical_not(held))
        def _():
            for i in range(count):
                out_refs[i][...] = got_refs[i][...]

    return pl.pallas_call(
        kernel,
        out_shape=(shape,) * count,
        in_specs=[pl.BlockSpec(memory_space=pltpu.SMEM)] + whole_specs(2 * count),
        out_specs=tuple(whole_specs(count)),
        compiler_params=pltpu.CompilerParams(vmem_limit_bytes=VMEM_GRANT),
        name="pick",
    )(is_holder, *own, *received)


def update(step, kept, part, taken, block, factors, coefs, n, last):
    half, cols = block.shape
    width = part.shape[0]
    rows = half // n
    before = len(coefs)

    def kernel(kept_ref, part_ref, taken_ref, block_ref, *refs):
        u_refs, c_refs, out_refs = refs[: before + 1], refs[before + 1 : 2 * before + 1], refs[2 * before + 1 :]
        heights = lax.broadcasted_iota(jnp.int32, (width, cols), 0)
        total = part_ref[...] + taken_ref[...]
        coef = jnp.where(heights < kept_ref[step], total, 0.0).astype(BF16)
        if not last:
            out_refs[-1][...] = coef
        for i in range(rows):
            span = slice(i * n, (i + 1) * n)
            value = block_ref[span, :].astype(F32)
            for u_ref, c_ref in zip(u_refs, c_refs):
                value -= jnp.dot(u_ref[span, :], c_ref[...], preferred_element_type=F32)
            value -= jnp.dot(u_refs[before][span, :], coef, preferred_element_type=F32)
            if last:
                out_refs[0][span, :] = value
            else:
                out_refs[i][...] = value.astype(BF16)

    piece = jax.ShapeDtypeStruct((n, cols), BF16)
    if last:
        out_shape = (jax.ShapeDtypeStruct((half, cols), F32),)
    else:
        out_shape = (piece,) * rows + (jax.ShapeDtypeStruct((width, cols), BF16),)
    return pl.pallas_call(
        kernel,
        out_shape=out_shape,
        in_specs=[pl.BlockSpec(memory_space=pltpu.SMEM)] + whole_specs(4 + 2 * before),
        out_specs=tuple(whole_specs(len(out_shape))),
        compiler_params=pltpu.CompilerParams(vmem_limit_bytes=VMEM_GRANT),
        cost_estimate=pl.CostEstimate(
            flops=2 * (before + 1) * half * width * cols,
            bytes_accessed=2 * (before + 2) * half * cols,
            transcendentals=0,
        ),
        name="update",
    )(kept, part, taken, block, *factors, *coefs)


def ring_steps(rows, half, n):
    ring = ring_order(rows)
    forward = [(ring[i], ring[(i + 1) % rows]) for i in range(rows)]
    backward = [(b, a) for a, b in forward]
    reach = rows // 2

    def gather(piece):
        got = [None] * rows
        got[0] = down = up = piece
        for hop in range(1, reach + 1):
            got[hop] = down = lax.ppermute(down, "row", forward)
            if hop < rows - hop:
                got[rows - hop] = up = lax.ppermute(up, "row", backward)
        return got

    def spread(pieces, is_holder):
        downs, ups = [], []
        for hop in range(rows - 1):
            down, up = pieces[hop], pieces[rows - 1 - hop]
            if hop:
                down, up = pick(is_holder, [down, up], [downs[-1], ups[-1]])
            downs.append(lax.ppermute(down, "row", forward))
            ups.append(lax.ppermute(up, "row", backward))
        return downs, ups

    def local(right_side, diag_inverse, u_factor, v_factor, ranks, pivots):
        steps = pivots.shape[0]
        me, tile = lax.axis_index("row"), lax.axis_index("tile")
        block = right_side[0]
        distances = lax.rem(ring_place(me, rows) - ring_place(pivots, rows) + rows, rows)
        wheres = jnp.stack([jnp.full_like(distances, tile), distances], 1)
        holders = (pivots == me).astype(jnp.int32)
        kept = jnp.where(jnp.cumsum(holders) > 0, 0, ranks[0])

        orders = [
            [[(ring[(ring.index(j) - k) % rows] + t * reach) % rows for k in range(rows)] for j in range(rows)]
            for t in range(2)
        ]
        order = lax.dynamic_slice(
            jnp.array(orders, jnp.int32).reshape(2 * rows, rows), (tile * rows + me, 0), (1, rows)
        )[0]

        width = u_factor.shape[3]
        d_give = lax.dynamic_slice_in_dim(diag_inverse, (1 - tile) * half, half, 2)
        v_pairs = v_factor[0].reshape(steps, reach, 2, n, width)
        v_keep = lax.dynamic_index_in_dim(v_pairs, tile, 2, keepdims=False)
        v_give = lax.dynamic_index_in_dim(v_pairs, 1 - tile, 2, keepdims=False)
        d_take = [lax.ppermute(d_give[p], "tile", SWAP) for p in range(steps)]
        v_take = lax.ppermute(v_give, "tile", SWAP)
        v_pieces = jnp.concatenate([v_keep, v_take], 1)

        pieces = [block[d * n : (d + 1) * n] for d in range(rows)]
        factors, coefs, solved = [], [], []
        for step in range(steps):
            downs, ups = spread(pieces, holders[step : step + 1])
            mine, other = diag_product(wheres[step], diag_inverse[step], d_take[step], pieces, downs, ups)
            x = (mine + lax.ppermute(other, "tile", SWAP)).astype(BF16)
            solved.append(x)
            part = coef_product(order, v_pieces[step], gather(x))
            taken = lax.ppermute(part, "tile", SWAP)
            factors.append(u_factor[0, step])
            *pieces, coef = update(step, kept, part, taken, block, factors, coefs, n, step == steps - 1)
            coefs.append(coef)
        return jnp.stack(solved), coefs[-1][None]

    return local


def gathered_steps(right_side, diag_inverse, u_factor, v_factor, ranks, pivots):
    residual = right_side[0].astype(F32)
    half = residual.shape[0]
    heights = lax.broadcasted_iota(jnp.int32, (u_factor.shape[3], 1), 0)
    me, tile = lax.axis_index("row"), lax.axis_index("tile")
    solved = []
    for step in range(pivots.shape[0]):
        current = residual.astype(BF16)
        held = lax.psum(jnp.where(me == pivots[step], current, jnp.zeros_like(current)), "row")
        other = lax.ppermute(held, "tile", SWAP)
        pivot = jnp.where(tile == 0, jnp.concatenate([held, other]), jnp.concatenate([other, held]))
        x = jnp.dot(diag_inverse[step], pivot, preferred_element_type=F32).astype(BF16)
        solved.append(x)
        x_all = lax.all_gather(x, ("row", "tile"), axis=0, tiled=True)
        x_mine = lax.dynamic_slice_in_dim(x_all, tile * half, half, 0)
        part = lax.dot_general(
            v_factor[0, step], x_mine, (((0,), (0,)), ((), ())), preferred_element_type=F32
        )
        coef = part + lax.ppermute(part, "tile", SWAP)
        finished = jnp.any(pivots[: step + 1] == me)
        kept = jnp.where(finished, 0, ranks[0, step])
        coef = jnp.where(heights < kept, coef, F32(0.0)).astype(BF16)
        residual = residual - jnp.dot(u_factor[0, step], coef, preferred_element_type=F32)
    return jnp.stack(solved), residual[None]


def solution(mesh):
    rows = mesh.shape["row"]

    def local(right_side, diag_inverse, *others):
        half, n = right_side.shape[1], diag_inverse.shape[1]
        short = rows % 2 == 0 and rows <= MOST_HOPS and n % LANES == 0 and half == rows * n
        run = ring_steps(rows, half, n) if short else gathered_steps
        return run(right_side, diag_inverse, *others)

    in_specs = (
        P(("grp", "row"), "tile", None),
        P(None, ("row", "tile"), None),
        P("row", None, "tile", None),
        P("row", None, "tile", None),
        P("row", None),
        P(),
    )
    out_specs = (P(None, ("grp", "row", "tile"), None), P(("grp", "row"), "tile", None))
    return jax.shard_map(local, mesh=mesh, in_specs=in_specs, out_specs=out_specs, check_vma=False)
```

```python
import jax
import jax.numpy as jnp
from jax import lax
from jax.experimental import pallas as pl
from jax.experimental.pallas import tpu as pltpu
from jax.sharding import PartitionSpec as P


MOST_HOPS = 8
LANES = 128
SWAP = [(0, 1), (1, 0)]
BF16 = jnp.bfloat16
F32 = jnp.float32
VMEM_GRANT = 16 * 1024 * 1024


def ring_order(rows):
    return list(range(0, rows, 2)) + list(range(rows - 1, 0, -2))


def ring_place(index, rows):
    return jnp.where(index % 2 == 0, index // 2, rows - (index + 1) // 2)


def whole_specs(count):
    return [pl.BlockSpec(memory_space=pltpu.VMEM)] * count


def in_hbm(count):
    return [pl.BlockSpec(memory_space=pltpu.HBM)] * count


def diag_product(step, where, diag, diag_other, held, downs, ups):
    hops = len(downs)
    rows = hops + 1
    n, cols = downs[0].shape
    half = rows * n

    def kernel(where_ref, diag_ref, diag_other_ref, held_ref, *refs):
        down_refs, up_refs, refs = refs[:hops], refs[hops : 2 * hops], refs[2 * hops :]
        mine_ref, other_ref, whole_ref, own_ref, take_ref, sems = refs
        base = pl.multiple_of(where_ref[0] * half, half)
        fetches = [
            pltpu.make_async_copy(source.at[step, :, pl.ds(base, half)], target, sems.at[i])
            for i, (source, target) in enumerate(((diag_other_ref, take_ref), (diag_ref, own_ref)))
        ]
        for fetch in fetches:
            fetch.start()
        distance = where_ref[1]

        @pl.when(distance == 0)
        def _():
            whole_ref[...] = held_ref[...]

        for hop in range(1, hops + 1):

            @pl.when(jnp.logical_and(distance > 0, distance <= hop))
            def _(hop=hop):
                at = pl.multiple_of((hop - distance) * n, n)
                whole_ref[pl.ds(at, n), :] = down_refs[hop - 1][...]

            @pl.when(jnp.logical_and(distance > 0, distance >= rows - hop))
            def _(hop=hop):
                at = pl.multiple_of((2 * rows - 1 - hop - distance) * n, n)
                whole_ref[pl.ds(at, n), :] = up_refs[hop - 1][...]

        whole = whole_ref[...]
        fetches[0].wait()
        other_ref[...] = jnp.dot(take_ref[...], whole, preferred_element_type=F32)
        fetches[1].wait()
        mine_ref[...] = jnp.dot(own_ref[...], whole, preferred_element_type=F32)

    out = jax.ShapeDtypeStruct((n, cols), F32)
    return pl.pallas_call(
        kernel,
        out_shape=(out, out),
        in_specs=[pl.BlockSpec(memory_space=pltpu.SMEM)] + in_hbm(2) + whole_specs(1 + 2 * hops),
        out_specs=tuple(whole_specs(2)),
        scratch_shapes=[pltpu.VMEM((half, cols), BF16)]
        + [pltpu.VMEM((n, half), BF16)] * 2
        + [pltpu.SemaphoreType.DMA((2,))],
        compiler_params=pltpu.CompilerParams(vmem_limit_bytes=VMEM_GRANT),
        cost_estimate=pl.CostEstimate(flops=4 * n * half * cols, bytes_accessed=8 * n * half, transcendentals=0),
        name="diag_product",
    )(where, diag, diag_other, held, *downs, *ups)


def coef_product(step, order, v_own, v_other, pieces):
    rows = len(pieces)
    n, cols = pieces[0].shape
    width = v_own.shape[-1]

    def kernel(order_ref, own_ref, other_ref, *refs):
        piece_refs, (out_ref, v_ref, sems) = refs[:rows], refs[rows:]
        for k in range(rows):
            span = pl.ds(pl.multiple_of(order_ref[1, k] * n, n), n)
            for here, source in ((1, own_ref), (0, other_ref)):

                @pl.when(order_ref[0, k] == here)
                def _(k=k, span=span, source=source):
                    pltpu.make_async_copy(source.at[0, step, span, :], v_ref.at[k], sems.at[k]).start()

        for k in range(rows):
            pltpu.make_async_copy(own_ref.at[0, step, pl.ds(0, n), :], v_ref.at[k], sems.at[k]).wait()
            part = lax.dot_general(
                v_ref[k], piece_refs[k][...], (((0,), (0,)), ((), ())), preferred_element_type=F32
            )
            if k == 0:
                out_ref[...] = part
            else:
                out_ref[...] += part

    return pl.pallas_call(
        kernel,
        out_shape=jax.ShapeDtypeStruct((width, cols), F32),
        in_specs=[pl.BlockSpec(memory_space=pltpu.SMEM)] + in_hbm(2) + whole_specs(rows),
        out_specs=whole_specs(1)[0],
        scratch_shapes=[pltpu.VMEM((rows, n, width), BF16), pltpu.SemaphoreType.DMA((rows,))],
        compiler_params=pltpu.CompilerParams(vmem_limit_bytes=VMEM_GRANT),
        cost_estimate=pl.CostEstimate(
            flops=2 * rows * n * width * cols, bytes_accessed=4 * rows * n * width, transcendentals=0
        ),
        name="coef_product",
    )(order, v_own, v_other, *pieces)


def pick(is_holder, held, index, received):
    n = received.shape[0]

    def kernel(holder_ref, held_ref, got_ref, out_ref):
        holds = holder_ref[0] == 1

        @pl.when(holds)
        def _():
            out_ref[...] = held_ref[index * n : (index + 1) * n, :]

        @pl.when(jnp.logical_not(holds))
        def _():
            out_ref[...] = got_ref[...]

    return pl.pallas_call(
        kernel,
        out_shape=jax.ShapeDtypeStruct(received.shape, received.dtype),
        in_specs=[pl.BlockSpec(memory_space=pltpu.SMEM)] + whole_specs(2),
        out_specs=whole_specs(1)[0],
        compiler_params=pltpu.CompilerParams(vmem_limit_bytes=VMEM_GRANT),
        name="pick",
    )(is_holder, held, received)


def update(step, kept, part, taken, block, factors, coefs, n, last):
    half, cols = block.shape
    width = part.shape[0]
    rows = half // n
    before = len(coefs)

    def kernel(kept_ref, part_ref, taken_ref, block_ref, *refs):
        u_refs, c_refs, out_refs = refs[: before + 1], refs[before + 1 : 2 * before + 1], refs[2 * before + 1 :]
        heights = lax.broadcasted_iota(jnp.int32, (width, cols), 0)
        total = part_ref[...] + taken_ref[...]
        coef = jnp.where(heights < kept_ref[step], total, 0.0).astype(BF16)
        if not last:
            out_refs[-1][...] = coef
        for i in range(rows):
            span = slice(i * n, (i + 1) * n)
            value = block_ref[span, :].astype(F32)
            for u_ref, c_ref in zip(u_refs, c_refs):
                value -= jnp.dot(u_ref[span, :], c_ref[...], preferred_element_type=F32)
            value -= jnp.dot(u_refs[before][span, :], coef, preferred_element_type=F32)
            out_refs[0][span, :] = value.astype(out_refs[0].dtype)
            if not last and i == 0:
                out_refs[1][...] = value.astype(BF16)
            if not last and i == rows - 1:
                out_refs[2][...] = value.astype(BF16)

    piece = jax.ShapeDtypeStruct((n, cols), BF16)
    if last:
        out_shape = (jax.ShapeDtypeStruct((half, cols), F32),)
    else:
        out_shape = (
            jax.ShapeDtypeStruct((half, cols), BF16),
            piece,
            piece,
            jax.ShapeDtypeStruct((width, cols), BF16),
        )
    return pl.pallas_call(
        kernel,
        out_shape=out_shape,
        in_specs=[pl.BlockSpec(memory_space=pltpu.SMEM)] + whole_specs(4 + 2 * before),
        out_specs=tuple(whole_specs(len(out_shape))),
        compiler_params=pltpu.CompilerParams(vmem_limit_bytes=VMEM_GRANT),
        cost_estimate=pl.CostEstimate(
            flops=2 * (before + 1) * half * width * cols,
            bytes_accessed=2 * (before + 2) * half * cols,
            transcendentals=0,
        ),
        name="update",
    )(kept, part, taken, block, *factors, *coefs)


def ring_steps(rows, half, n):
    ring = ring_order(rows)
    forward = [(ring[i], ring[(i + 1) % rows]) for i in range(rows)]
    backward = [(b, a) for a, b in forward]
    reach = rows // 2

    def gather(piece):
        got = [None] * rows
        got[0] = down = up = piece
        for hop in range(1, reach + 1):
            got[hop] = down = lax.ppermute(down, "row", forward)
            if hop < rows - hop:
                got[rows - hop] = up = lax.ppermute(up, "row", backward)
        return got

    def spread(held, first, last, is_holder):
        downs, ups = [lax.ppermute(first, "row", forward)], [lax.ppermute(last, "row", backward)]
        for hop in range(1, rows - 1):
            downs.append(lax.ppermute(pick(is_holder, held, hop, downs[-1]), "row", forward))
            ups.append(lax.ppermute(pick(is_holder, held, rows - 1 - hop, ups[-1]), "row", backward))
        return downs, ups

    def local(right_side, diag_inverse, u_factor, v_factor, ranks, pivots):
        steps = pivots.shape[0]
        me, tile = lax.axis_index("row"), lax.axis_index("tile")
        block = right_side[0]
        distances = lax.rem(ring_place(me, rows) - ring_place(pivots, rows) + rows, rows)
        wheres = jnp.stack([jnp.full_like(distances, tile), distances], 1)
        holders = (pivots == me).astype(jnp.int32)
        kept = jnp.where(jnp.cumsum(holders) > 0, 0, ranks[0])

        orders = []
        for device_row in range(rows):
            for t in range(2):
                sources = [ring[(ring.index(device_row) - k) % rows] for k in range(rows)]
                orders.append([[int(j // reach == t) for j in sources], [2 * (j % reach) + t for j in sources]])
        order = lax.dynamic_index_in_dim(jnp.array(orders, jnp.int32), 2 * me + tile, 0, keepdims=False)

        diag_other = lax.ppermute(diag_inverse, "tile", SWAP)
        v_other = lax.ppermute(v_factor, "tile", SWAP)

        held, first, final = block, block[:n], block[half - n :]
        factors, coefs, solved = [], [], []
        for step in range(steps):
            downs, ups = spread(held, first, final, holders[step : step + 1])
            mine, other = diag_product(step, wheres[step], diag_inverse, diag_other, held, downs, ups)
            x = (mine + lax.ppermute(other, "tile", SWAP)).astype(BF16)
            solved.append(x)
            part = coef_product(step, order, v_factor, v_other, gather(x))
            taken = lax.ppermute(part, "tile", SWAP)
            factors.append(u_factor[0, step])
            if step < steps - 1:
                held, first, final, coef = update(step, kept, part, taken, block, factors, coefs, n, False)
                coefs.append(coef)
        (residual,) = update(steps - 1, kept, part, taken, block, factors, coefs, n, True)
        return jnp.stack(solved), residual[None]

    return local


def gathered_steps(right_side, diag_inverse, u_factor, v_factor, ranks, pivots):
    residual = right_side[0].astype(F32)
    half = residual.shape[0]
    heights = lax.broadcasted_iota(jnp.int32, (u_factor.shape[3], 1), 0)
    me, tile = lax.axis_index("row"), lax.axis_index("tile")
    solved = []
    for step in range(pivots.shape[0]):
        current = residual.astype(BF16)
        held = lax.psum(jnp.where(me == pivots[step], current, jnp.zeros_like(current)), "row")
        other = lax.ppermute(held, "tile", SWAP)
        pivot = jnp.where(tile == 0, jnp.concatenate([held, other]), jnp.concatenate([other, held]))
        x = jnp.dot(diag_inverse[step], pivot, preferred_element_type=F32).astype(BF16)
        solved.append(x)
        x_all = lax.all_gather(x, ("row", "tile"), axis=0, tiled=True)
        x_mine = lax.dynamic_slice_in_dim(x_all, tile * half, half, 0)
        part = lax.dot_general(
            v_factor[0, step], x_mine, (((0,), (0,)), ((), ())), preferred_element_type=F32
        )
        coef = part + lax.ppermute(part, "tile", SWAP)
        finished = jnp.any(pivots[: step + 1] == me)
        kept = jnp.where(finished, 0, ranks[0, step])
        coef = jnp.where(heights < kept, coef, F32(0.0)).astype(BF16)
        residual = residual - jnp.dot(u_factor[0, step], coef, preferred_element_type=F32)
    return jnp.stack(solved), residual[None]


def solution(mesh):
    rows = mesh.shape["row"]

    def local(right_side, diag_inverse, *others):
        half, n = right_side.shape[1], diag_inverse.shape[1]
        short = rows % 2 == 0 and rows <= MOST_HOPS and n % LANES == 0 and half == rows * n
        run = ring_steps(rows, half, n) if short else gathered_steps
        return run(right_side, diag_inverse, *others)

    in_specs = (
        P(("grp", "row"), "tile", None),
        P(None, ("row", "tile"), None),
        P("row", None, "tile", None),
        P("row", None, "tile", None),
        P("row", None),
        P(),
    )
    out_specs = (P(None, ("grp", "row", "tile"), None), P(("grp", "row"), "tile", None))
    return jax.shard_map(local, mesh=mesh, in_specs=in_specs, out_specs=out_specs, check_vma=False)
```

```python
import jax
import jax.numpy as jnp
from jax import lax
from jax.experimental import pallas as pl
from jax.experimental.pallas import tpu as pltpu
from jax.sharding import PartitionSpec as P


MOST_HOPS = 8
LANES = 128
SWAP = [(0, 1), (1, 0)]
BF16 = jnp.bfloat16
F32 = jnp.float32
VMEM_GRANT = 6 * 1024 * 1024


def ring_order(rows):
    return list(range(0, rows, 2)) + list(range(rows - 1, 0, -2))


def ring_place(index, rows):
    return jnp.where(index % 2 == 0, index // 2, rows - (index + 1) // 2)


def whole_specs(count):
    return [pl.BlockSpec(memory_space=pltpu.VMEM)] * count


def diag_product(step, where, diag, take, held, downs, ups):
    hops = len(downs)
    rows = hops + 1
    n, cols = downs[0].shape
    half = rows * n

    def kernel(where_ref, diag_ref, take_ref, held_ref, *refs):
        down_refs, up_refs, refs = refs[:hops], refs[hops : 2 * hops], refs[2 * hops :]
        mine_ref, other_ref, whole_ref = refs
        base = pl.multiple_of(where_ref[0] * half, half)
        distance = where_ref[1]

        @pl.when(distance == 0)
        def _():
            whole_ref[...] = held_ref[...]

        for hop in range(1, hops + 1):

            @pl.when(jnp.logical_and(distance > 0, distance <= hop))
            def _(hop=hop):
                at = pl.multiple_of((hop - distance) * n, n)
                whole_ref[pl.ds(at, n), :] = down_refs[hop - 1][...]

            @pl.when(jnp.logical_and(distance > 0, distance >= rows - hop))
            def _(hop=hop):
                at = pl.multiple_of((2 * rows - 1 - hop - distance) * n, n)
                whole_ref[pl.ds(at, n), :] = up_refs[hop - 1][...]

        whole = whole_ref[...]
        mine_ref[...] = jnp.dot(diag_ref[step, :, pl.ds(base, half)], whole, preferred_element_type=F32)
        other_ref[...] = jnp.dot(take_ref[...], whole, preferred_element_type=F32)

    out = jax.ShapeDtypeStruct((n, cols), F32)
    return pl.pallas_call(
        kernel,
        out_shape=(out, out),
        in_specs=[pl.BlockSpec(memory_space=pltpu.SMEM)] + whole_specs(3 + 2 * hops),
        out_specs=tuple(whole_specs(2)),
        scratch_shapes=[pltpu.VMEM((half, cols), BF16)],
        compiler_params=pltpu.CompilerParams(vmem_limit_bytes=VMEM_GRANT),
        cost_estimate=pl.CostEstimate(flops=4 * n * half * cols, bytes_accessed=8 * n * half, transcendentals=0),
        name="diag_product",
    )(where, diag, take, held, *downs, *ups)


def coef_product(order, v_pieces, pieces):
    rows, n, width = v_pieces.shape
    cols = pieces[0].shape[1]

    def kernel(order_ref, v_ref, *refs):
        piece_refs, out_ref = refs[:rows], refs[rows]
        for k in range(rows):
            part = lax.dot_general(
                v_ref[order_ref[k]], piece_refs[k][...], (((0,), (0,)), ((), ())), preferred_element_type=F32
            )
            if k == 0:
                out_ref[...] = part
            else:
                out_ref[...] += part

    return pl.pallas_call(
        kernel,
        out_shape=jax.ShapeDtypeStruct((width, cols), F32),
        in_specs=[pl.BlockSpec(memory_space=pltpu.SMEM)] + whole_specs(1 + rows),
        out_specs=whole_specs(1)[0],
        compiler_params=pltpu.CompilerParams(vmem_limit_bytes=VMEM_GRANT),
        cost_estimate=pl.CostEstimate(
            flops=2 * rows * n * width * cols, bytes_accessed=4 * rows * n * width, transcendentals=0
        ),
        name="coef_product",
    )(order, v_pieces, *pieces)


def pick(mask, held, index, received):
    n = received.shape[0]

    def kernel(mask_ref, held_ref, got_ref, out_ref):
        own = held_ref[index * n : (index + 1) * n, :]
        out_ref[...] = jnp.where(mask_ref[...] > 0, own, got_ref[...])

    return pl.pallas_call(
        kernel,
        out_shape=jax.ShapeDtypeStruct(received.shape, received.dtype),
        in_specs=whole_specs(3),
        out_specs=whole_specs(1)[0],
        compiler_params=pltpu.CompilerParams(vmem_limit_bytes=VMEM_GRANT),
        name="pick",
    )(mask, held, received)


def update(step, state, part, taken, block, factor, coefs, n, last):
    half, cols = block.shape
    width = part.shape[0]
    rows = half // n
    before = len(coefs)

    def kernel(state_ref, part_ref, taken_ref, block_ref, u_ref, *refs):
        c_refs, out_refs = refs[:before], refs[before:]
        kept = state_ref[state_ref.shape[0] // 2 + step]
        for q in range(step + 1):
            kept = jnp.where(state_ref[q] == 0, 0, kept)
        heights = lax.broadcasted_iota(jnp.int32, (width, cols), 0)
        coef = jnp.where(heights < kept, part_ref[...] + taken_ref[...], 0.0).astype(BF16)
        if not last:
            out_refs[-1][...] = coef
        for i in range(rows):
            span = slice(i * n, (i + 1) * n)
            value = block_ref[span, :].astype(F32)
            for q, c_ref in enumerate(c_refs):
                value -= jnp.dot(u_ref[0, q, span, :], c_ref[...], preferred_element_type=F32)
            value -= jnp.dot(u_ref[0, step, span, :], coef, preferred_element_type=F32)
            out_refs[0][span, :] = value.astype(out_refs[0].dtype)
            if not last and i == 0:
                out_refs[1][...] = value.astype(BF16)
            if not last and i == rows - 1:
                out_refs[2][...] = value.astype(BF16)

    piece = jax.ShapeDtypeStruct((n, cols), BF16)
    if last:
        out_shape = (jax.ShapeDtypeStruct((half, cols), F32),)
    else:
        out_shape = (
            jax.ShapeDtypeStruct((half, cols), BF16),
            piece,
            piece,
            jax.ShapeDtypeStruct((width, cols), BF16),
        )
    return pl.pallas_call(
        kernel,
        out_shape=out_shape,
        in_specs=[pl.BlockSpec(memory_space=pltpu.SMEM)] + whole_specs(4 + before),
        out_specs=tuple(whole_specs(len(out_shape))),
        compiler_params=pltpu.CompilerParams(vmem_limit_bytes=VMEM_GRANT),
        cost_estimate=pl.CostEstimate(
            flops=2 * (before + 1) * half * width * cols,
            bytes_accessed=2 * (before + 2) * half * cols,
            transcendentals=0,
        ),
        name="update",
    )(state, part, taken, block, factor, *coefs)


def ring_steps(rows, half, n):
    ring = ring_order(rows)
    forward = [(ring[i], ring[(i + 1) % rows]) for i in range(rows)]
    backward = [(b, a) for a, b in forward]
    reach = rows // 2

    def gather(piece):
        got = [None] * rows
        got[0] = down = up = piece
        for hop in range(1, reach + 1):
            got[hop] = down = lax.ppermute(down, "row", forward)
            if hop < rows - hop:
                got[rows - hop] = up = lax.ppermute(up, "row", backward)
        return got

    def spread(held, first, last, step, beside):
        down, up = lax.ppermute(first, "row", forward), lax.ppermute(last, "row", backward)
        if step == 0:
            down, up, beside = lax.optimization_barrier((down, up, beside))
        mask = beside[-1][step]
        downs, ups = [down], [up]
        for hop in range(1, rows - 1):
            downs.append(lax.ppermute(pick(mask, held, hop, downs[-1]), "row", forward))
            ups.append(lax.ppermute(pick(mask, held, rows - 1 - hop, ups[-1]), "row", backward))
        return downs, ups, beside

    def local(right_side, diag_inverse, u_factor, v_factor, ranks, pivots):
        steps = pivots.shape[0]
        me, tile = lax.axis_index("row"), lax.axis_index("tile")
        mine_at = tile.astype(jnp.uint32)
        other_at = 1 - mine_at
        block = right_side[0]
        cols, width = block.shape[1], u_factor.shape[3]
        table = []
        for device_row in range(rows):
            at = ring.index(device_row)
            for t in range(2):
                table.append([(ring[(at - k) % rows] + t * reach) % rows for k in range(rows)] + [t, at])
        facts = lax.dynamic_slice(
            jnp.array(table, jnp.int32), ((2 * me + tile).astype(jnp.uint32), jnp.uint32(0)), (1, rows + 2)
        )[0]
        order, my_tile, place = facts[:rows], facts[rows : rows + 1], facts[rows + 1 :]
        distances = lax.rem(place - ring_place(pivots, rows) + rows, rows)
        wheres = [jnp.concatenate([my_tile, distances[p : p + 1]]) for p in range(steps)]
        holders = (distances == 0).astype(jnp.int32)
        state = jnp.concatenate([distances, ranks[0]])
        masks = [jnp.broadcast_to(holders[p : p + 1, None].astype(BF16), (n, cols)) for p in range(steps)]

        d_give = lax.dynamic_slice_in_dim(diag_inverse, other_at * half, half, 2)
        beside = (d_give, mine_at, other_at, order, wheres, state, masks)
        held, first, final = block, block[:n], block[half - n :]
        coefs, solved = [], []
        for step in range(steps):
            downs, ups, beside = spread(held, first, final, step, beside)
            d_give, mine_at, other_at, order, wheres, state, masks = beside
            if step == 0:
                d_take = [lax.ppermute(d_give[p], "tile", SWAP) for p in range(steps)]
            mine, other = diag_product(step, wheres[step], diag_inverse, d_take[step], held, downs, ups)
            if step == 0:
                mine, other, v_rows = lax.optimization_barrier((mine, other, v_factor[0]))
                v_pairs = v_rows.reshape(steps, reach, 2, n, width)
                v_keep = lax.dynamic_index_in_dim(v_pairs, mine_at, 2, keepdims=False)
                v_give = lax.dynamic_index_in_dim(v_pairs, other_at, 2, keepdims=False)
                v_take = lax.ppermute(v_give, "tile", SWAP)
                v_pieces = jnp.concatenate([v_keep, v_take], 1)
            x = (mine + lax.ppermute(other, "tile", SWAP)).astype(BF16)
            solved.append(x)
            part = coef_product(order, v_pieces[step], gather(x))
            taken = lax.ppermute(part, "tile", SWAP)
            if step < steps - 1:
                held, first, final, coef = update(step, state, part, taken, block, u_factor, coefs, n, False)
                coefs.append(coef)
        (residual,) = update(steps - 1, state, part, taken, block, u_factor, coefs, n, True)
        return jnp.stack(solved), residual[None]

    return local


def gathered_steps(right_side, diag_inverse, u_factor, v_factor, ranks, pivots):
    residual = right_side[0].astype(F32)
    half = residual.shape[0]
    heights = lax.broadcasted_iota(jnp.int32, (u_factor.shape[3], 1), 0)
    me, tile = lax.axis_index("row"), lax.axis_index("tile")
    solved = []
    for step in range(pivots.shape[0]):
        current = residual.astype(BF16)
        held = lax.psum(jnp.where(me == pivots[step], current, jnp.zeros_like(current)), "row")
        other = lax.ppermute(held, "tile", SWAP)
        pivot = jnp.where(tile == 0, jnp.concatenate([held, other]), jnp.concatenate([other, held]))
        x = jnp.dot(diag_inverse[step], pivot, preferred_element_type=F32).astype(BF16)
        solved.append(x)
        x_all = lax.all_gather(x, ("row", "tile"), axis=0, tiled=True)
        x_mine = lax.dynamic_slice_in_dim(x_all, tile * half, half, 0)
        part = lax.dot_general(
            v_factor[0, step], x_mine, (((0,), (0,)), ((), ())), preferred_element_type=F32
        )
        coef = part + lax.ppermute(part, "tile", SWAP)
        finished = jnp.any(pivots[: step + 1] == me)
        kept = jnp.where(finished, 0, ranks[0, step])
        coef = jnp.where(heights < kept, coef, F32(0.0)).astype(BF16)
        residual = residual - jnp.dot(u_factor[0, step], coef, preferred_element_type=F32)
    return jnp.stack(solved), residual[None]


def solution(mesh):
    rows = mesh.shape["row"]

    def local(right_side, diag_inverse, *others):
        half, n = right_side.shape[1], diag_inverse.shape[1]
        short = rows % 2 == 0 and rows <= MOST_HOPS and n % LANES == 0 and half == rows * n
        run = ring_steps(rows, half, n) if short else gathered_steps
        return run(right_side, diag_inverse, *others)

    in_specs = (
        P(("grp", "row"), "tile", None),
        P(None, ("row", "tile"), None),
        P("row", None, "tile", None),
        P("row", None, "tile", None),
        P("row", None),
        P(),
    )
    out_specs = (P(None, ("grp", "row", "tile"), None), P(("grp", "row"), "tile", None))
    return jax.shard_map(local, mesh=mesh, in_specs=in_specs, out_specs=out_specs, check_vma=False)
```

```python
import jax
import jax.numpy as jnp
from jax import lax
from jax.experimental import pallas as pl
from jax.experimental.pallas import tpu as pltpu
from jax.sharding import PartitionSpec as P


MOST_HOPS = 8
LANES = 128
PARTS = 2
SWAP = [(0, 1), (1, 0)]
BF16 = jnp.bfloat16
F32 = jnp.float32
VMEM_GRANT = 6 * 1024 * 1024


def ring_order(rows):
    return list(range(0, rows, 2)) + list(range(rows - 1, 0, -2))


def ring_place(index, rows):
    return jnp.where(lax.rem(index, 2) == 0, lax.div(index, 2), rows - lax.div(index + 1, 2))


def ring_row(place, rows):
    return jnp.where(place < rows // 2, 2 * place, 2 * (rows - place) - 1)


def ring_distance(holder, rows):
    return lax.rem(ring_place(lax.axis_index("row"), rows) - ring_place(holder, rows) + rows, rows)


def whole_specs(count):
    return [pl.BlockSpec(memory_space=pltpu.VMEM)] * count


def in_smem(count):
    return [pl.BlockSpec(memory_space=pltpu.SMEM)] * count


def cost(flops, moved):
    return pl.CostEstimate(flops=flops, bytes_accessed=moved, transcendentals=0)


PARAMS = pltpu.CompilerParams(vmem_limit_bytes=VMEM_GRANT)


def holder_masks(pivots, shape):
    steps = pivots.shape[0]

    def kernel(pivots_ref, *out_refs):
        me = lax.axis_index("row")
        for p in range(steps):
            value = jnp.where(pivots_ref[p] == me, 1.0, 0.0)
            out_refs[p][...] = jnp.full(shape, value, F32).astype(BF16)

    return pl.pallas_call(
        kernel,
        out_shape=(jax.ShapeDtypeStruct(shape, BF16),) * steps,
        in_specs=in_smem(1),
        out_specs=tuple(whole_specs(steps)),
        compiler_params=PARAMS,
        name="holder_masks",
    )(pivots)


def pick(mask, held, start, received):
    n = received.shape[0]

    def kernel(mask_ref, held_ref, got_ref, out_ref):
        out_ref[...] = jnp.where(mask_ref[...] > 0, held_ref[start : start + n, :], got_ref[...])

    return pl.pallas_call(
        kernel,
        out_shape=jax.ShapeDtypeStruct(received.shape, received.dtype),
        in_specs=whole_specs(3),
        out_specs=whole_specs(1)[0],
        compiler_params=PARAMS,
        name="pick",
    )(mask, held, received)


def diag_product(step, pivots, diag, take, held, downs, ups):
    hops, parts = len(downs), len(downs[0])
    rows = hops + 1
    m, cols = downs[0][0].shape
    n = m * parts
    half = rows * n

    def kernel(pivots_ref, diag_ref, take_ref, held_ref, *refs):
        got_refs, (mine_ref, other_ref, whole_ref) = refs[: 2 * hops * parts], refs[2 * hops * parts :]
        down_refs, up_refs = got_refs[: hops * parts], got_refs[hops * parts :]
        distance = ring_distance(pivots_ref[step], rows)

        @pl.when(distance == 0)
        def _():
            whole_ref[...] = held_ref[...]

        for hop in range(1, hops + 1):
            for near, at, side in (
                (distance <= hop, hop - distance, down_refs),
                (distance >= rows - hop, 2 * rows - 1 - hop - distance, up_refs),
            ):

                @pl.when(jnp.logical_and(distance > 0, near))
                def _(at=at, side=side, hop=hop):
                    for c in range(parts):
                        rows_at = pl.multiple_of(at * n + c * m, m)
                        whole_ref[pl.ds(rows_at, m), :] = side[(hop - 1) * parts + c][...]

        base = pl.multiple_of(lax.axis_index("tile") * half, half)
        whole = whole_ref[...]
        mine_ref[...] = jnp.dot(diag_ref[step, :, pl.ds(base, half)], whole, preferred_element_type=F32)
        other_ref[...] = jnp.dot(take_ref[...], whole, preferred_element_type=F32)

    out = jax.ShapeDtypeStruct((n, cols), F32)
    flat = [part for side in (downs, ups) for hop in side for part in hop]
    return pl.pallas_call(
        kernel,
        out_shape=(out, out),
        in_specs=in_smem(1) + whole_specs(3 + len(flat)),
        out_specs=tuple(whole_specs(2)),
        scratch_shapes=[pltpu.VMEM((half, cols), BF16)],
        compiler_params=PARAMS,
        cost_estimate=cost(4 * n * half * cols, 8 * n * half),
        name="diag_product",
    )(pivots, diag, take, held, *flat)


def coef_product(v_pieces, pieces):
    rows, n, width = v_pieces.shape
    parts = len(pieces[0])
    m, cols = pieces[0][0].shape
    reach = rows // 2

    def kernel(v_ref, *refs):
        piece_refs, out_ref = refs[: rows * parts], refs[rows * parts]
        place, tile = ring_place(lax.axis_index("row"), rows), lax.axis_index("tile")
        for k in range(rows):
            row = ring_row(lax.rem(place - k + rows, rows), rows)
            at = lax.rem(row + tile * reach, rows)
            for c in range(parts):
                part = lax.dot_general(
                    v_ref[at, c * m : (c + 1) * m, :],
                    piece_refs[k * parts + c][...],
                    (((0,), (0,)), ((), ())),
                    preferred_element_type=F32,
                )
                if k == 0 and c == 0:
                    out_ref[...] = part
                else:
                    out_ref[...] += part

    flat = [part for piece in pieces for part in piece]
    return pl.pallas_call(
        kernel,
        out_shape=jax.ShapeDtypeStruct((width, cols), F32),
        in_specs=whole_specs(1 + len(flat)),
        out_specs=whole_specs(1)[0],
        compiler_params=PARAMS,
        cost_estimate=cost(2 * rows * n * width * cols, 4 * rows * n * width),
        name="coef_product",
    )(v_pieces, *flat)


def update(step, pivots, ranks, part, taken, residual, factor, n, parts, last):
    half, cols = residual.shape
    width = part.shape[0]
    rows, m = half // n, n // parts

    def kernel(pivots_ref, ranks_ref, part_ref, taken_ref, residual_ref, u_ref, *refs):
        kept = ranks_ref[0, step]
        for q in range(step + 1):
            kept = jnp.where(pivots_ref[q] == lax.axis_index("row"), 0, kept)
        heights = lax.broadcasted_iota(jnp.int32, (width, cols), 0)
        coef = jnp.where(heights < kept, part_ref[...] + taken_ref[...], 0.0).astype(BF16)
        for i in range(rows):
            span = slice(i * n, (i + 1) * n)
            value = residual_ref[span, :].astype(F32)
            value -= jnp.dot(u_ref[0, step, span, :], coef, preferred_element_type=F32)
            if last:
                out_ref, whole_ref, sems = refs
                whole_ref[span, :] = value
                pltpu.make_async_copy(whole_ref.at[span, :], out_ref.at[span, :], sems.at[i]).start()
                continue
            refs[0][span, :] = value
            rounded = value.astype(BF16)
            refs[1][span, :] = rounded
            for c in range(parts):
                if i == 0:
                    refs[2 + c][...] = rounded[c * m : (c + 1) * m, :]
                if i == rows - 1:
                    refs[2 + parts + c][...] = rounded[c * m : (c + 1) * m, :]
        if last:
            for i in range(rows):
                span = slice(i * n, (i + 1) * n)
                pltpu.make_async_copy(whole_ref.at[span, :], out_ref.at[span, :], sems.at[i]).wait()

    full = jax.ShapeDtypeStruct((half, cols), F32)
    if last:
        out_shape, out_specs = full, pl.BlockSpec(memory_space=pl.ANY)
        scratch = [pltpu.VMEM((half, cols), F32), pltpu.SemaphoreType.DMA((rows,))]
    else:
        piece = jax.ShapeDtypeStruct((m, cols), BF16)
        out_shape = (full, jax.ShapeDtypeStruct((half, cols), BF16)) + (piece,) * (2 * parts)
        out_specs, scratch = tuple(whole_specs(2 + 2 * parts)), []
    return pl.pallas_call(
        kernel,
        out_shape=out_shape,
        in_specs=in_smem(2) + whole_specs(4),
        out_specs=out_specs,
        scratch_shapes=scratch,
        compiler_params=PARAMS,
        cost_estimate=cost(2 * half * width * cols, 8 * half * cols),
        name="update",
    )(pivots, ranks, part, taken, residual, factor)


def ring_steps(rows, half, n):
    ring = ring_order(rows)
    forward = [(ring[i], ring[(i + 1) % rows]) for i in range(rows)]
    backward = [(b, a) for a, b in forward]
    reach = rows // 2
    m = n // PARTS

    def gather(piece):
        got = [None] * rows
        got[0] = down = up = piece
        for hop in range(1, reach + 1):
            got[hop] = down = [lax.ppermute(part, "row", forward) for part in down]
            if hop < rows - hop:
                got[rows - hop] = up = [lax.ppermute(part, "row", backward) for part in up]
        return got

    def spread(held, first, last, masks, step, beside):
        down = [lax.ppermute(part, "row", forward) for part in first]
        up = [lax.ppermute(part, "row", backward) for part in last]
        if step == 0:
            down, up, masks, beside = lax.optimization_barrier((down, up, masks, beside))
        downs, ups = [down], [up]
        for hop in range(1, rows - 1):
            down, up = list(down), list(up)
            for c in range(PARTS):
                own = pick(masks[step], held, hop * n + c * m, down[c])
                down[c] = lax.ppermute(own, "row", forward)
                own = pick(masks[step], held, (rows - 1 - hop) * n + c * m, up[c])
                up[c] = lax.ppermute(own, "row", backward)
            downs.append(down)
            ups.append(up)
        return downs, ups, masks, beside

    def local(right_side, diag_inverse, u_factor, v_factor, ranks, pivots):
        steps = pivots.shape[0]
        mine_at = lax.axis_index("tile").astype(jnp.uint32)
        other_at = 1 - mine_at
        held = residual = right_side[0]
        cols, width = held.shape[1], u_factor.shape[3]
        masks = holder_masks(pivots, (m, cols))
        d_give = lax.dynamic_slice_in_dim(diag_inverse, other_at * half, half, 2)
        first = [held[c * m : (c + 1) * m] for c in range(PARTS)]
        final = [held[half - n + c * m : half - n + (c + 1) * m] for c in range(PARTS)]
        beside = (d_give, mine_at, other_at)
        solved = []
        for step in range(steps):
            downs, ups, masks, beside = spread(held, first, final, masks, step, beside)
            d_give, mine_at, other_at = beside
            if step == 0:
                d_take = [lax.ppermute(d_give[p], "tile", SWAP) for p in range(steps)]
            mine, other = diag_product(step, pivots, diag_inverse, d_take[step], held, downs, ups)
            total = mine + lax.ppermute(other, "tile", SWAP)
            x = [total[c * m : (c + 1) * m].astype(BF16) for c in range(PARTS)]
            solved += x
            if step == 0:
                x, v_rows = lax.optimization_barrier((x, v_factor[0]))
                v_pairs = v_rows.reshape(steps, reach, 2, n, width)
                v_keep = lax.dynamic_index_in_dim(v_pairs, mine_at, 2, keepdims=False)
                v_give = lax.dynamic_index_in_dim(v_pairs, other_at, 2, keepdims=False)
                v_take = lax.ppermute(v_give, "tile", SWAP)
                v_pieces = jnp.concatenate([v_keep, v_take], 1)
            part = coef_product(v_pieces[step], gather(x))
            taken = lax.ppermute(part, "tile", SWAP)
            last = step == steps - 1
            out = update(step, pivots, ranks, part, taken, residual, u_factor, n, PARTS, last)
            if not last:
                residual, held, first, final = out[0], out[1], out[2 : 2 + PARTS], out[2 + PARTS :]
        return jnp.concatenate(solved).reshape(steps, n, cols), out[None]

    return local


def gathered_steps(right_side, diag_inverse, u_factor, v_factor, ranks, pivots):
    residual = right_side[0].astype(F32)
    half = residual.shape[0]
    heights = lax.broadcasted_iota(jnp.int32, (u_factor.shape[3], 1), 0)
    me, tile = lax.axis_index("row"), lax.axis_index("tile")
    solved = []
    for step in range(pivots.shape[0]):
        current = residual.astype(BF16)
        held = lax.psum(jnp.where(me == pivots[step], current, jnp.zeros_like(current)), "row")
        other = lax.ppermute(held, "tile", SWAP)
        pivot = jnp.where(tile == 0, jnp.concatenate([held, other]), jnp.concatenate([other, held]))
        x = jnp.dot(diag_inverse[step], pivot, preferred_element_type=F32).astype(BF16)
        solved.append(x)
        x_all = lax.all_gather(x, ("row", "tile"), axis=0, tiled=True)
        x_mine = lax.dynamic_slice_in_dim(x_all, tile * half, half, 0)
        part = lax.dot_general(
            v_factor[0, step], x_mine, (((0,), (0,)), ((), ())), preferred_element_type=F32
        )
        coef = part + lax.ppermute(part, "tile", SWAP)
        finished = jnp.any(pivots[: step + 1] == me)
        kept = jnp.where(finished, 0, ranks[0, step])
        coef = jnp.where(heights < kept, coef, F32(0.0)).astype(BF16)
        residual = residual - jnp.dot(u_factor[0, step], coef, preferred_element_type=F32)
    return jnp.stack(solved), residual[None]


def solution(mesh):
    rows = mesh.shape["row"]

    def local(right_side, diag_inverse, *others):
        half, n = right_side.shape[1], diag_inverse.shape[1]
        short = rows % 2 == 0 and rows <= MOST_HOPS and n % LANES == 0 and half == rows * n
        run = ring_steps(rows, half, n) if short else gathered_steps
        return run(right_side, diag_inverse, *others)

    in_specs = (
        P(("grp", "row"), "tile", None),
        P(None, ("row", "tile"), None),
        P("row", None, "tile", None),
        P("row", None, "tile", None),
        P("row", None),
        P(),
    )
    out_specs = (P(None, ("grp", "row", "tile"), None), P(("grp", "row"), "tile", None))
    return jax.shard_map(local, mesh=mesh, in_specs=in_specs, out_specs=out_specs, check_vma=False)
```

```python
import jax
import jax.numpy as jnp
from jax import lax
from jax.experimental import pallas as pl
from jax.experimental.pallas import tpu as pltpu
from jax.sharding import PartitionSpec as P


MOST_HOPS = 8
LANES = 128
PARTS = 2
SWAP = [(0, 1), (1, 0)]
BF16 = jnp.bfloat16
F32 = jnp.float32
VMEM_GRANT = 6 * 1024 * 1024


def ring_order(rows):
    return list(range(0, rows, 2)) + list(range(rows - 1, 0, -2))


def ring_place(index, rows):
    return jnp.where(lax.rem(index, 2) == 0, lax.div(index, 2), rows - lax.div(index + 1, 2))


def ring_row(place, rows):
    return jnp.where(place < rows // 2, 2 * place, 2 * (rows - place) - 1)


def ring_distance(holder, rows):
    return lax.rem(ring_place(lax.axis_index("row"), rows) - ring_place(holder, rows) + rows, rows)


def whole_specs(count):
    return [pl.BlockSpec(memory_space=pltpu.VMEM)] * count


def in_smem(count):
    return [pl.BlockSpec(memory_space=pltpu.SMEM)] * count


def cost(flops, moved):
    return pl.CostEstimate(flops=flops, bytes_accessed=moved, transcendentals=0)


PARAMS = pltpu.CompilerParams(vmem_limit_bytes=VMEM_GRANT)


def holder_masks(pivots, shape):
    steps = pivots.shape[0]

    def kernel(pivots_ref, *out_refs):
        me = lax.axis_index("row")
        for p in range(steps):
            value = jnp.where(pivots_ref[p] == me, 1.0, 0.0)
            out_refs[p][...] = jnp.full(shape, value, F32).astype(BF16)

    return pl.pallas_call(
        kernel,
        out_shape=(jax.ShapeDtypeStruct(shape, BF16),) * steps,
        in_specs=in_smem(1),
        out_specs=tuple(whole_specs(steps)),
        compiler_params=PARAMS,
        name="holder_masks",
    )(pivots)


def pick(mask, held, start, received):
    n = received.shape[0]

    def kernel(mask_ref, held_ref, got_ref, out_ref):
        out_ref[...] = jnp.where(mask_ref[...] > 0, held_ref[start : start + n, :], got_ref[...])

    return pl.pallas_call(
        kernel,
        out_shape=jax.ShapeDtypeStruct(received.shape, received.dtype),
        in_specs=whole_specs(3),
        out_specs=whole_specs(1)[0],
        compiler_params=PARAMS,
        name="pick",
    )(mask, held, received)


def diag_product(step, pivots, diag, take, held, downs, ups):
    hops, parts = len(downs), len(downs[0])
    rows = hops + 1
    m, cols = downs[0][0].shape
    n = m * parts
    half = rows * n

    def kernel(pivots_ref, diag_ref, take_ref, held_ref, *refs):
        got_refs, (mine_ref, other_ref, whole_ref) = refs[: 2 * hops * parts], refs[2 * hops * parts :]
        down_refs, up_refs = got_refs[: hops * parts], got_refs[hops * parts :]
        distance = ring_distance(pivots_ref[step], rows)

        @pl.when(distance == 0)
        def _():
            whole_ref[...] = held_ref[...]

        for hop in range(1, hops + 1):
            for near, at, side in (
                (distance <= hop, hop - distance, down_refs),
                (distance >= rows - hop, 2 * rows - 1 - hop - distance, up_refs),
            ):

                @pl.when(jnp.logical_and(distance > 0, near))
                def _(at=at, side=side, hop=hop):
                    for c in range(parts):
                        rows_at = pl.multiple_of(at * n + c * m, m)
                        whole_ref[pl.ds(rows_at, m), :] = side[(hop - 1) * parts + c][...]

        base = pl.multiple_of(lax.axis_index("tile") * half, half)
        whole = whole_ref[...]
        mine_ref[...] = jnp.dot(diag_ref[step, :, pl.ds(base, half)], whole, preferred_element_type=F32)
        other_ref[...] = jnp.dot(take_ref[...], whole, preferred_element_type=F32).astype(BF16)

    flat = [part for side in (downs, ups) for hop in side for part in hop]
    return pl.pallas_call(
        kernel,
        out_shape=(jax.ShapeDtypeStruct((n, cols), F32), jax.ShapeDtypeStruct((n, cols), BF16)),
        in_specs=in_smem(1) + whole_specs(3 + len(flat)),
        out_specs=tuple(whole_specs(2)),
        scratch_shapes=[pltpu.VMEM((half, cols), BF16)],
        compiler_params=PARAMS,
        cost_estimate=cost(4 * n * half * cols, 8 * n * half),
        name="diag_product",
    )(pivots, diag, take, held, *flat)


def coef_product(v_pieces, pieces):
    rows, n, width = v_pieces.shape
    parts = len(pieces[0])
    m, cols = pieces[0][0].shape
    reach = rows // 2

    def kernel(v_ref, *refs):
        piece_refs, (out_ref, sent_ref) = refs[: rows * parts], refs[rows * parts :]
        place, tile = ring_place(lax.axis_index("row"), rows), lax.axis_index("tile")
        for k in range(rows):
            row = ring_row(lax.rem(place - k + rows, rows), rows)
            at = lax.rem(row + tile * reach, rows)
            for c in range(parts):
                part = lax.dot_general(
                    v_ref[at, c * m : (c + 1) * m, :],
                    piece_refs[k * parts + c][...],
                    (((0,), (0,)), ((), ())),
                    preferred_element_type=F32,
                )
                if k == 0 and c == 0:
                    out_ref[...] = part
                else:
                    out_ref[...] += part
        sent_ref[...] = out_ref[...].astype(BF16)

    flat = [part for piece in pieces for part in piece]
    return pl.pallas_call(
        kernel,
        out_shape=(jax.ShapeDtypeStruct((width, cols), F32), jax.ShapeDtypeStruct((width, cols), BF16)),
        in_specs=whole_specs(1 + len(flat)),
        out_specs=tuple(whole_specs(2)),
        compiler_params=PARAMS,
        cost_estimate=cost(2 * rows * n * width * cols, 4 * rows * n * width),
        name="coef_product",
    )(v_pieces, *flat)


def update(step, pivots, ranks, part, taken, residual, factor, n, parts, last):
    half, cols = residual.shape
    width = part.shape[0]
    rows, m = half // n, n // parts

    def kernel(pivots_ref, ranks_ref, part_ref, taken_ref, residual_ref, u_ref, *refs):
        kept = ranks_ref[0, step]
        for q in range(step + 1):
            kept = jnp.where(pivots_ref[q] == lax.axis_index("row"), 0, kept)
        heights = lax.broadcasted_iota(jnp.int32, (width, cols), 0)
        coef = jnp.where(heights < kept, part_ref[...] + taken_ref[...].astype(F32), 0.0).astype(BF16)
        for i in range(rows):
            span = slice(i * n, (i + 1) * n)
            value = residual_ref[span, :].astype(F32)
            value -= jnp.dot(u_ref[0, step, span, :], coef, preferred_element_type=F32)
            if last:
                out_ref, whole_ref, sems = refs
                whole_ref[span, :] = value
                pltpu.make_async_copy(whole_ref.at[span, :], out_ref.at[span, :], sems.at[i]).start()
                continue
            refs[0][span, :] = value
            rounded = value.astype(BF16)
            refs[1][span, :] = rounded
            for c in range(parts):
                if i == 0:
                    refs[2 + c][...] = rounded[c * m : (c + 1) * m, :]
                if i == rows - 1:
                    refs[2 + parts + c][...] = rounded[c * m : (c + 1) * m, :]
        if last:
            for i in range(rows):
                span = slice(i * n, (i + 1) * n)
                pltpu.make_async_copy(whole_ref.at[span, :], out_ref.at[span, :], sems.at[i]).wait()

    full = jax.ShapeDtypeStruct((half, cols), F32)
    if last:
        out_shape, out_specs = full, pl.BlockSpec(memory_space=pl.ANY)
        scratch = [pltpu.VMEM((half, cols), F32), pltpu.SemaphoreType.DMA((rows,))]
    else:
        piece = jax.ShapeDtypeStruct((m, cols), BF16)
        out_shape = (full, jax.ShapeDtypeStruct((half, cols), BF16)) + (piece,) * (2 * parts)
        out_specs, scratch = tuple(whole_specs(2 + 2 * parts)), []
    return pl.pallas_call(
        kernel,
        out_shape=out_shape,
        in_specs=in_smem(2) + whole_specs(4),
        out_specs=out_specs,
        scratch_shapes=scratch,
        compiler_params=PARAMS,
        cost_estimate=cost(2 * half * width * cols, 8 * half * cols),
        name="update",
    )(pivots, ranks, part, taken, residual, factor)


def ring_steps(rows, half, n):
    ring = ring_order(rows)
    forward = [(ring[i], ring[(i + 1) % rows]) for i in range(rows)]
    backward = [(b, a) for a, b in forward]
    reach = rows // 2
    m = n // PARTS

    def gather(piece):
        got = [None] * rows
        got[0] = down = up = piece
        for hop in range(1, reach):
            got[hop] = down = [lax.ppermute(part, "row", forward) for part in down]
            got[rows - hop] = up = [lax.ppermute(part, "row", backward) for part in up]
        sides = [(down, forward) if c % 2 == 0 else (up, backward) for c in range(PARTS)]
        got[reach] = [lax.ppermute(side[c], "row", way) for c, (side, way) in enumerate(sides)]
        return got

    def spread(held, first, last, masks, step, beside):
        down = [lax.ppermute(part, "row", forward) for part in first]
        up = [lax.ppermute(part, "row", backward) for part in last]
        if step == 0:
            down[0], masks, beside = lax.optimization_barrier((down[0], masks, beside))
        downs, ups = [down], [up]
        for hop in range(1, rows - 1):
            down, up = list(down), list(up)
            for c in range(PARTS):
                own = pick(masks[step], held, hop * n + c * m, down[c])
                down[c] = lax.ppermute(own, "row", forward)
                own = pick(masks[step], held, (rows - 1 - hop) * n + c * m, up[c])
                up[c] = lax.ppermute(own, "row", backward)
            downs.append(down)
            ups.append(up)
        return downs, ups, masks, beside

    def local(right_side, diag_inverse, u_factor, v_factor, ranks, pivots):
        steps = pivots.shape[0]
        mine_at = lax.axis_index("tile").astype(jnp.uint32)
        other_at = 1 - mine_at
        held = residual = right_side[0]
        cols, width = held.shape[1], u_factor.shape[3]
        masks = holder_masks(pivots, (m, cols))
        d_give = lax.dynamic_slice_in_dim(diag_inverse, other_at * half, half, 2)
        first = [held[c * m : (c + 1) * m] for c in range(PARTS)]
        final = [held[half - n + c * m : half - n + (c + 1) * m] for c in range(PARTS)]
        beside = (d_give, mine_at, other_at)
        solved = []
        for step in range(steps):
            downs, ups, masks, beside = spread(held, first, final, masks, step, beside)
            d_give, mine_at, other_at = beside
            if step == 0:
                d_take = [lax.ppermute(d_give[p], "tile", SWAP) for p in range(steps)]
            mine, other = diag_product(step, pivots, diag_inverse, d_take[step], held, downs, ups)
            total = mine + lax.ppermute(other, "tile", SWAP).astype(F32)
            x = [total[c * m : (c + 1) * m].astype(BF16) for c in range(PARTS)]
            solved += x
            if step == 0:
                x, v_rows = lax.optimization_barrier((x, v_factor[0]))
                v_pairs = v_rows.reshape(steps, reach, 2, n, width)
                v_keep = lax.dynamic_index_in_dim(v_pairs, mine_at, 2, keepdims=False)
                v_give = lax.dynamic_index_in_dim(v_pairs, other_at, 2, keepdims=False)
                v_take = lax.ppermute(v_give, "tile", SWAP)
                v_pieces = jnp.concatenate([v_keep, v_take], 1)
            part, sent = coef_product(v_pieces[step], gather(x))
            taken = lax.ppermute(sent, "tile", SWAP)
            last = step == steps - 1
            out = update(step, pivots, ranks, part, taken, residual, u_factor, n, PARTS, last)
            if not last:
                residual, held, first, final = out[0], out[1], out[2 : 2 + PARTS], out[2 + PARTS :]
        return jnp.concatenate(solved).reshape(steps, n, cols), out[None]

    return local


def gathered_steps(right_side, diag_inverse, u_factor, v_factor, ranks, pivots):
    residual = right_side[0].astype(F32)
    half = residual.shape[0]
    heights = lax.broadcasted_iota(jnp.int32, (u_factor.shape[3], 1), 0)
    me, tile = lax.axis_index("row"), lax.axis_index("tile")
    solved = []
    for step in range(pivots.shape[0]):
        current = residual.astype(BF16)
        held = lax.psum(jnp.where(me == pivots[step], current, jnp.zeros_like(current)), "row")
        other = lax.ppermute(held, "tile", SWAP)
        pivot = jnp.where(tile == 0, jnp.concatenate([held, other]), jnp.concatenate([other, held]))
        x = jnp.dot(diag_inverse[step], pivot, preferred_element_type=F32).astype(BF16)
        solved.append(x)
        x_all = lax.all_gather(x, ("row", "tile"), axis=0, tiled=True)
        x_mine = lax.dynamic_slice_in_dim(x_all, tile * half, half, 0)
        part = lax.dot_general(
            v_factor[0, step], x_mine, (((0,), (0,)), ((), ())), preferred_element_type=F32
        )
        coef = part + lax.ppermute(part, "tile", SWAP)
        finished = jnp.any(pivots[: step + 1] == me)
        kept = jnp.where(finished, 0, ranks[0, step])
        coef = jnp.where(heights < kept, coef, F32(0.0)).astype(BF16)
        residual = residual - jnp.dot(u_factor[0, step], coef, preferred_element_type=F32)
    return jnp.stack(solved), residual[None]


def solution(mesh):
    rows = mesh.shape["row"]

    def local(right_side, diag_inverse, *others):
        half, n = right_side.shape[1], diag_inverse.shape[1]
        short = rows % 2 == 0 and rows <= MOST_HOPS and n % LANES == 0 and half == rows * n
        run = ring_steps(rows, half, n) if short else gathered_steps
        return run(right_side, diag_inverse, *others)

    in_specs = (
        P(("grp", "row"), "tile", None),
        P(None, ("row", "tile"), None),
        P("row", None, "tile", None),
        P("row", None, "tile", None),
        P("row", None),
        P(),
    )
    out_specs = (P(None, ("grp", "row", "tile"), None), P(("grp", "row"), "tile", None))
    return jax.shard_map(local, mesh=mesh, in_specs=in_specs, out_specs=out_specs, check_vma=False)
```

```python
import jax
import jax.numpy as jnp
from jax import lax
from jax.experimental import pallas as pl
from jax.experimental.pallas import tpu as pltpu
from jax.sharding import PartitionSpec as P


MOST_HOPS = 8
LANES = 128
PARTS = 2
SWAP = [(0, 1), (1, 0)]
BF16 = jnp.bfloat16
F32 = jnp.float32
VMEM_GRANT = 20 * 1024 * 1024


def ring_order(rows):
    return list(range(0, rows, 2)) + list(range(rows - 1, 0, -2))


def ring_place(index, rows):
    return jnp.where(lax.rem(index, 2) == 0, lax.div(index, 2), rows - lax.div(index + 1, 2))


def ring_row(place, rows):
    return jnp.where(place < rows // 2, 2 * place, 2 * (rows - place) - 1)


def ring_distance(holder, rows):
    return lax.rem(ring_place(lax.axis_index("row"), rows) - ring_place(holder, rows) + rows, rows)


def whole_specs(count):
    return [pl.BlockSpec(memory_space=pltpu.VMEM)] * count


def in_smem(count):
    return [pl.BlockSpec(memory_space=pltpu.SMEM)] * count


def cost(flops, moved):
    return pl.CostEstimate(flops=flops, bytes_accessed=moved, transcendentals=0)


SMALL = pltpu.CompilerParams(vmem_limit_bytes=VMEM_GRANT // 4)
PARAMS = pltpu.CompilerParams(vmem_limit_bytes=VMEM_GRANT)


def holder_masks(pivots, shape):
    steps = pivots.shape[0]

    def kernel(pivots_ref, *out_refs):
        me = lax.axis_index("row")
        for p in range(steps):
            value = jnp.where(pivots_ref[p] == me, 1.0, 0.0)
            out_refs[p][...] = jnp.full(shape, value, F32).astype(BF16)

    return pl.pallas_call(
        kernel,
        out_shape=(jax.ShapeDtypeStruct(shape, BF16),) * steps,
        in_specs=in_smem(1),
        out_specs=tuple(whole_specs(steps)),
        compiler_params=SMALL,
        name="holder_masks",
    )(pivots)


def pick(mask, held, start, received):
    n = received.shape[0]

    def kernel(mask_ref, held_ref, got_ref, out_ref):
        out_ref[...] = jnp.where(mask_ref[...] > 0, held_ref[start : start + n, :], got_ref[...])

    return pl.pallas_call(
        kernel,
        out_shape=jax.ShapeDtypeStruct(received.shape, received.dtype),
        in_specs=whole_specs(3),
        out_specs=whole_specs(1)[0],
        compiler_params=SMALL,
        name="pick",
    )(mask, held, received)


def diag_give(step, pivots, diag_other, held, downs, ups):
    hops, parts = len(downs), len(downs[0])
    rows = hops + 1
    m, cols = downs[0][0].shape
    n = m * parts
    half = rows * n

    def kernel(pivots_ref, diag_ref, held_ref, *refs):
        got_refs, (other_ref, whole_ref) = refs[: 2 * hops * parts], refs[2 * hops * parts :]
        down_refs, up_refs = got_refs[: hops * parts], got_refs[hops * parts :]
        distance = ring_distance(pivots_ref[step], rows)

        @pl.when(distance == 0)
        def _():
            whole_ref[...] = held_ref[...]

        for hop in range(1, hops + 1):
            for near, at, side in (
                (distance <= hop, hop - distance, down_refs),
                (distance >= rows - hop, 2 * rows - 1 - hop - distance, up_refs),
            ):

                @pl.when(jnp.logical_and(distance > 0, near))
                def _(at=at, side=side, hop=hop):
                    for c in range(parts):
                        rows_at = pl.multiple_of(at * n + c * m, m)
                        whole_ref[pl.ds(rows_at, m), :] = side[(hop - 1) * parts + c][...]

        base = pl.multiple_of(lax.axis_index("tile") * half, half)
        other = jnp.dot(diag_ref[step, :, pl.ds(base, half)], whole_ref[...], preferred_element_type=F32)
        other_ref[...] = other.astype(BF16)

    flat = [part for side in (downs, ups) for hop in side for part in hop]
    return pl.pallas_call(
        kernel,
        out_shape=(jax.ShapeDtypeStruct((n, cols), BF16), jax.ShapeDtypeStruct((half, cols), BF16)),
        in_specs=in_smem(1) + whole_specs(2 + len(flat)),
        out_specs=tuple(whole_specs(2)),
        compiler_params=PARAMS,
        cost_estimate=cost(2 * n * half * cols, 8 * n * half),
        name="diag_give",
    )(pivots, diag_other, held, *flat)


def diag_keep(step, diag, whole):
    n = diag.shape[1]
    half, cols = whole.shape

    def kernel(diag_ref, whole_ref, out_ref):
        base = pl.multiple_of(lax.axis_index("tile") * half, half)
        out_ref[...] = jnp.dot(
            diag_ref[step, :, pl.ds(base, half)], whole_ref[...], preferred_element_type=F32
        )

    return pl.pallas_call(
        kernel,
        out_shape=jax.ShapeDtypeStruct((n, cols), F32),
        in_specs=whole_specs(2),
        out_specs=whole_specs(1)[0],
        compiler_params=PARAMS,
        cost_estimate=cost(2 * n * half * cols, 4 * n * half),
        name="diag_keep",
    )(diag, whole)


def coef_product(v_pieces, pieces):
    rows, n, width = v_pieces.shape
    parts = len(pieces[0])
    m, cols = pieces[0][0].shape
    reach = rows // 2

    def kernel(v_ref, *refs):
        piece_refs, (out_ref, sent_ref) = refs[: rows * parts], refs[rows * parts :]
        place, tile = ring_place(lax.axis_index("row"), rows), lax.axis_index("tile")
        for k in range(rows):
            row = ring_row(lax.rem(place - k + rows, rows), rows)
            at = lax.rem(row + tile * reach, rows)
            for c in range(parts):
                part = lax.dot_general(
                    v_ref[at, c * m : (c + 1) * m, :],
                    piece_refs[k * parts + c][...],
                    (((0,), (0,)), ((), ())),
                    preferred_element_type=F32,
                )
                if k == 0 and c == 0:
                    out_ref[...] = part
                else:
                    out_ref[...] += part
        sent_ref[...] = out_ref[...].astype(BF16)

    flat = [part for piece in pieces for part in piece]
    return pl.pallas_call(
        kernel,
        out_shape=(jax.ShapeDtypeStruct((width, cols), F32), jax.ShapeDtypeStruct((width, cols), BF16)),
        in_specs=whole_specs(1 + len(flat)),
        out_specs=tuple(whole_specs(2)),
        compiler_params=PARAMS,
        cost_estimate=cost(2 * rows * n * width * cols, 4 * rows * n * width),
        name="coef_product",
    )(v_pieces, *flat)


def masked_coef(step, pivots_ref, ranks_ref, part_ref, taken_ref):
    kept = ranks_ref[0, step]
    for q in range(step + 1):
        kept = jnp.where(pivots_ref[q] == lax.axis_index("row"), 0, kept)
    heights = lax.broadcasted_iota(jnp.int32, part_ref.shape, 0)
    return jnp.where(heights < kept, part_ref[...] + taken_ref[...].astype(F32), 0.0).astype(BF16)


def update_ends(step, pivots, ranks, part, taken, residual, factor, n, parts):
    half, cols = residual.shape
    m = n // parts

    def kernel(pivots_ref, ranks_ref, part_ref, taken_ref, residual_ref, u_ref, *refs):
        end_refs, coef_ref = refs[: 2 * parts], refs[2 * parts]
        coef = masked_coef(step, pivots_ref, ranks_ref, part_ref, taken_ref)
        coef_ref[...] = coef
        for i, start in enumerate((0, half - n)):
            span = slice(start, start + n)
            change = jnp.dot(u_ref[0, step, span, :], coef, preferred_element_type=F32)
            rounded = (residual_ref[span, :].astype(F32) - change).astype(BF16)
            for c in range(parts):
                end_refs[i * parts + c][...] = rounded[c * m : (c + 1) * m, :]

    ends = (jax.ShapeDtypeStruct((m, cols), BF16),) * (2 * parts)
    return pl.pallas_call(
        kernel,
        out_shape=ends + (jax.ShapeDtypeStruct(part.shape, BF16),),
        in_specs=in_smem(2) + whole_specs(4),
        out_specs=tuple(whole_specs(2 * parts + 1)),
        compiler_params=PARAMS,
        cost_estimate=cost(4 * n * part.shape[0] * cols, 8 * n * cols),
        name="update_ends",
    )(pivots, ranks, part, taken, residual, factor)


def update_whole(step, coef, residual, factor, n):
    half, cols = residual.shape

    def kernel(coef_ref, residual_ref, u_ref, out_ref, rounded_ref):
        for start in range(0, half, n):
            span = slice(start, start + n)
            change = jnp.dot(u_ref[0, step, span, :], coef_ref[...], preferred_element_type=F32)
            value = residual_ref[span, :].astype(F32) - change
            out_ref[span, :] = value
            rounded_ref[span, :] = value.astype(BF16)

    return pl.pallas_call(
        kernel,
        out_shape=(jax.ShapeDtypeStruct((half, cols), F32), jax.ShapeDtypeStruct((half, cols), BF16)),
        in_specs=whole_specs(3),
        out_specs=tuple(whole_specs(2)),
        compiler_params=PARAMS,
        cost_estimate=cost(2 * half * coef.shape[0] * cols, 8 * half * cols),
        name="update_whole",
    )(coef, residual, factor)


def update_last(step, pivots, ranks, part, taken, residual, factor, n):
    half, cols = residual.shape
    rows = half // n

    def kernel(pivots_ref, ranks_ref, part_ref, taken_ref, residual_ref, u_ref, out_ref, whole_ref, sems):
        coef = masked_coef(step, pivots_ref, ranks_ref, part_ref, taken_ref)
        copies = []
        for i in range(rows):
            span = slice(i * n, (i + 1) * n)
            change = jnp.dot(u_ref[0, step, span, :], coef, preferred_element_type=F32)
            whole_ref[span, :] = residual_ref[span, :].astype(F32) - change
            copies.append(pltpu.make_async_copy(whole_ref.at[span, :], out_ref.at[span, :], sems.at[i]))
            copies[-1].start()
        for copy in copies:
            copy.wait()

    return pl.pallas_call(
        kernel,
        out_shape=jax.ShapeDtypeStruct((half, cols), F32),
        in_specs=in_smem(2) + whole_specs(4),
        out_specs=pl.BlockSpec(memory_space=pl.ANY),
        scratch_shapes=[pltpu.VMEM((half, cols), F32), pltpu.SemaphoreType.DMA((rows,))],
        compiler_params=PARAMS,
        cost_estimate=cost(2 * half * part.shape[0] * cols, 8 * half * cols),
        name="update_last",
    )(pivots, ranks, part, taken, residual, factor)


def ring_steps(rows, half, n):
    ring = ring_order(rows)
    forward = [(ring[i], ring[(i + 1) % rows]) for i in range(rows)]
    backward = [(b, a) for a, b in forward]
    reach = rows // 2
    m = n // PARTS

    def gather(piece):
        got = [None] * rows
        got[0] = down = up = piece
        for hop in range(1, reach):
            got[hop] = down = [lax.ppermute(part, "row", forward) for part in down]
            got[rows - hop] = up = [lax.ppermute(part, "row", backward) for part in up]
        sides = [(down, forward) if c % 2 == 0 else (up, backward) for c in range(PARTS)]
        got[reach] = [lax.ppermute(side[c], "row", way) for c, (side, way) in enumerate(sides)]
        return got

    def spread(held, first, last, masks, step, beside):
        down = [lax.ppermute(part, "row", forward) for part in first]
        up = [lax.ppermute(part, "row", backward) for part in last]
        if step == 0:
            down[0], masks, beside = lax.optimization_barrier((down[0], masks, beside))
        downs, ups = [down], [up]
        for hop in range(1, rows - 1):
            down, up = list(down), list(up)
            for c in range(PARTS):
                own = pick(masks[step], held, hop * n + c * m, down[c])
                down[c] = lax.ppermute(own, "row", forward)
                own = pick(masks[step], held, (rows - 1 - hop) * n + c * m, up[c])
                up[c] = lax.ppermute(own, "row", backward)
            downs.append(down)
            ups.append(up)
        return downs, ups, masks, beside

    def local(right_side, diag_inverse, u_factor, v_factor, ranks, pivots):
        steps = pivots.shape[0]
        mine_at = lax.axis_index("tile").astype(jnp.uint32)
        other_at = 1 - mine_at
        held = residual = right_side[0]
        cols, width = held.shape[1], u_factor.shape[3]
        masks = holder_masks(pivots, (m, cols))
        diag_other = lax.ppermute(diag_inverse, "tile", SWAP)
        first = [held[c * m : (c + 1) * m] for c in range(PARTS)]
        final = [held[half - n + c * m : half - n + (c + 1) * m] for c in range(PARTS)]
        beside = (mine_at, other_at)
        solved = []
        for step in range(steps):
            downs, ups, masks, beside = spread(held, first, final, masks, step, beside)
            mine_at, other_at = beside
            other, whole = diag_give(step, pivots, diag_other, held, downs, ups)
            mine = diag_keep(step, diag_inverse, whole)
            total = mine + lax.ppermute(other, "tile", SWAP).astype(F32)
            x = [total[c * m : (c + 1) * m].astype(BF16) for c in range(PARTS)]
            solved += x
            if step == 0:
                x, v_rows = lax.optimization_barrier((x, v_factor[0]))
                v_pairs = v_rows.reshape(steps, reach, 2, n, width)
                v_keep = lax.dynamic_index_in_dim(v_pairs, mine_at, 2, keepdims=False)
                v_give = lax.dynamic_index_in_dim(v_pairs, other_at, 2, keepdims=False)
                v_take = lax.ppermute(v_give, "tile", SWAP)
                v_pieces = jnp.concatenate([v_keep, v_take], 1)
            part, sent = coef_product(v_pieces[step], gather(x))
            taken = lax.ppermute(sent, "tile", SWAP)
            if step == steps - 1:
                out = update_last(step, pivots, ranks, part, taken, residual, u_factor, n)
                continue
            *ends, coef = update_ends(step, pivots, ranks, part, taken, residual, u_factor, n, PARTS)
            first, final = ends[:PARTS], ends[PARTS:]
            residual, held = update_whole(step, coef, residual, u_factor, n)
        return jnp.concatenate(solved).reshape(steps, n, cols), out[None]

    return local


def gathered_steps(right_side, diag_inverse, u_factor, v_factor, ranks, pivots):
    residual = right_side[0].astype(F32)
    half = residual.shape[0]
    heights = lax.broadcasted_iota(jnp.int32, (u_factor.shape[3], 1), 0)
    me, tile = lax.axis_index("row"), lax.axis_index("tile")
    solved = []
    for step in range(pivots.shape[0]):
        current = residual.astype(BF16)
        held = lax.psum(jnp.where(me == pivots[step], current, jnp.zeros_like(current)), "row")
        other = lax.ppermute(held, "tile", SWAP)
        pivot = jnp.where(tile == 0, jnp.concatenate([held, other]), jnp.concatenate([other, held]))
        x = jnp.dot(diag_inverse[step], pivot, preferred_element_type=F32).astype(BF16)
        solved.append(x)
        x_all = lax.all_gather(x, ("row", "tile"), axis=0, tiled=True)
        x_mine = lax.dynamic_slice_in_dim(x_all, tile * half, half, 0)
        part = lax.dot_general(
            v_factor[0, step], x_mine, (((0,), (0,)), ((), ())), preferred_element_type=F32
        )
        coef = part + lax.ppermute(part, "tile", SWAP)
        finished = jnp.any(pivots[: step + 1] == me)
        kept = jnp.where(finished, 0, ranks[0, step])
        coef = jnp.where(heights < kept, coef, F32(0.0)).astype(BF16)
        residual = residual - jnp.dot(u_factor[0, step], coef, preferred_element_type=F32)
    return jnp.stack(solved), residual[None]


def solution(mesh):
    rows = mesh.shape["row"]

    def local(right_side, diag_inverse, *others):
        half, n = right_side.shape[1], diag_inverse.shape[1]
        short = rows % 2 == 0 and rows <= MOST_HOPS and n % LANES == 0 and half == rows * n
        run = ring_steps(rows, half, n) if short else gathered_steps
        return run(right_side, diag_inverse, *others)

    in_specs = (
        P(("grp", "row"), "tile", None),
        P(None, ("row", "tile"), None),
        P("row", None, "tile", None),
        P("row", None, "tile", None),
        P("row", None),
        P(),
    )
    out_specs = (P(None, ("grp", "row", "tile"), None), P(("grp", "row"), "tile", None))
    return jax.shard_map(local, mesh=mesh, in_specs=in_specs, out_specs=out_specs, check_vma=False)
```

```python
import jax
import jax.numpy as jnp
from jax import lax
from jax.experimental import pallas as pl
from jax.experimental.pallas import tpu as pltpu
from jax.sharding import PartitionSpec as P


MOST_HOPS = 8
LANES = 128
PARTS = 2
SWAP = [(0, 1), (1, 0)]
BF16 = jnp.bfloat16
F32 = jnp.float32
VMEM_GRANT = 20 * 1024 * 1024


def ring_order(rows):
    return list(range(0, rows, 2)) + list(range(rows - 1, 0, -2))


def ring_place(index, rows):
    return jnp.where(lax.rem(index, 2) == 0, lax.div(index, 2), rows - lax.div(index + 1, 2))


def ring_row(place, rows):
    return jnp.where(place < rows // 2, 2 * place, 2 * (rows - place) - 1)


def ring_distance(holder, rows):
    return lax.rem(ring_place(lax.axis_index("row"), rows) - ring_place(holder, rows) + rows, rows)


def whole_specs(count):
    return [pl.BlockSpec(memory_space=pltpu.VMEM)] * count


def in_smem(count):
    return [pl.BlockSpec(memory_space=pltpu.SMEM)] * count


def cost(flops, moved):
    return pl.CostEstimate(flops=flops, bytes_accessed=moved, transcendentals=0)


SMALL = pltpu.CompilerParams(vmem_limit_bytes=VMEM_GRANT // 4)
PARAMS = pltpu.CompilerParams(vmem_limit_bytes=VMEM_GRANT)


def holder_masks(pivots, shape):
    steps = pivots.shape[0]

    def kernel(pivots_ref, *out_refs):
        me = lax.axis_index("row")
        for p in range(steps):
            value = jnp.where(pivots_ref[p] == me, 1.0, 0.0)
            out_refs[p][...] = jnp.full(shape, value, F32).astype(BF16)

    return pl.pallas_call(
        kernel,
        out_shape=(jax.ShapeDtypeStruct(shape, BF16),) * steps,
        in_specs=in_smem(1),
        out_specs=tuple(whole_specs(steps)),
        compiler_params=SMALL,
        name="holder_masks",
    )(pivots)


def pick(mask, held, start, received):
    n = received.shape[0]

    def kernel(mask_ref, held_ref, got_ref, out_ref):
        out_ref[...] = jnp.where(mask_ref[...] > 0, held_ref[start : start + n, :], got_ref[...])

    return pl.pallas_call(
        kernel,
        out_shape=jax.ShapeDtypeStruct(received.shape, received.dtype),
        in_specs=whole_specs(3),
        out_specs=whole_specs(1)[0],
        compiler_params=SMALL,
        name="pick",
    )(mask, held, received)


def diag_give(step, pivots, diag_other, held, downs, ups):
    hops, parts = len(downs), len(downs[0])
    rows = hops + 1
    m, cols = downs[0][0].shape
    n = m * parts
    half = rows * n

    def kernel(pivots_ref, diag_ref, held_ref, *refs):
        got_refs, (other_ref, whole_ref, take_ref, sem) = refs[: 2 * hops * parts], refs[2 * hops * parts :]
        down_refs, up_refs = got_refs[: hops * parts], got_refs[hops * parts :]
        base = pl.multiple_of(lax.axis_index("tile") * half, half)
        fetch = pltpu.make_async_copy(diag_ref.at[step, :, pl.ds(base, half)], take_ref, sem)
        fetch.start()
        distance = ring_distance(pivots_ref[step], rows)

        @pl.when(distance == 0)
        def _():
            whole_ref[...] = held_ref[...]

        for hop in range(1, hops + 1):
            for near, at, side in (
                (distance <= hop, hop - distance, down_refs),
                (distance >= rows - hop, 2 * rows - 1 - hop - distance, up_refs),
            ):

                @pl.when(jnp.logical_and(distance > 0, near))
                def _(at=at, side=side, hop=hop):
                    for c in range(parts):
                        rows_at = pl.multiple_of(at * n + c * m, m)
                        whole_ref[pl.ds(rows_at, m), :] = side[(hop - 1) * parts + c][...]

        fetch.wait()
        other_ref[...] = jnp.dot(take_ref[...], whole_ref[...], preferred_element_type=F32).astype(BF16)

    flat = [part for side in (downs, ups) for hop in side for part in hop]
    return pl.pallas_call(
        kernel,
        out_shape=(jax.ShapeDtypeStruct((n, cols), BF16), jax.ShapeDtypeStruct((half, cols), BF16)),
        in_specs=in_smem(1) + [pl.BlockSpec(memory_space=pl.ANY)] + whole_specs(1 + len(flat)),
        out_specs=tuple(whole_specs(2)),
        scratch_shapes=[pltpu.VMEM((n, half), BF16), pltpu.SemaphoreType.DMA],
        compiler_params=PARAMS,
        cost_estimate=cost(2 * n * half * cols, 8 * n * half),
        name="diag_give",
    )(pivots, diag_other, held, *flat)


def diag_keep(step, diag, whole):
    n = diag.shape[1]
    half, cols = whole.shape

    def kernel(diag_ref, whole_ref, out_ref):
        base = pl.multiple_of(lax.axis_index("tile") * half, half)
        out_ref[...] = jnp.dot(
            diag_ref[step, :, pl.ds(base, half)], whole_ref[...], preferred_element_type=F32
        )

    return pl.pallas_call(
        kernel,
        out_shape=jax.ShapeDtypeStruct((n, cols), F32),
        in_specs=whole_specs(2),
        out_specs=whole_specs(1)[0],
        compiler_params=PARAMS,
        cost_estimate=cost(2 * n * half * cols, 4 * n * half),
        name="diag_keep",
    )(diag, whole)


def coef_product(v_pieces, pieces):
    rows, n, width = v_pieces.shape
    parts = len(pieces[0])
    m, cols = pieces[0][0].shape
    reach = rows // 2

    def kernel(v_ref, *refs):
        piece_refs, (out_ref, sent_ref) = refs[: rows * parts], refs[rows * parts :]
        place, tile = ring_place(lax.axis_index("row"), rows), lax.axis_index("tile")
        for k in range(rows):
            row = ring_row(lax.rem(place - k + rows, rows), rows)
            at = lax.rem(row + tile * reach, rows)
            for c in range(parts):
                part = lax.dot_general(
                    v_ref[at, c * m : (c + 1) * m, :],
                    piece_refs[k * parts + c][...],
                    (((0,), (0,)), ((), ())),
                    preferred_element_type=F32,
                )
                if k == 0 and c == 0:
                    out_ref[...] = part
                else:
                    out_ref[...] += part
        sent_ref[...] = out_ref[...].astype(BF16)

    flat = [part for piece in pieces for part in piece]
    return pl.pallas_call(
        kernel,
        out_shape=(jax.ShapeDtypeStruct((width, cols), F32), jax.ShapeDtypeStruct((width, cols), BF16)),
        in_specs=whole_specs(1 + len(flat)),
        out_specs=tuple(whole_specs(2)),
        compiler_params=PARAMS,
        cost_estimate=cost(2 * rows * n * width * cols, 4 * rows * n * width),
        name="coef_product",
    )(v_pieces, *flat)


def masked_coef(step, pivots_ref, ranks_ref, part_ref, taken_ref):
    kept = ranks_ref[0, step]
    for q in range(step + 1):
        kept = jnp.where(pivots_ref[q] == lax.axis_index("row"), 0, kept)
    heights = lax.broadcasted_iota(jnp.int32, part_ref.shape, 0)
    return jnp.where(heights < kept, part_ref[...] + taken_ref[...].astype(F32), 0.0).astype(BF16)


def update_ends(step, pivots, ranks, part, taken, residual, factor, n, parts):
    half, cols = residual.shape
    m = n // parts

    def kernel(pivots_ref, ranks_ref, part_ref, taken_ref, residual_ref, u_ref, *refs):
        end_refs, coef_ref = refs[: 2 * parts], refs[2 * parts]
        coef = masked_coef(step, pivots_ref, ranks_ref, part_ref, taken_ref)
        coef_ref[...] = coef
        for i, start in enumerate((0, half - n)):
            span = slice(start, start + n)
            change = jnp.dot(u_ref[0, step, span, :], coef, preferred_element_type=F32)
            rounded = (residual_ref[span, :].astype(F32) - change).astype(BF16)
            for c in range(parts):
                end_refs[i * parts + c][...] = rounded[c * m : (c + 1) * m, :]

    ends = (jax.ShapeDtypeStruct((m, cols), BF16),) * (2 * parts)
    return pl.pallas_call(
        kernel,
        out_shape=ends + (jax.ShapeDtypeStruct(part.shape, BF16),),
        in_specs=in_smem(2) + whole_specs(4),
        out_specs=tuple(whole_specs(2 * parts + 1)),
        compiler_params=PARAMS,
        cost_estimate=cost(4 * n * part.shape[0] * cols, 8 * n * cols),
        name="update_ends",
    )(pivots, ranks, part, taken, residual, factor)


def update_whole(step, coef, residual, factor, n):
    half, cols = residual.shape

    def kernel(coef_ref, residual_ref, u_ref, out_ref, rounded_ref):
        for start in range(0, half, n):
            span = slice(start, start + n)
            change = jnp.dot(u_ref[0, step, span, :], coef_ref[...], preferred_element_type=F32)
            value = residual_ref[span, :].astype(F32) - change
            out_ref[span, :] = value
            rounded_ref[span, :] = value.astype(BF16)

    return pl.pallas_call(
        kernel,
        out_shape=(jax.ShapeDtypeStruct((half, cols), F32), jax.ShapeDtypeStruct((half, cols), BF16)),
        in_specs=whole_specs(3),
        out_specs=tuple(whole_specs(2)),
        compiler_params=PARAMS,
        cost_estimate=cost(2 * half * coef.shape[0] * cols, 8 * half * cols),
        name="update_whole",
    )(coef, residual, factor)


def update_last(step, pivots, ranks, part, taken, residual, factor, n):
    half, cols = residual.shape
    rows = half // n

    def kernel(pivots_ref, ranks_ref, part_ref, taken_ref, residual_ref, u_ref, out_ref, whole_ref, sems):
        coef = masked_coef(step, pivots_ref, ranks_ref, part_ref, taken_ref)
        copies = []
        for i in range(rows):
            span = slice(i * n, (i + 1) * n)
            change = jnp.dot(u_ref[0, step, span, :], coef, preferred_element_type=F32)
            whole_ref[span, :] = residual_ref[span, :].astype(F32) - change
            copies.append(pltpu.make_async_copy(whole_ref.at[span, :], out_ref.at[span, :], sems.at[i]))
            copies[-1].start()
        for copy in copies:
            copy.wait()

    return pl.pallas_call(
        kernel,
        out_shape=jax.ShapeDtypeStruct((half, cols), F32),
        in_specs=in_smem(2) + whole_specs(4),
        out_specs=pl.BlockSpec(memory_space=pl.ANY),
        scratch_shapes=[pltpu.VMEM((half, cols), F32), pltpu.SemaphoreType.DMA((rows,))],
        compiler_params=PARAMS,
        cost_estimate=cost(2 * half * part.shape[0] * cols, 8 * half * cols),
        name="update_last",
    )(pivots, ranks, part, taken, residual, factor)


def ring_steps(rows, half, n):
    ring = ring_order(rows)
    forward = [(ring[i], ring[(i + 1) % rows]) for i in range(rows)]
    backward = [(b, a) for a, b in forward]
    reach = rows // 2
    m = n // PARTS

    def gather(piece):
        got = [None] * rows
        got[0] = down = up = piece
        for hop in range(1, reach):
            got[hop] = down = [lax.ppermute(part, "row", forward) for part in down]
            got[rows - hop] = up = [lax.ppermute(part, "row", backward) for part in up]
        sides = [(down, forward) if c % 2 == 0 else (up, backward) for c in range(PARTS)]
        got[reach] = [lax.ppermute(side[c], "row", way) for c, (side, way) in enumerate(sides)]
        return got

    def spread(held, first, last, masks, step, beside):
        down = [lax.ppermute(part, "row", forward) for part in first]
        up = [lax.ppermute(part, "row", backward) for part in last]
        if step == 0:
            down[0], masks, beside = lax.optimization_barrier((down[0], masks, beside))
        downs, ups = [down], [up]
        for hop in range(1, rows - 1):
            down, up = list(down), list(up)
            for c in range(PARTS):
                own = pick(masks[step], held, hop * n + c * m, down[c])
                down[c] = lax.ppermute(own, "row", forward)
                own = pick(masks[step], held, (rows - 1 - hop) * n + c * m, up[c])
                up[c] = lax.ppermute(own, "row", backward)
            downs.append(down)
            ups.append(up)
        return downs, ups, masks, beside

    def local(right_side, diag_inverse, u_factor, v_factor, ranks, pivots):
        steps = pivots.shape[0]
        mine_at = lax.axis_index("tile").astype(jnp.uint32)
        other_at = 1 - mine_at
        held = residual = right_side[0]
        cols, width = held.shape[1], u_factor.shape[3]
        masks = holder_masks(pivots, (m, cols))
        diag_other = lax.ppermute(diag_inverse, "tile", SWAP)
        first = [held[c * m : (c + 1) * m] for c in range(PARTS)]
        final = [held[half - n + c * m : half - n + (c + 1) * m] for c in range(PARTS)]
        beside = (mine_at, other_at)
        solved = []
        for step in range(steps):
            downs, ups, masks, beside = spread(held, first, final, masks, step, beside)
            mine_at, other_at = beside
            other, whole = diag_give(step, pivots, diag_other, held, downs, ups)
            mine = diag_keep(step, diag_inverse, whole)
            total = mine + lax.ppermute(other, "tile", SWAP).astype(F32)
            x = [total[c * m : (c + 1) * m].astype(BF16) for c in range(PARTS)]
            solved += x
            if step == 0:
                x, v_rows = lax.optimization_barrier((x, v_factor[0]))
                v_pairs = v_rows.reshape(steps, reach, 2, n, width)
                v_keep = lax.dynamic_index_in_dim(v_pairs, mine_at, 2, keepdims=False)
                v_give = lax.dynamic_index_in_dim(v_pairs, other_at, 2, keepdims=False)
                v_take = lax.ppermute(v_give, "tile", SWAP)
                v_pieces = jnp.concatenate([v_keep, v_take], 1)
            part, sent = coef_product(v_pieces[step], gather(x))
            taken = lax.ppermute(sent, "tile", SWAP)
            if step == steps - 1:
                out = update_last(step, pivots, ranks, part, taken, residual, u_factor, n)
                continue
            *ends, coef = update_ends(step, pivots, ranks, part, taken, residual, u_factor, n, PARTS)
            first, final = ends[:PARTS], ends[PARTS:]
            residual, held = update_whole(step, coef, residual, u_factor, n)
        return jnp.concatenate(solved).reshape(steps, n, cols), out[None]

    return local


def gathered_steps(right_side, diag_inverse, u_factor, v_factor, ranks, pivots):
    residual = right_side[0].astype(F32)
    half = residual.shape[0]
    heights = lax.broadcasted_iota(jnp.int32, (u_factor.shape[3], 1), 0)
    me, tile = lax.axis_index("row"), lax.axis_index("tile")
    solved = []
    for step in range(pivots.shape[0]):
        current = residual.astype(BF16)
        held = lax.psum(jnp.where(me == pivots[step], current, jnp.zeros_like(current)), "row")
        other = lax.ppermute(held, "tile", SWAP)
        pivot = jnp.where(tile == 0, jnp.concatenate([held, other]), jnp.concatenate([other, held]))
        x = jnp.dot(diag_inverse[step], pivot, preferred_element_type=F32).astype(BF16)
        solved.append(x)
        x_all = lax.all_gather(x, ("row", "tile"), axis=0, tiled=True)
        x_mine = lax.dynamic_slice_in_dim(x_all, tile * half, half, 0)
        part = lax.dot_general(
            v_factor[0, step], x_mine, (((0,), (0,)), ((), ())), preferred_element_type=F32
        )
        coef = part + lax.ppermute(part, "tile", SWAP)
        finished = jnp.any(pivots[: step + 1] == me)
        kept = jnp.where(finished, 0, ranks[0, step])
        coef = jnp.where(heights < kept, coef, F32(0.0)).astype(BF16)
        residual = residual - jnp.dot(u_factor[0, step], coef, preferred_element_type=F32)
    return jnp.stack(solved), residual[None]


def solution(mesh):
    rows = mesh.shape["row"]

    def local(right_side, diag_inverse, *others):
        half, n = right_side.shape[1], diag_inverse.shape[1]
        short = rows % 2 == 0 and rows <= MOST_HOPS and n % LANES == 0 and half == rows * n
        run = ring_steps(rows, half, n) if short else gathered_steps
        return run(right_side, diag_inverse, *others)

    in_specs = (
        P(("grp", "row"), "tile", None),
        P(None, ("row", "tile"), None),
        P("row", None, "tile", None),
        P("row", None, "tile", None),
        P("row", None),
        P(),
    )
    out_specs = (P(None, ("grp", "row", "tile"), None), P(("grp", "row"), "tile", None))
    return jax.shard_map(local, mesh=mesh, in_specs=in_specs, out_specs=out_specs, check_vma=False)
```

```python
import jax
import jax.numpy as jnp
from jax import lax
from jax.experimental import pallas as pl
from jax.experimental.pallas import tpu as pltpu
from jax.sharding import PartitionSpec as P


MOST_HOPS = 8
LANES = 128
PARTS = 2
SWAP = [(0, 1), (1, 0)]
BF16 = jnp.bfloat16
F32 = jnp.float32
VMEM_GRANT = 20 * 1024 * 1024


def ring_order(rows):
    return list(range(0, rows, 2)) + list(range(rows - 1, 0, -2))


def ring_place(index, rows):
    return jnp.where(lax.rem(index, 2) == 0, lax.div(index, 2), rows - lax.div(index + 1, 2))


def ring_row(place, rows):
    return jnp.where(place < rows // 2, 2 * place, 2 * (rows - place) - 1)


def ring_distance(holder, rows):
    return lax.rem(ring_place(lax.axis_index("row"), rows) - ring_place(holder, rows) + rows, rows)


def half_held(distance):
    return lax.rem(lax.axis_index("tile") + distance, 2)


def whole_specs(count):
    return [pl.BlockSpec(memory_space=pltpu.VMEM)] * count


def in_smem(count):
    return [pl.BlockSpec(memory_space=pltpu.SMEM)] * count


def cost(flops, moved):
    return pl.CostEstimate(flops=flops, bytes_accessed=moved, transcendentals=0)


SMALL = pltpu.CompilerParams(vmem_limit_bytes=VMEM_GRANT // 4)
PARAMS = pltpu.CompilerParams(vmem_limit_bytes=VMEM_GRANT)


def holder_masks(pivots, shape, rows):
    steps = pivots.shape[0]
    reach = rows // 2
    sides_shape = (-(-reach // 8) * 8, LANES)

    def kernel(pivots_ref, *out_refs):
        me, tile = lax.axis_index("row"), lax.axis_index("tile")
        for p in range(steps):
            value = jnp.where(pivots_ref[p] == me, 1.0, 0.0)
            out_refs[p][...] = jnp.full(shape, value, F32).astype(BF16)
        heights = lax.broadcasted_iota(jnp.int32, sides_shape, 0)
        sides = jnp.zeros(sides_shape, jnp.int32)
        for i in range(reach):
            hops = ring_distance(tile * reach + i, rows)
            sides = jnp.where(heights == i, lax.rem(tile + hops, 2), sides)
        out_refs[steps][...] = sides

    out = pl.pallas_call(
        kernel,
        out_shape=(jax.ShapeDtypeStruct(shape, BF16),) * steps + (jax.ShapeDtypeStruct(sides_shape, jnp.int32),),
        in_specs=in_smem(1),
        out_specs=tuple(whole_specs(steps + 1)),
        compiler_params=SMALL,
        name="holder_masks",
    )(pivots)
    return out[:steps], out[steps][:reach, :1]


def pick(mask, held, start, received):
    n = received.shape[0]

    def kernel(mask_ref, held_ref, got_ref, out_ref):
        out_ref[...] = jnp.where(mask_ref[...] > 0, held_ref[start : start + n, :], got_ref[...])

    return pl.pallas_call(
        kernel,
        out_shape=jax.ShapeDtypeStruct(received.shape, received.dtype),
        in_specs=whole_specs(3),
        out_specs=whole_specs(1)[0],
        compiler_params=SMALL,
        name="pick",
    )(mask, held, received)


def diag_give(step, pivots, diag_other, held, downs, ups):
    hops, parts = len(downs), len(downs[0])
    rows = hops + 1
    m, cols = downs[0][0].shape
    n = m * parts
    half = rows * n

    def kernel(pivots_ref, diag_ref, held_ref, *refs):
        got_refs, (other_ref, whole_ref, take_ref, sem) = refs[: 2 * hops * parts], refs[2 * hops * parts :]
        down_refs, up_refs = got_refs[: hops * parts], got_refs[hops * parts :]
        distance = ring_distance(pivots_ref[step], rows)
        base = pl.multiple_of(half_held(distance) * half, half)
        fetch = pltpu.make_async_copy(diag_ref.at[step, :, pl.ds(base, half)], take_ref, sem)
        fetch.start()

        @pl.when(distance == 0)
        def _():
            whole_ref[...] = held_ref[...]

        for hop in range(1, hops + 1):
            for near, at, side in (
                (distance <= hop, hop - distance, down_refs),
                (distance >= rows - hop, 2 * rows - 1 - hop - distance, up_refs),
            ):

                @pl.when(jnp.logical_and(distance > 0, near))
                def _(at=at, side=side, hop=hop):
                    for c in range(parts):
                        rows_at = pl.multiple_of(at * n + c * m, m)
                        whole_ref[pl.ds(rows_at, m), :] = side[(hop - 1) * parts + c][...]

        fetch.wait()
        other_ref[...] = jnp.dot(take_ref[...], whole_ref[...], preferred_element_type=F32).astype(BF16)

    flat = [part for side in (downs, ups) for hop in side for part in hop]
    return pl.pallas_call(
        kernel,
        out_shape=(jax.ShapeDtypeStruct((n, cols), BF16), jax.ShapeDtypeStruct((half, cols), BF16)),
        in_specs=in_smem(1) + [pl.BlockSpec(memory_space=pl.ANY)] + whole_specs(1 + len(flat)),
        out_specs=tuple(whole_specs(2)),
        scratch_shapes=[pltpu.VMEM((n, half), BF16), pltpu.SemaphoreType.DMA],
        compiler_params=PARAMS,
        cost_estimate=cost(2 * n * half * cols, 8 * n * half),
        name="diag_give",
    )(pivots, diag_other, held, *flat)


def diag_keep(step, rows, pivots, diag, whole):
    n = diag.shape[1]
    half, cols = whole.shape

    def kernel(pivots_ref, diag_ref, whole_ref, out_ref):
        base = pl.multiple_of(half_held(ring_distance(pivots_ref[step], rows)) * half, half)
        out_ref[...] = jnp.dot(
            diag_ref[step, :, pl.ds(base, half)], whole_ref[...], preferred_element_type=F32
        )

    return pl.pallas_call(
        kernel,
        out_shape=jax.ShapeDtypeStruct((n, cols), F32),
        in_specs=in_smem(1) + whole_specs(2),
        out_specs=whole_specs(1)[0],
        compiler_params=PARAMS,
        cost_estimate=cost(2 * n * half * cols, 4 * n * half),
        name="diag_keep",
    )(pivots, diag, whole)


def coef_product(v_pieces, pieces):
    rows, n, width = v_pieces.shape
    parts = len(pieces[0])
    m, cols = pieces[0][0].shape
    reach = rows // 2

    def kernel(v_ref, *refs):
        piece_refs, (out_ref, sent_ref) = refs[: rows * parts], refs[rows * parts :]
        place, tile = ring_place(lax.axis_index("row"), rows), lax.axis_index("tile")
        for k in range(rows):
            row = ring_row(lax.rem(place - k + rows, rows), rows)
            at = lax.rem(row + tile * reach, rows)
            for c in range(parts):
                part = lax.dot_general(
                    v_ref[at, c * m : (c + 1) * m, :],
                    piece_refs[k * parts + c][...],
                    (((0,), (0,)), ((), ())),
                    preferred_element_type=F32,
                )
                if k == 0 and c == 0:
                    out_ref[...] = part
                else:
                    out_ref[...] += part
        sent_ref[...] = out_ref[...].astype(BF16)

    flat = [part for piece in pieces for part in piece]
    return pl.pallas_call(
        kernel,
        out_shape=(jax.ShapeDtypeStruct((width, cols), F32), jax.ShapeDtypeStruct((width, cols), BF16)),
        in_specs=whole_specs(1 + len(flat)),
        out_specs=tuple(whole_specs(2)),
        compiler_params=PARAMS,
        cost_estimate=cost(2 * rows * n * width * cols, 4 * rows * n * width),
        name="coef_product",
    )(v_pieces, *flat)


def masked_coef(step, pivots_ref, ranks_ref, part_ref, taken_ref):
    kept = ranks_ref[0, step]
    for q in range(step + 1):
        kept = jnp.where(pivots_ref[q] == lax.axis_index("row"), 0, kept)
    heights = lax.broadcasted_iota(jnp.int32, part_ref.shape, 0)
    return jnp.where(heights < kept, part_ref[...] + taken_ref[...].astype(F32), 0.0).astype(BF16)


def update_ends(step, pivots, ranks, part, taken, residual, factor, n, parts):
    half, cols = residual.shape
    m = n // parts

    def kernel(pivots_ref, ranks_ref, part_ref, taken_ref, residual_ref, u_ref, *refs):
        end_refs, coef_ref = refs[: 2 * parts], refs[2 * parts]
        coef = masked_coef(step, pivots_ref, ranks_ref, part_ref, taken_ref)
        coef_ref[...] = coef
        for i, start in enumerate((0, half - n)):
            span = slice(start, start + n)
            change = jnp.dot(u_ref[0, step, span, :], coef, preferred_element_type=F32)
            rounded = (residual_ref[span, :].astype(F32) - change).astype(BF16)
            for c in range(parts):
                end_refs[i * parts + c][...] = rounded[c * m : (c + 1) * m, :]

    ends = (jax.ShapeDtypeStruct((m, cols), BF16),) * (2 * parts)
    return pl.pallas_call(
        kernel,
        out_shape=ends + (jax.ShapeDtypeStruct(part.shape, BF16),),
        in_specs=in_smem(2) + whole_specs(4),
        out_specs=tuple(whole_specs(2 * parts + 1)),
        compiler_params=PARAMS,
        cost_estimate=cost(4 * n * part.shape[0] * cols, 8 * n * cols),
        name="update_ends",
    )(pivots, ranks, part, taken, residual, factor)


def update_whole(step, coef, residual, factor, n):
    half, cols = residual.shape

    def kernel(coef_ref, residual_ref, u_ref, out_ref, rounded_ref):
        for start in range(0, half, n):
            span = slice(start, start + n)
            change = jnp.dot(u_ref[0, step, span, :], coef_ref[...], preferred_element_type=F32)
            value = residual_ref[span, :].astype(F32) - change
            out_ref[span, :] = value
            rounded_ref[span, :] = value.astype(BF16)

    return pl.pallas_call(
        kernel,
        out_shape=(jax.ShapeDtypeStruct((half, cols), F32), jax.ShapeDtypeStruct((half, cols), BF16)),
        in_specs=whole_specs(3),
        out_specs=tuple(whole_specs(2)),
        compiler_params=PARAMS,
        cost_estimate=cost(2 * half * coef.shape[0] * cols, 8 * half * cols),
        name="update_whole",
    )(coef, residual, factor)


def update_last(step, pivots, ranks, part, taken, residual, factor, n):
    half, cols = residual.shape
    rows = half // n

    def kernel(pivots_ref, ranks_ref, part_ref, taken_ref, residual_ref, u_ref, out_ref, whole_ref, sems):
        coef = masked_coef(step, pivots_ref, ranks_ref, part_ref, taken_ref)
        copies = []
        for i in range(rows):
            span = slice(i * n, (i + 1) * n)
            change = jnp.dot(u_ref[0, step, span, :], coef, preferred_element_type=F32)
            whole_ref[span, :] = residual_ref[span, :].astype(F32) - change
            copies.append(pltpu.make_async_copy(whole_ref.at[span, :], out_ref.at[span, :], sems.at[i]))
            copies[-1].start()
        for copy in copies:
            copy.wait()

    return pl.pallas_call(
        kernel,
        out_shape=jax.ShapeDtypeStruct((half, cols), F32),
        in_specs=in_smem(2) + whole_specs(4),
        out_specs=pl.BlockSpec(memory_space=pl.ANY),
        scratch_shapes=[pltpu.VMEM((half, cols), F32), pltpu.SemaphoreType.DMA((rows,))],
        compiler_params=PARAMS,
        cost_estimate=cost(2 * half * part.shape[0] * cols, 8 * half * cols),
        name="update_last",
    )(pivots, ranks, part, taken, residual, factor)


def ring_steps(rows, half, n):
    ring = ring_order(rows)
    links = [(ring[i], ring[(i + 1) % rows]) for i in range(rows)]
    forward = [(2 * a + tile, 2 * b + 1 - tile) for a, b in links for tile in range(2)]
    backward = [(b, a) for a, b in forward]
    reach = rows // 2
    m = n // PARTS

    def hop_to(value, way):
        return lax.ppermute(value, ("row", "tile"), way)

    def gather(piece):
        got = [None] * rows
        got[0] = down = up = piece
        for hop in range(1, reach):
            got[hop] = down = [hop_to(part, forward) for part in down]
            got[rows - hop] = up = [hop_to(part, backward) for part in up]
        sides = [(down, forward) if c % 2 == 0 else (up, backward) for c in range(PARTS)]
        got[reach] = [hop_to(side[c], way) for c, (side, way) in enumerate(sides)]
        return got

    def spread(held, first, last, masks, step):
        down = [hop_to(part, forward) for part in first]
        up = [hop_to(part, backward) for part in last]
        if step == 0:
            down[0], masks = lax.optimization_barrier((down[0], masks))
        downs, ups = [down], [up]
        for hop in range(1, rows - 1):
            down, up = list(down), list(up)
            for c in range(PARTS):
                own = pick(masks[step], held, hop * n + c * m, down[c])
                down[c] = hop_to(own, forward)
                own = pick(masks[step], held, (rows - 1 - hop) * n + c * m, up[c])
                up[c] = hop_to(own, backward)
            downs.append(down)
            ups.append(up)
        return downs, ups, masks

    def local(right_side, diag_inverse, u_factor, v_factor, ranks, pivots):
        steps = pivots.shape[0]
        held = residual = right_side[0]
        cols, width = held.shape[1], u_factor.shape[3]
        masks, sides = holder_masks(pivots, (m, cols), rows)
        diag_other = lax.ppermute(diag_inverse, "tile", SWAP)
        first = [held[c * m : (c + 1) * m] for c in range(PARTS)]
        final = [held[half - n + c * m : half - n + (c + 1) * m] for c in range(PARTS)]
        solved = []
        for step in range(steps):
            downs, ups, masks = spread(held, first, final, masks, step)
            other, whole = diag_give(step, pivots, diag_other, held, downs, ups)
            mine = diag_keep(step, rows, pivots, diag_inverse, whole)
            total = mine + lax.ppermute(other, "tile", SWAP).astype(F32)
            x = [total[c * m : (c + 1) * m].astype(BF16) for c in range(PARTS)]
            solved += x
            if step == 0:
                x, v_rows = lax.optimization_barrier((x, v_factor[0]))
                v_pairs = v_rows.reshape(steps, reach, 2, n, width)
                upper = sides[None, :, :, None] == 1
                v_keep = jnp.where(upper, v_pairs[:, :, 1], v_pairs[:, :, 0])
                v_give = jnp.where(upper, v_pairs[:, :, 0], v_pairs[:, :, 1])
                v_take = lax.ppermute(v_give, "tile", SWAP)
                v_pieces = jnp.concatenate([v_keep, v_take], 1)
            part, sent = coef_product(v_pieces[step], gather(x))
            taken = lax.ppermute(sent, "tile", SWAP)
            if step == steps - 1:
                out = update_last(step, pivots, ranks, part, taken, residual, u_factor, n)
                continue
            *ends, coef = update_ends(step, pivots, ranks, part, taken, residual, u_factor, n, PARTS)
            first, final = ends[:PARTS], ends[PARTS:]
            residual, held = update_whole(step, coef, residual, u_factor, n)
        return jnp.concatenate(solved).reshape(steps, n, cols), out[None]

    return local


def gathered_steps(right_side, diag_inverse, u_factor, v_factor, ranks, pivots):
    residual = right_side[0].astype(F32)
    half = residual.shape[0]
    heights = lax.broadcasted_iota(jnp.int32, (u_factor.shape[3], 1), 0)
    me, tile = lax.axis_index("row"), lax.axis_index("tile")
    solved = []
    for step in range(pivots.shape[0]):
        current = residual.astype(BF16)
        held = lax.psum(jnp.where(me == pivots[step], current, jnp.zeros_like(current)), "row")
        other = lax.ppermute(held, "tile", SWAP)
        pivot = jnp.where(tile == 0, jnp.concatenate([held, other]), jnp.concatenate([other, held]))
        x = jnp.dot(diag_inverse[step], pivot, preferred_element_type=F32).astype(BF16)
        solved.append(x)
        x_all = lax.all_gather(x, ("row", "tile"), axis=0, tiled=True)
        x_mine = lax.dynamic_slice_in_dim(x_all, tile * half, half, 0)
        part = lax.dot_general(
            v_factor[0, step], x_mine, (((0,), (0,)), ((), ())), preferred_element_type=F32
        )
        coef = part + lax.ppermute(part, "tile", SWAP)
        finished = jnp.any(pivots[: step + 1] == me)
        kept = jnp.where(finished, 0, ranks[0, step])
        coef = jnp.where(heights < kept, coef, F32(0.0)).astype(BF16)
        residual = residual - jnp.dot(u_factor[0, step], coef, preferred_element_type=F32)
    return jnp.stack(solved), residual[None]


def solution(mesh):
    rows = mesh.shape["row"]

    def local(right_side, diag_inverse, *others):
        half, n = right_side.shape[1], diag_inverse.shape[1]
        short = rows % 2 == 0 and rows <= MOST_HOPS and n % LANES == 0 and half == rows * n
        run = ring_steps(rows, half, n) if short else gathered_steps
        return run(right_side, diag_inverse, *others)

    in_specs = (
        P(("grp", "row"), "tile", None),
        P(None, ("row", "tile"), None),
        P("row", None, "tile", None),
        P("row", None, "tile", None),
        P("row", None),
        P(),
    )
    out_specs = (P(None, ("grp", "row", "tile"), None), P(("grp", "row"), "tile", None))
    return jax.shard_map(local, mesh=mesh, in_specs=in_specs, out_specs=out_specs, check_vma=False)
```

```python
import jax
import jax.numpy as jnp
from jax import lax
from jax.experimental import pallas as pl
from jax.experimental.pallas import tpu as pltpu
from jax.sharding import PartitionSpec as P


MOST_HOPS = 8
LANES = 128
PARTS = 2
SWAP = [(0, 1), (1, 0)]
BF16 = jnp.bfloat16
F32 = jnp.float32
VMEM_GRANT = 20 * 1024 * 1024


def ring_order(rows):
    return list(range(0, rows, 2)) + list(range(rows - 1, 0, -2))


def ring_place(index, rows):
    return jnp.where(lax.rem(index, 2) == 0, lax.div(index, 2), rows - lax.div(index + 1, 2))


def ring_row(place, rows):
    return jnp.where(place < rows // 2, 2 * place, 2 * (rows - place) - 1)


def ring_distance(holder, rows):
    return lax.rem(ring_place(lax.axis_index("row"), rows) - ring_place(holder, rows) + rows, rows)


def half_held(distance):
    return lax.rem(lax.axis_index("tile") + distance, 2)


def whole_specs(count):
    return [pl.BlockSpec(memory_space=pltpu.VMEM)] * count


def in_smem(count):
    return [pl.BlockSpec(memory_space=pltpu.SMEM)] * count


def cost(flops, moved):
    return pl.CostEstimate(flops=flops, bytes_accessed=moved, transcendentals=0)


SMALL = pltpu.CompilerParams(vmem_limit_bytes=VMEM_GRANT // 4)
PARAMS = pltpu.CompilerParams(vmem_limit_bytes=VMEM_GRANT)


def holder_masks(pivots, shape, rows):
    steps = pivots.shape[0]
    reach = rows // 2
    sides_shape = (-(-reach // 8) * 8, LANES)

    def kernel(pivots_ref, *out_refs):
        me, tile = lax.axis_index("row"), lax.axis_index("tile")
        for p in range(steps):
            value = jnp.where(pivots_ref[p] == me, 1.0, 0.0)
            out_refs[p][...] = jnp.full(shape, value, F32).astype(BF16)
        heights = lax.broadcasted_iota(jnp.int32, sides_shape, 0)
        sides = jnp.zeros(sides_shape, jnp.int32)
        for i in range(reach):
            hops = ring_distance(tile * reach + i, rows)
            sides = jnp.where(heights == i, lax.rem(tile + hops, 2), sides)
        out_refs[steps][...] = sides

    out = pl.pallas_call(
        kernel,
        out_shape=(jax.ShapeDtypeStruct(shape, BF16),) * steps + (jax.ShapeDtypeStruct(sides_shape, jnp.int32),),
        in_specs=in_smem(1),
        out_specs=tuple(whole_specs(steps + 1)),
        compiler_params=SMALL,
        name="holder_masks",
    )(pivots)
    return out[:steps], out[steps][:reach, :1]


def pick(mask, held, start, received):
    n = received.shape[0]

    def kernel(mask_ref, held_ref, got_ref, out_ref):
        out_ref[...] = jnp.where(mask_ref[...] > 0, held_ref[start : start + n, :], got_ref[...])

    return pl.pallas_call(
        kernel,
        out_shape=jax.ShapeDtypeStruct(received.shape, received.dtype),
        in_specs=whole_specs(3),
        out_specs=whole_specs(1)[0],
        compiler_params=SMALL,
        name="pick",
    )(mask, held, received)


def diag_give(step, pivots, diag_other, held, downs, ups):
    hops, parts = len(downs), len(downs[0])
    rows = hops + 1
    m, cols = downs[0][0].shape
    n = m * parts
    half = rows * n

    def kernel(pivots_ref, diag_ref, held_ref, *refs):
        got_refs, (other_ref, whole_ref, take_ref, sem) = refs[: 2 * hops * parts], refs[2 * hops * parts :]
        down_refs, up_refs = got_refs[: hops * parts], got_refs[hops * parts :]
        distance = ring_distance(pivots_ref[step], rows)
        base = pl.multiple_of(half_held(distance) * half, half)
        fetch = pltpu.make_async_copy(diag_ref.at[step, :, pl.ds(base, half)], take_ref, sem)
        fetch.start()

        @pl.when(distance == 0)
        def _():
            whole_ref[...] = held_ref[...]

        for hop in range(1, hops + 1):
            for near, at, side in (
                (distance <= hop, hop - distance, down_refs),
                (distance >= rows - hop, 2 * rows - 1 - hop - distance, up_refs),
            ):

                @pl.when(jnp.logical_and(distance > 0, near))
                def _(at=at, side=side, hop=hop):
                    for c in range(parts):
                        rows_at = pl.multiple_of(at * n + c * m, m)
                        whole_ref[pl.ds(rows_at, m), :] = side[(hop - 1) * parts + c][...]

        fetch.wait()
        other_ref[...] = jnp.dot(take_ref[...], whole_ref[...], preferred_element_type=F32).astype(BF16)

    flat = [part for side in (downs, ups) for hop in side for part in hop]
    return pl.pallas_call(
        kernel,
        out_shape=(jax.ShapeDtypeStruct((n, cols), BF16), jax.ShapeDtypeStruct((half, cols), BF16)),
        in_specs=in_smem(1) + [pl.BlockSpec(memory_space=pl.ANY)] + whole_specs(1 + len(flat)),
        out_specs=tuple(whole_specs(2)),
        scratch_shapes=[pltpu.VMEM((n, half), BF16), pltpu.SemaphoreType.DMA],
        compiler_params=PARAMS,
        cost_estimate=cost(2 * n * half * cols, 8 * n * half),
        name="diag_give",
    )(pivots, diag_other, held, *flat)


def diag_keep(step, rows, pivots, diag, whole):
    n = diag.shape[1]
    half, cols = whole.shape

    def kernel(pivots_ref, diag_ref, whole_ref, out_ref):
        base = pl.multiple_of(half_held(ring_distance(pivots_ref[step], rows)) * half, half)
        out_ref[...] = jnp.dot(
            diag_ref[step, :, pl.ds(base, half)], whole_ref[...], preferred_element_type=F32
        )

    return pl.pallas_call(
        kernel,
        out_shape=jax.ShapeDtypeStruct((n, cols), F32),
        in_specs=in_smem(1) + whole_specs(2),
        out_specs=whole_specs(1)[0],
        compiler_params=PARAMS,
        cost_estimate=cost(2 * n * half * cols, 4 * n * half),
        name="diag_keep",
    )(pivots, diag, whole)


def coef_product(v_pieces, places, pieces, before=None):
    rows, n, width = v_pieces.shape
    parts = len(pieces[places[0]])
    m, cols = pieces[places[0]][0].shape
    reach = rows // 2
    flat = [part for k in places for part in pieces[k]]
    final = before is not None

    def kernel(v_ref, *refs):
        piece_refs, refs = refs[: len(flat)], refs[len(flat) :]
        out_ref = refs[1] if final else refs[0]
        place, tile = ring_place(lax.axis_index("row"), rows), lax.axis_index("tile")
        for i, k in enumerate(places):
            row = ring_row(lax.rem(place - k + rows, rows), rows)
            at = lax.rem(row + tile * reach, rows)
            for c in range(parts):
                part = lax.dot_general(
                    v_ref[at, c * m : (c + 1) * m, :],
                    piece_refs[i * parts + c][...],
                    (((0,), (0,)), ((), ())),
                    preferred_element_type=F32,
                )
                if i == 0 and c == 0:
                    out_ref[...] = refs[0][...] + part if final else part
                else:
                    out_ref[...] += part
        if final:
            refs[2][...] = out_ref[...].astype(BF16)

    full = jax.ShapeDtypeStruct((width, cols), F32)
    return pl.pallas_call(
        kernel,
        out_shape=(full, jax.ShapeDtypeStruct((width, cols), BF16)) if final else full,
        in_specs=whole_specs(1 + len(flat) + int(final)),
        out_specs=tuple(whole_specs(2)) if final else whole_specs(1)[0],
        compiler_params=PARAMS,
        cost_estimate=cost(2 * len(places) * n * width * cols, 4 * len(places) * n * width),
        name="coef_product",
    )(v_pieces, *flat, *([before] if final else []))


def masked_coef(step, pivots_ref, ranks_ref, part_ref, taken_ref):
    kept = ranks_ref[0, step]
    for q in range(step + 1):
        kept = jnp.where(pivots_ref[q] == lax.axis_index("row"), 0, kept)
    heights = lax.broadcasted_iota(jnp.int32, part_ref.shape, 0)
    return jnp.where(heights < kept, part_ref[...] + taken_ref[...].astype(F32), 0.0).astype(BF16)


def update_ends(step, pivots, ranks, part, taken, residual, factor, n, parts):
    half, cols = residual.shape
    m = n // parts

    def kernel(pivots_ref, ranks_ref, part_ref, taken_ref, residual_ref, u_ref, *refs):
        end_refs, coef_ref = refs[: 2 * parts], refs[2 * parts]
        coef = masked_coef(step, pivots_ref, ranks_ref, part_ref, taken_ref)
        coef_ref[...] = coef
        for i, start in enumerate((0, half - n)):
            span = slice(start, start + n)
            change = jnp.dot(u_ref[0, step, span, :], coef, preferred_element_type=F32)
            rounded = (residual_ref[span, :].astype(F32) - change).astype(BF16)
            for c in range(parts):
                end_refs[i * parts + c][...] = rounded[c * m : (c + 1) * m, :]

    ends = (jax.ShapeDtypeStruct((m, cols), BF16),) * (2 * parts)
    return pl.pallas_call(
        kernel,
        out_shape=ends + (jax.ShapeDtypeStruct(part.shape, BF16),),
        in_specs=in_smem(2) + whole_specs(4),
        out_specs=tuple(whole_specs(2 * parts + 1)),
        compiler_params=PARAMS,
        cost_estimate=cost(4 * n * part.shape[0] * cols, 8 * n * cols),
        name="update_ends",
    )(pivots, ranks, part, taken, residual, factor)


def update_whole(step, coef, residual, factor, n):
    half, cols = residual.shape

    def kernel(coef_ref, residual_ref, u_ref, out_ref, rounded_ref):
        for start in range(0, half, n):
            span = slice(start, start + n)
            change = jnp.dot(u_ref[0, step, span, :], coef_ref[...], preferred_element_type=F32)
            value = residual_ref[span, :].astype(F32) - change
            out_ref[span, :] = value
            rounded_ref[span, :] = value.astype(BF16)

    return pl.pallas_call(
        kernel,
        out_shape=(jax.ShapeDtypeStruct((half, cols), F32), jax.ShapeDtypeStruct((half, cols), BF16)),
        in_specs=whole_specs(3),
        out_specs=tuple(whole_specs(2)),
        compiler_params=PARAMS,
        cost_estimate=cost(2 * half * coef.shape[0] * cols, 8 * half * cols),
        name="update_whole",
    )(coef, residual, factor)


def update_last(step, pivots, ranks, part, taken, residual, factor, n):
    half, cols = residual.shape
    rows = half // n

    def kernel(pivots_ref, ranks_ref, part_ref, taken_ref, residual_ref, u_ref, out_ref, whole_ref, sems):
        coef = masked_coef(step, pivots_ref, ranks_ref, part_ref, taken_ref)
        copies = []
        for i in range(rows):
            span = slice(i * n, (i + 1) * n)
            change = jnp.dot(u_ref[0, step, span, :], coef, preferred_element_type=F32)
            whole_ref[span, :] = residual_ref[span, :].astype(F32) - change
            copies.append(pltpu.make_async_copy(whole_ref.at[span, :], out_ref.at[span, :], sems.at[i]))
            copies[-1].start()
        for copy in copies:
            copy.wait()

    return pl.pallas_call(
        kernel,
        out_shape=jax.ShapeDtypeStruct((half, cols), F32),
        in_specs=in_smem(2) + whole_specs(4),
        out_specs=pl.BlockSpec(memory_space=pl.ANY),
        scratch_shapes=[pltpu.VMEM((half, cols), F32), pltpu.SemaphoreType.DMA((rows,))],
        compiler_params=PARAMS,
        cost_estimate=cost(2 * half * part.shape[0] * cols, 8 * half * cols),
        name="update_last",
    )(pivots, ranks, part, taken, residual, factor)


def ring_steps(rows, half, n):
    ring = ring_order(rows)
    links = [(ring[i], ring[(i + 1) % rows]) for i in range(rows)]
    forward = [(2 * a + tile, 2 * b + 1 - tile) for a, b in links for tile in range(2)]
    backward = [(b, a) for a, b in forward]
    reach = rows // 2
    m = n // PARTS

    def hop_to(value, way):
        return lax.ppermute(value, ("row", "tile"), way)

    def gather(piece):
        got = [None] * rows
        got[0] = down = up = piece
        for hop in range(1, reach):
            got[hop] = down = [hop_to(part, forward) for part in down]
            got[rows - hop] = up = [hop_to(part, backward) for part in up]
        sides = [(down, forward) if c % 2 == 0 else (up, backward) for c in range(PARTS)]
        got[reach] = [hop_to(side[c], way) for c, (side, way) in enumerate(sides)]
        return got

    def spread(held, first, last, masks, step):
        down = [hop_to(part, forward) for part in first]
        up = [hop_to(part, backward) for part in last]
        if step == 0:
            down[0], masks = lax.optimization_barrier((down[0], masks))
        downs, ups = [down], [up]
        for hop in range(1, rows - 1):
            down, up = list(down), list(up)
            for c in range(PARTS):
                own = pick(masks[step], held, hop * n + c * m, down[c])
                down[c] = hop_to(own, forward)
                own = pick(masks[step], held, (rows - 1 - hop) * n + c * m, up[c])
                up[c] = hop_to(own, backward)
            downs.append(down)
            ups.append(up)
        return downs, ups, masks

    def local(right_side, diag_inverse, u_factor, v_factor, ranks, pivots):
        steps = pivots.shape[0]
        held = residual = right_side[0]
        cols, width = held.shape[1], u_factor.shape[3]
        masks, sides = holder_masks(pivots, (m, cols), rows)
        diag_other = lax.ppermute(diag_inverse, "tile", SWAP)
        first = [held[c * m : (c + 1) * m] for c in range(PARTS)]
        final = [held[half - n + c * m : half - n + (c + 1) * m] for c in range(PARTS)]
        solved = []
        for step in range(steps):
            downs, ups, masks = spread(held, first, final, masks, step)
            other, whole = diag_give(step, pivots, diag_other, held, downs, ups)
            mine = diag_keep(step, rows, pivots, diag_inverse, whole)
            total = mine + lax.ppermute(other, "tile", SWAP).astype(F32)
            x = [total[c * m : (c + 1) * m].astype(BF16) for c in range(PARTS)]
            solved += x
            if step == 0:
                x, v_rows = lax.optimization_barrier((x, v_factor[0]))
                v_pairs = v_rows.reshape(steps, reach, 2, n, width)
                upper = sides[None, :, :, None] == 1
                v_keep = jnp.where(upper, v_pairs[:, :, 1], v_pairs[:, :, 0])
                v_give = jnp.where(upper, v_pairs[:, :, 0], v_pairs[:, :, 1])
                v_take = lax.ppermute(v_give, "tile", SWAP)
                v_pieces = jnp.concatenate([v_keep, v_take], 1)
            got = gather(x)
            part = coef_product(v_pieces[step], [k for k in range(rows) if k != reach], got)
            part, sent = coef_product(v_pieces[step], [reach], got, part)
            taken = lax.ppermute(sent, "tile", SWAP)
            if step == steps - 1:
                out = update_last(step, pivots, ranks, part, taken, residual, u_factor, n)
                continue
            *ends, coef = update_ends(step, pivots, ranks, part, taken, residual, u_factor, n, PARTS)
            first, final = ends[:PARTS], ends[PARTS:]
            residual, held = update_whole(step, coef, residual, u_factor, n)
        return jnp.concatenate(solved).reshape(steps, n, cols), out[None]

    return local


def gathered_steps(right_side, diag_inverse, u_factor, v_factor, ranks, pivots):
    residual = right_side[0].astype(F32)
    half = residual.shape[0]
    heights = lax.broadcasted_iota(jnp.int32, (u_factor.shape[3], 1), 0)
    me, tile = lax.axis_index("row"), lax.axis_index("tile")
    solved = []
    for step in range(pivots.shape[0]):
        current = residual.astype(BF16)
        held = lax.psum(jnp.where(me == pivots[step], current, jnp.zeros_like(current)), "row")
        other = lax.ppermute(held, "tile", SWAP)
        pivot = jnp.where(tile == 0, jnp.concatenate([held, other]), jnp.concatenate([other, held]))
        x = jnp.dot(diag_inverse[step], pivot, preferred_element_type=F32).astype(BF16)
        solved.append(x)
        x_all = lax.all_gather(x, ("row", "tile"), axis=0, tiled=True)
        x_mine = lax.dynamic_slice_in_dim(x_all, tile * half, half, 0)
        part = lax.dot_general(
            v_factor[0, step], x_mine, (((0,), (0,)), ((), ())), preferred_element_type=F32
        )
        coef = part + lax.ppermute(part, "tile", SWAP)
        finished = jnp.any(pivots[: step + 1] == me)
        kept = jnp.where(finished, 0, ranks[0, step])
        coef = jnp.where(heights < kept, coef, F32(0.0)).astype(BF16)
        residual = residual - jnp.dot(u_factor[0, step], coef, preferred_element_type=F32)
    return jnp.stack(solved), residual[None]


def solution(mesh):
    rows = mesh.shape["row"]

    def local(right_side, diag_inverse, *others):
        half, n = right_side.shape[1], diag_inverse.shape[1]
        short = rows % 2 == 0 and rows <= MOST_HOPS and n % LANES == 0 and half == rows * n
        run = ring_steps(rows, half, n) if short else gathered_steps
        return run(right_side, diag_inverse, *others)

    in_specs = (
        P(("grp", "row"), "tile", None),
        P(None, ("row", "tile"), None),
        P("row", None, "tile", None),
        P("row", None, "tile", None),
        P("row", None),
        P(),
    )
    out_specs = (P(None, ("grp", "row", "tile"), None), P(("grp", "row"), "tile", None))
    return jax.shard_map(local, mesh=mesh, in_specs=in_specs, out_specs=out_specs, check_vma=False)
```

```python
import jax
import jax.numpy as jnp
from jax import lax
from jax.experimental import pallas as pl
from jax.experimental.pallas import tpu as pltpu
from jax.sharding import PartitionSpec as P


MOST_HOPS = 8
LANES = 128
PARTS = 2
SWAP = [(0, 1), (1, 0)]
BF16 = jnp.bfloat16
F32 = jnp.float32
VMEM_GRANT = 20 * 1024 * 1024


def ring_order(rows):
    return list(range(0, rows, 2)) + list(range(rows - 1, 0, -2))


def ring_place(index, rows):
    return jnp.where(lax.rem(index, 2) == 0, lax.div(index, 2), rows - lax.div(index + 1, 2))


def ring_row(place, rows):
    return jnp.where(place < rows // 2, 2 * place, 2 * (rows - place) - 1)


def ring_distance(holder, rows):
    return lax.rem(ring_place(lax.axis_index("row"), rows) - ring_place(holder, rows) + rows, rows)


def half_held(distance):
    return lax.rem(lax.axis_index("tile") + distance, 2)


def whole_specs(count):
    return [pl.BlockSpec(memory_space=pltpu.VMEM)] * count


def in_smem(count):
    return [pl.BlockSpec(memory_space=pltpu.SMEM)] * count


def cost(flops, moved):
    return pl.CostEstimate(flops=flops, bytes_accessed=moved, transcendentals=0)


SMALL = pltpu.CompilerParams(vmem_limit_bytes=VMEM_GRANT // 4)
PARAMS = pltpu.CompilerParams(vmem_limit_bytes=VMEM_GRANT)


def holder_masks(pivots, shape, rows):
    steps = pivots.shape[0]
    reach = rows // 2
    sides_shape = (-(-reach // 8) * 8, LANES)

    def kernel(pivots_ref, *out_refs):
        me, tile = lax.axis_index("row"), lax.axis_index("tile")
        for p in range(steps):
            value = jnp.where(pivots_ref[p] == me, 1.0, 0.0)
            out_refs[p][...] = jnp.full(shape, value, F32).astype(BF16)
        heights = lax.broadcasted_iota(jnp.int32, sides_shape, 0)
        sides = jnp.zeros(sides_shape, jnp.int32)
        for i in range(reach):
            hops = ring_distance(tile * reach + i, rows)
            sides = jnp.where(heights == i, lax.rem(tile + hops, 2), sides)
        out_refs[steps][...] = sides

    out = pl.pallas_call(
        kernel,
        out_shape=(jax.ShapeDtypeStruct(shape, BF16),) * steps + (jax.ShapeDtypeStruct(sides_shape, jnp.int32),),
        in_specs=in_smem(1),
        out_specs=tuple(whole_specs(steps + 1)),
        compiler_params=SMALL,
        name="holder_masks",
    )(pivots)
    return out[:steps], out[steps][:reach, :1]


def pick(mask, held, start, received):
    n = received.shape[0]

    def kernel(mask_ref, held_ref, got_ref, out_ref):
        out_ref[...] = jnp.where(mask_ref[...] > 0, held_ref[start : start + n, :], got_ref[...])

    return pl.pallas_call(
        kernel,
        out_shape=jax.ShapeDtypeStruct(received.shape, received.dtype),
        in_specs=whole_specs(3),
        out_specs=whole_specs(1)[0],
        compiler_params=SMALL,
        name="pick",
    )(mask, held, received)


def diag_early(step, pivots, diag_other, held, downs, ups):
    hops, parts = len(downs), len(downs[0])
    rows = hops + 2
    m, cols = downs[0][0].shape
    n = m * parts
    half = rows * n

    def kernel(pivots_ref, diag_ref, held_ref, *refs):
        got_refs, (take_ref, whole_ref, part_ref, sem) = refs[: 2 * hops * parts], refs[2 * hops * parts :]
        down_refs, up_refs = got_refs[: hops * parts], got_refs[hops * parts :]
        distance = ring_distance(pivots_ref[step], rows)
        base = pl.multiple_of(half_held(distance) * half, half)
        fetch = pltpu.make_async_copy(diag_ref.at[step, :, pl.ds(base, half)], take_ref, sem)
        fetch.start()

        @pl.when(distance == 0)
        def _():
            whole_ref[...] = held_ref[...]

        @pl.when(distance > 0)
        def _():
            missing = pl.multiple_of((rows - 1 - distance) * n, n)
            whole_ref[pl.ds(missing, 2 * n), :] = jnp.zeros((2 * n, cols), BF16)

        for hop in range(1, hops + 1):
            for near, at, side in (
                (distance <= hop, hop - distance, down_refs),
                (distance >= rows - hop, 2 * rows - 1 - hop - distance, up_refs),
            ):

                @pl.when(jnp.logical_and(distance > 0, near))
                def _(at=at, side=side, hop=hop):
                    for c in range(parts):
                        rows_at = pl.multiple_of(at * n + c * m, m)
                        whole_ref[pl.ds(rows_at, m), :] = side[(hop - 1) * parts + c][...]

        fetch.wait()
        part_ref[...] = jnp.dot(take_ref[...], whole_ref[...], preferred_element_type=F32)

    flat = [part for side in (downs, ups) for hop in side for part in hop]
    return pl.pallas_call(
        kernel,
        out_shape=(
            jax.ShapeDtypeStruct((n, half), BF16),
            jax.ShapeDtypeStruct((half, cols), BF16),
            jax.ShapeDtypeStruct((n, cols), F32),
        ),
        in_specs=in_smem(1) + [pl.BlockSpec(memory_space=pl.ANY)] + whole_specs(1 + len(flat)),
        out_specs=tuple(whole_specs(3)),
        scratch_shapes=[pltpu.SemaphoreType.DMA],
        compiler_params=PARAMS,
        cost_estimate=cost(2 * n * half * cols, 8 * n * half),
        name="diag_early",
    )(pivots, diag_other, held, *flat)


def diag_late(step, diag, column, pivots, so_far, part, down, up, kind, name):
    parts = len(down)
    m, cols = down[0].shape
    n = m * parts
    half = so_far.shape[0]
    rows = half // n

    def kernel(pivots_ref, diag_ref, so_far_ref, *refs):
        piece_refs, refs = refs[: 2 * parts], refs[2 * parts :]
        out_ref, total_ref, pair_ref = refs[-3:]
        distance = ring_distance(pivots_ref[step], rows)
        if column:
            base = pl.multiple_of(half_held(distance) * half, half)
            total_ref[...] = jnp.dot(
                diag_ref[step, :, pl.ds(base, half)], so_far_ref[...], preferred_element_type=F32
            )
        else:
            total_ref[...] = refs[0][...]

        @pl.when(distance > 0)
        def _():
            for c in range(2 * parts):
                pair_ref[c * m : (c + 1) * m, :] = piece_refs[c][...]
            at = pl.multiple_of((rows - 1 - distance) * n, n)
            if column:
                factor = diag_ref[step, :, pl.ds(pl.multiple_of(base + at, n), 2 * n)]
            else:
                factor = diag_ref[:, pl.ds(at, 2 * n)]
            total_ref[...] += jnp.dot(factor, pair_ref[...], preferred_element_type=F32)

        out_ref[...] = total_ref[...].astype(kind)

    given = [] if column else [part]
    return pl.pallas_call(
        kernel,
        out_shape=jax.ShapeDtypeStruct((n, cols), kind),
        in_specs=in_smem(1) + whole_specs(2 + 2 * parts + len(given)),
        out_specs=whole_specs(1)[0],
        scratch_shapes=[pltpu.VMEM((n, cols), F32), pltpu.VMEM((2 * n, cols), BF16)],
        compiler_params=PARAMS,
        cost_estimate=cost(2 * n * (half if column else 2 * n) * cols, 8 * n * n),
        name=name,
    )(pivots, diag, so_far, *down, *up, *given)


def coef_product(v_pieces, places, pieces, before=None):
    rows, n, width = v_pieces.shape
    parts = len(pieces[places[0]])
    m, cols = pieces[places[0]][0].shape
    reach = rows // 2
    flat = [part for k in places for part in pieces[k]]
    final = before is not None

    def kernel(v_ref, *refs):
        piece_refs, refs = refs[: len(flat)], refs[len(flat) :]
        out_ref = refs[1] if final else refs[0]
        place, tile = ring_place(lax.axis_index("row"), rows), lax.axis_index("tile")
        for i, k in enumerate(places):
            row = ring_row(lax.rem(place - k + rows, rows), rows)
            at = lax.rem(row + tile * reach, rows)
            for c in range(parts):
                part = lax.dot_general(
                    v_ref[at, c * m : (c + 1) * m, :],
                    piece_refs[i * parts + c][...],
                    (((0,), (0,)), ((), ())),
                    preferred_element_type=F32,
                )
                if i == 0 and c == 0:
                    out_ref[...] = refs[0][...] + part if final else part
                else:
                    out_ref[...] += part
        if final:
            refs[2][...] = out_ref[...].astype(BF16)

    full = jax.ShapeDtypeStruct((width, cols), F32)
    return pl.pallas_call(
        kernel,
        out_shape=(full, jax.ShapeDtypeStruct((width, cols), BF16)) if final else full,
        in_specs=whole_specs(1 + len(flat) + int(final)),
        out_specs=tuple(whole_specs(2)) if final else whole_specs(1)[0],
        compiler_params=PARAMS,
        cost_estimate=cost(2 * len(places) * n * width * cols, 4 * len(places) * n * width),
        name="coef_product",
    )(v_pieces, *flat, *([before] if final else []))


def masked_coef(step, pivots_ref, ranks_ref, part_ref, taken_ref):
    kept = ranks_ref[0, step]
    for q in range(step + 1):
        kept = jnp.where(pivots_ref[q] == lax.axis_index("row"), 0, kept)
    heights = lax.broadcasted_iota(jnp.int32, part_ref.shape, 0)
    return jnp.where(heights < kept, part_ref[...] + taken_ref[...].astype(F32), 0.0).astype(BF16)


def update_ends(step, pivots, ranks, part, taken, residual, factor, n, parts):
    half, cols = residual.shape
    m = n // parts

    def kernel(pivots_ref, ranks_ref, part_ref, taken_ref, residual_ref, u_ref, *refs):
        end_refs, coef_ref = refs[: 2 * parts], refs[2 * parts]
        coef = masked_coef(step, pivots_ref, ranks_ref, part_ref, taken_ref)
        coef_ref[...] = coef
        for i, start in enumerate((0, half - n)):
            span = slice(start, start + n)
            change = jnp.dot(u_ref[0, step, span, :], coef, preferred_element_type=F32)
            rounded = (residual_ref[span, :].astype(F32) - change).astype(BF16)
            for c in range(parts):
                end_refs[i * parts + c][...] = rounded[c * m : (c + 1) * m, :]

    ends = (jax.ShapeDtypeStruct((m, cols), BF16),) * (2 * parts)
    return pl.pallas_call(
        kernel,
        out_shape=ends + (jax.ShapeDtypeStruct(part.shape, BF16),),
        in_specs=in_smem(2) + whole_specs(4),
        out_specs=tuple(whole_specs(2 * parts + 1)),
        compiler_params=PARAMS,
        cost_estimate=cost(4 * n * part.shape[0] * cols, 8 * n * cols),
        name="update_ends",
    )(pivots, ranks, part, taken, residual, factor)


def update_whole(step, coef, residual, factor, n):
    half, cols = residual.shape

    def kernel(coef_ref, residual_ref, u_ref, out_ref, rounded_ref):
        for start in range(0, half, n):
            span = slice(start, start + n)
            change = jnp.dot(u_ref[0, step, span, :], coef_ref[...], preferred_element_type=F32)
            value = residual_ref[span, :].astype(F32) - change
            out_ref[span, :] = value
            rounded_ref[span, :] = value.astype(BF16)

    return pl.pallas_call(
        kernel,
        out_shape=(jax.ShapeDtypeStruct((half, cols), F32), jax.ShapeDtypeStruct((half, cols), BF16)),
        in_specs=whole_specs(3),
        out_specs=tuple(whole_specs(2)),
        compiler_params=PARAMS,
        cost_estimate=cost(2 * half * coef.shape[0] * cols, 8 * half * cols),
        name="update_whole",
    )(coef, residual, factor)


def update_last(step, pivots, ranks, part, taken, residual, factor, n):
    half, cols = residual.shape
    rows = half // n

    def kernel(pivots_ref, ranks_ref, part_ref, taken_ref, residual_ref, u_ref, out_ref, whole_ref, sems):
        coef = masked_coef(step, pivots_ref, ranks_ref, part_ref, taken_ref)
        copies = []
        for i in range(rows):
            span = slice(i * n, (i + 1) * n)
            change = jnp.dot(u_ref[0, step, span, :], coef, preferred_element_type=F32)
            whole_ref[span, :] = residual_ref[span, :].astype(F32) - change
            copies.append(pltpu.make_async_copy(whole_ref.at[span, :], out_ref.at[span, :], sems.at[i]))
            copies[-1].start()
        for copy in copies:
            copy.wait()

    return pl.pallas_call(
        kernel,
        out_shape=jax.ShapeDtypeStruct((half, cols), F32),
        in_specs=in_smem(2) + whole_specs(4),
        out_specs=pl.BlockSpec(memory_space=pl.ANY),
        scratch_shapes=[pltpu.VMEM((half, cols), F32), pltpu.SemaphoreType.DMA((rows,))],
        compiler_params=PARAMS,
        cost_estimate=cost(2 * half * part.shape[0] * cols, 8 * half * cols),
        name="update_last",
    )(pivots, ranks, part, taken, residual, factor)


def ring_steps(rows, half, n):
    ring = ring_order(rows)
    links = [(ring[i], ring[(i + 1) % rows]) for i in range(rows)]
    forward = [(2 * a + tile, 2 * b + 1 - tile) for a, b in links for tile in range(2)]
    backward = [(b, a) for a, b in forward]
    reach = rows // 2
    m = n // PARTS

    def hop_to(value, way):
        return lax.ppermute(value, ("row", "tile"), way)

    def gather(piece):
        got = [None] * rows
        got[0] = down = up = piece
        for hop in range(1, reach):
            got[hop] = down = [hop_to(part, forward) for part in down]
            got[rows - hop] = up = [hop_to(part, backward) for part in up]
        sides = [(down, forward) if c % 2 == 0 else (up, backward) for c in range(PARTS)]
        got[reach] = [hop_to(side[c], way) for c, (side, way) in enumerate(sides)]
        return got

    def spread(held, first, last, masks, step):
        down = [hop_to(part, forward) for part in first]
        up = [hop_to(part, backward) for part in last]
        if step == 0:
            down[0], masks = lax.optimization_barrier((down[0], masks))
        downs, ups = [down], [up]
        for hop in range(1, rows - 1):
            down, up = list(down), list(up)
            for c in range(PARTS):
                own = pick(masks[step], held, hop * n + c * m, down[c])
                down[c] = hop_to(own, forward)
                own = pick(masks[step], held, (rows - 1 - hop) * n + c * m, up[c])
                up[c] = hop_to(own, backward)
            downs.append(down)
            ups.append(up)
        return downs, ups, masks

    def local(right_side, diag_inverse, u_factor, v_factor, ranks, pivots):
        steps = pivots.shape[0]
        held = residual = right_side[0]
        cols, width = held.shape[1], u_factor.shape[3]
        masks, sides = holder_masks(pivots, (m, cols), rows)
        diag_other = lax.ppermute(diag_inverse, "tile", SWAP)
        first = [held[c * m : (c + 1) * m] for c in range(PARTS)]
        final = [held[half - n + c * m : half - n + (c + 1) * m] for c in range(PARTS)]
        solved = []
        for step in range(steps):
            downs, ups, masks = spread(held, first, final, masks, step)
            take, so_far, early = diag_early(step, pivots, diag_other, held, downs[:-1], ups[:-1])
            ends = (downs[-1], ups[-1])
            other = diag_late(step, take, False, pivots, so_far, early, *ends, BF16, "diag_give")
            mine = diag_late(step, diag_inverse, True, pivots, so_far, None, *ends, F32, "diag_keep")
            total = mine + lax.ppermute(other, "tile", SWAP).astype(F32)
            x = [total[c * m : (c + 1) * m].astype(BF16) for c in range(PARTS)]
            solved += x
            if step == 0:
                x, v_rows = lax.optimization_barrier((x, v_factor[0]))
                v_pairs = v_rows.reshape(steps, reach, 2, n, width)
                upper = sides[None, :, :, None] == 1
                v_keep = jnp.where(upper, v_pairs[:, :, 1], v_pairs[:, :, 0])
                v_give = jnp.where(upper, v_pairs[:, :, 0], v_pairs[:, :, 1])
                v_take = lax.ppermute(v_give, "tile", SWAP)
                v_pieces = jnp.concatenate([v_keep, v_take], 1)
            got = gather(x)
            part = coef_product(v_pieces[step], [k for k in range(rows) if k != reach], got)
            part, sent = coef_product(v_pieces[step], [reach], got, part)
            taken = lax.ppermute(sent, "tile", SWAP)
            if step == steps - 1:
                out = update_last(step, pivots, ranks, part, taken, residual, u_factor, n)
                continue
            *ends, coef = update_ends(step, pivots, ranks, part, taken, residual, u_factor, n, PARTS)
            first, final = ends[:PARTS], ends[PARTS:]
            residual, held = update_whole(step, coef, residual, u_factor, n)
        return jnp.concatenate(solved).reshape(steps, n, cols), out[None]

    return local


def gathered_steps(right_side, diag_inverse, u_factor, v_factor, ranks, pivots):
    residual = right_side[0].astype(F32)
    half = residual.shape[0]
    heights = lax.broadcasted_iota(jnp.int32, (u_factor.shape[3], 1), 0)
    me, tile = lax.axis_index("row"), lax.axis_index("tile")
    solved = []
    for step in range(pivots.shape[0]):
        current = residual.astype(BF16)
        held = lax.psum(jnp.where(me == pivots[step], current, jnp.zeros_like(current)), "row")
        other = lax.ppermute(held, "tile", SWAP)
        pivot = jnp.where(tile == 0, jnp.concatenate([held, other]), jnp.concatenate([other, held]))
        x = jnp.dot(diag_inverse[step], pivot, preferred_element_type=F32).astype(BF16)
        solved.append(x)
        x_all = lax.all_gather(x, ("row", "tile"), axis=0, tiled=True)
        x_mine = lax.dynamic_slice_in_dim(x_all, tile * half, half, 0)
        part = lax.dot_general(
            v_factor[0, step], x_mine, (((0,), (0,)), ((), ())), preferred_element_type=F32
        )
        coef = part + lax.ppermute(part, "tile", SWAP)
        finished = jnp.any(pivots[: step + 1] == me)
        kept = jnp.where(finished, 0, ranks[0, step])
        coef = jnp.where(heights < kept, coef, F32(0.0)).astype(BF16)
        residual = residual - jnp.dot(u_factor[0, step], coef, preferred_element_type=F32)
    return jnp.stack(solved), residual[None]


def solution(mesh):
    rows = mesh.shape["row"]

    def local(right_side, diag_inverse, *others):
        half, n = right_side.shape[1], diag_inverse.shape[1]
        short = rows % 2 == 0 and rows <= MOST_HOPS and n % LANES == 0 and half == rows * n
        run = ring_steps(rows, half, n) if short else gathered_steps
        return run(right_side, diag_inverse, *others)

    in_specs = (
        P(("grp", "row"), "tile", None),
        P(None, ("row", "tile"), None),
        P("row", None, "tile", None),
        P("row", None, "tile", None),
        P("row", None),
        P(),
    )
    out_specs = (P(None, ("grp", "row", "tile"), None), P(("grp", "row"), "tile", None))
    return jax.shard_map(local, mesh=mesh, in_specs=in_specs, out_specs=out_specs, check_vma=False)
```

```python
import jax
import jax.numpy as jnp
from jax import lax
from jax.experimental import pallas as pl
from jax.experimental.pallas import tpu as pltpu
from jax.sharding import PartitionSpec as P


MOST_HOPS = 8
LANES = 128
PARTS = 2
SWAP = [(0, 1), (1, 0)]
BF16 = jnp.bfloat16
F32 = jnp.float32
VMEM_GRANT = 20 * 1024 * 1024


def ring_order(rows):
    return list(range(0, rows, 2)) + list(range(rows - 1, 0, -2))


def ring_place(index, rows):
    return jnp.where(lax.rem(index, 2) == 0, lax.div(index, 2), rows - lax.div(index + 1, 2))


def ring_row(place, rows):
    return jnp.where(place < rows // 2, 2 * place, 2 * (rows - place) - 1)


def ring_distance(holder, rows):
    return lax.rem(ring_place(lax.axis_index("row"), rows) - ring_place(holder, rows) + rows, rows)


def half_held(distance):
    return lax.rem(lax.axis_index("tile") + distance, 2)


def whole_specs(count):
    return [pl.BlockSpec(memory_space=pltpu.VMEM)] * count


def in_smem(count):
    return [pl.BlockSpec(memory_space=pltpu.SMEM)] * count


def cost(flops, moved):
    return pl.CostEstimate(flops=flops, bytes_accessed=moved, transcendentals=0)


SMALL = pltpu.CompilerParams(vmem_limit_bytes=VMEM_GRANT // 4)
PARAMS = pltpu.CompilerParams(vmem_limit_bytes=VMEM_GRANT)


def device_facts(pivots, ranks, shape, rows):
    steps = pivots.shape[0]
    reach = rows // 2
    sides_shape = (-(-reach // 8) * 8, LANES)
    small = (8, LANES)

    def kernel(pivots_ref, ranks_ref, *out_refs):
        me, tile = lax.axis_index("row"), lax.axis_index("tile")
        finished = False
        for p in range(steps):
            holds = pivots_ref[p] == me
            out_refs[p][...] = jnp.full(shape, jnp.where(holds, 1.0, 0.0), F32).astype(BF16)
            finished = jnp.logical_or(finished, holds)
            out_refs[steps + p][...] = jnp.full(small, ring_distance(pivots_ref[p], rows), jnp.int32)
            out_refs[2 * steps + p][...] = jnp.full(small, jnp.where(finished, 0, ranks_ref[0, p]), jnp.int32)
        heights = lax.broadcasted_iota(jnp.int32, sides_shape, 0)
        sides = jnp.zeros(sides_shape, jnp.int32)
        for i in range(reach):
            hops = ring_distance(tile * reach + i, rows)
            sides = jnp.where(heights == i, lax.rem(tile + hops, 2), sides)
        out_refs[3 * steps][...] = sides

    out = pl.pallas_call(
        kernel,
        out_shape=(jax.ShapeDtypeStruct(shape, BF16),) * steps
        + (jax.ShapeDtypeStruct(small, jnp.int32),) * (2 * steps)
        + (jax.ShapeDtypeStruct(sides_shape, jnp.int32),),
        in_specs=in_smem(2),
        out_specs=tuple(whole_specs(3 * steps + 1)),
        compiler_params=SMALL,
        name="device_facts",
    )(pivots, ranks)
    return out[:steps], out[steps : 2 * steps], out[2 * steps : 3 * steps], out[3 * steps][:reach, :1]


def pick(mask, held, start, received):
    n = received.shape[0]

    def kernel(mask_ref, held_ref, got_ref, out_ref):
        out_ref[...] = jnp.where(mask_ref[...] > 0, held_ref[start : start + n, :], got_ref[...])

    return pl.pallas_call(
        kernel,
        out_shape=jax.ShapeDtypeStruct(received.shape, received.dtype),
        in_specs=whole_specs(3),
        out_specs=whole_specs(1)[0],
        compiler_params=SMALL,
        name="pick",
    )(mask, held, received)


def diag_early(step, pivots, diag_other, held, downs, ups):
    hops, parts = len(downs), len(downs[0])
    rows = hops + 2
    m, cols = downs[0][0].shape
    n = m * parts
    half = rows * n

    def kernel(pivots_ref, diag_ref, held_ref, *refs):
        got_refs, (take_ref, whole_ref, part_ref, sem) = refs[: 2 * hops * parts], refs[2 * hops * parts :]
        down_refs, up_refs = got_refs[: hops * parts], got_refs[hops * parts :]
        distance = ring_distance(pivots_ref[step], rows)
        base = pl.multiple_of(half_held(distance) * half, half)
        fetch = pltpu.make_async_copy(diag_ref.at[step, :, pl.ds(base, half)], take_ref, sem)
        fetch.start()

        @pl.when(distance == 0)
        def _():
            whole_ref[...] = held_ref[...]

        @pl.when(distance > 0)
        def _():
            missing = pl.multiple_of((rows - 1 - distance) * n, n)
            whole_ref[pl.ds(missing, 2 * n), :] = jnp.zeros((2 * n, cols), BF16)

        for hop in range(1, hops + 1):
            for near, at, side in (
                (distance <= hop, hop - distance, down_refs),
                (distance >= rows - hop, 2 * rows - 1 - hop - distance, up_refs),
            ):

                @pl.when(jnp.logical_and(distance > 0, near))
                def _(at=at, side=side, hop=hop):
                    for c in range(parts):
                        rows_at = pl.multiple_of(at * n + c * m, m)
                        whole_ref[pl.ds(rows_at, m), :] = side[(hop - 1) * parts + c][...]

        fetch.wait()
        part_ref[...] = jnp.dot(take_ref[...], whole_ref[...], preferred_element_type=F32)

    flat = [part for side in (downs, ups) for hop in side for part in hop]
    return pl.pallas_call(
        kernel,
        out_shape=(
            jax.ShapeDtypeStruct((n, half), BF16),
            jax.ShapeDtypeStruct((half, cols), BF16),
            jax.ShapeDtypeStruct((n, cols), F32),
        ),
        in_specs=in_smem(1) + [pl.BlockSpec(memory_space=pl.ANY)] + whole_specs(1 + len(flat)),
        out_specs=tuple(whole_specs(3)),
        scratch_shapes=[pltpu.SemaphoreType.DMA],
        compiler_params=PARAMS,
        cost_estimate=cost(2 * n * half * cols, 8 * n * half),
        name="diag_early",
    )(pivots, diag_other, held, *flat)


def diag_late(step, diag, column, distances, so_far, part, down, up, kind, name):
    parts = len(down)
    m, cols = down[0].shape
    n = m * parts
    half = so_far.shape[0]
    rows = half // n

    def kernel(distance_ref, diag_ref, so_far_ref, *refs):
        piece_refs, refs = refs[: 2 * parts], refs[2 * parts :]
        out_ref, total_ref, pair_ref = refs[-3:]
        distance = jnp.max(distance_ref[...])
        if column:
            base = pl.multiple_of(half_held(distance) * half, half)
            total_ref[...] = jnp.dot(
                diag_ref[step, :, pl.ds(base, half)], so_far_ref[...], preferred_element_type=F32
            )
        else:
            total_ref[...] = refs[0][...]

        @pl.when(distance > 0)
        def _():
            for c in range(2 * parts):
                pair_ref[c * m : (c + 1) * m, :] = piece_refs[c][...]
            at = pl.multiple_of((rows - 1 - distance) * n, n)
            if column:
                factor = diag_ref[step, :, pl.ds(pl.multiple_of(base + at, n), 2 * n)]
            else:
                factor = diag_ref[:, pl.ds(at, 2 * n)]
            total_ref[...] += jnp.dot(factor, pair_ref[...], preferred_element_type=F32)

        out_ref[...] = total_ref[...].astype(kind)

    given = [] if column else [part]
    return pl.pallas_call(
        kernel,
        out_shape=jax.ShapeDtypeStruct((n, cols), kind),
        in_specs=whole_specs(3 + 2 * parts + len(given)),
        out_specs=whole_specs(1)[0],
        scratch_shapes=[pltpu.VMEM((n, cols), F32), pltpu.VMEM((2 * n, cols), BF16)],
        compiler_params=PARAMS,
        cost_estimate=cost(2 * n * (half if column else 2 * n) * cols, 8 * n * n),
        name=name,
    )(distances[step], diag, so_far, *down, *up, *given)


def coef_product(v_pieces, places, pieces, before=None):
    rows, n, width = v_pieces.shape
    parts = len(pieces[places[0]])
    m, cols = pieces[places[0]][0].shape
    reach = rows // 2
    flat = [part for k in places for part in pieces[k]]
    final = before is not None

    def kernel(v_ref, *refs):
        piece_refs, refs = refs[: len(flat)], refs[len(flat) :]
        out_ref = refs[1] if final else refs[0]
        place, tile = ring_place(lax.axis_index("row"), rows), lax.axis_index("tile")
        for i, k in enumerate(places):
            row = ring_row(lax.rem(place - k + rows, rows), rows)
            at = lax.rem(row + tile * reach, rows)
            for c in range(parts):
                part = lax.dot_general(
                    v_ref[at, c * m : (c + 1) * m, :],
                    piece_refs[i * parts + c][...],
                    (((0,), (0,)), ((), ())),
                    preferred_element_type=F32,
                )
                if i == 0 and c == 0:
                    out_ref[...] = refs[0][...] + part if final else part
                else:
                    out_ref[...] += part
        if final:
            refs[2][...] = out_ref[...].astype(BF16)

    full = jax.ShapeDtypeStruct((width, cols), F32)
    return pl.pallas_call(
        kernel,
        out_shape=(full, jax.ShapeDtypeStruct((width, cols), BF16)) if final else full,
        in_specs=whole_specs(1 + len(flat) + int(final)),
        out_specs=tuple(whole_specs(2)) if final else whole_specs(1)[0],
        compiler_params=PARAMS,
        cost_estimate=cost(2 * len(places) * n * width * cols, 4 * len(places) * n * width),
        name="coef_product",
    )(v_pieces, *flat, *([before] if final else []))


def masked_coef(kept_ref, part_ref, taken_ref):
    kept = jnp.max(kept_ref[...])
    heights = lax.broadcasted_iota(jnp.int32, part_ref.shape, 0)
    return jnp.where(heights < kept, part_ref[...] + taken_ref[...].astype(F32), 0.0).astype(BF16)


def update_ends(step, kept, part, taken, residual, factor, n, parts):
    half, cols = residual.shape
    m = n // parts

    def kernel(kept_ref, part_ref, taken_ref, residual_ref, u_ref, *refs):
        end_refs, coef_ref = refs[: 2 * parts], refs[2 * parts]
        coef = masked_coef(kept_ref, part_ref, taken_ref)
        coef_ref[...] = coef
        for i, start in enumerate((0, half - n)):
            span = slice(start, start + n)
            change = jnp.dot(u_ref[0, step, span, :], coef, preferred_element_type=F32)
            rounded = (residual_ref[span, :].astype(F32) - change).astype(BF16)
            for c in range(parts):
                end_refs[i * parts + c][...] = rounded[c * m : (c + 1) * m, :]

    ends = (jax.ShapeDtypeStruct((m, cols), BF16),) * (2 * parts)
    return pl.pallas_call(
        kernel,
        out_shape=ends + (jax.ShapeDtypeStruct(part.shape, BF16),),
        in_specs=whole_specs(5),
        out_specs=tuple(whole_specs(2 * parts + 1)),
        compiler_params=PARAMS,
        cost_estimate=cost(4 * n * part.shape[0] * cols, 8 * n * cols),
        name="update_ends",
    )(kept[step], part, taken, residual, factor)


def update_whole(step, coef, residual, factor, n):
    half, cols = residual.shape

    def kernel(coef_ref, residual_ref, u_ref, out_ref, rounded_ref):
        for start in range(0, half, n):
            span = slice(start, start + n)
            change = jnp.dot(u_ref[0, step, span, :], coef_ref[...], preferred_element_type=F32)
            value = residual_ref[span, :].astype(F32) - change
            out_ref[span, :] = value
            rounded_ref[span, :] = value.astype(BF16)

    return pl.pallas_call(
        kernel,
        out_shape=(jax.ShapeDtypeStruct((half, cols), F32), jax.ShapeDtypeStruct((half, cols), BF16)),
        in_specs=whole_specs(3),
        out_specs=tuple(whole_specs(2)),
        compiler_params=PARAMS,
        cost_estimate=cost(2 * half * coef.shape[0] * cols, 8 * half * cols),
        name="update_whole",
    )(coef, residual, factor)


def update_last(step, kept, part, taken, residual, factor, n):
    half, cols = residual.shape
    rows = half // n

    def kernel(kept_ref, part_ref, taken_ref, residual_ref, u_ref, out_ref, whole_ref, sems):
        coef = masked_coef(kept_ref, part_ref, taken_ref)
        copies = []
        for i in range(rows):
            span = slice(i * n, (i + 1) * n)
            change = jnp.dot(u_ref[0, step, span, :], coef, preferred_element_type=F32)
            whole_ref[span, :] = residual_ref[span, :].astype(F32) - change
            copies.append(pltpu.make_async_copy(whole_ref.at[span, :], out_ref.at[span, :], sems.at[i]))
            copies[-1].start()
        for copy in copies:
            copy.wait()

    return pl.pallas_call(
        kernel,
        out_shape=jax.ShapeDtypeStruct((half, cols), F32),
        in_specs=whole_specs(5),
        out_specs=pl.BlockSpec(memory_space=pl.ANY),
        scratch_shapes=[pltpu.VMEM((half, cols), F32), pltpu.SemaphoreType.DMA((rows,))],
        compiler_params=PARAMS,
        cost_estimate=cost(2 * half * part.shape[0] * cols, 8 * half * cols),
        name="update_last",
    )(kept[step], part, taken, residual, factor)


def ring_steps(rows, half, n):
    ring = ring_order(rows)
    links = [(ring[i], ring[(i + 1) % rows]) for i in range(rows)]
    forward = [(2 * a + tile, 2 * b + 1 - tile) for a, b in links for tile in range(2)]
    backward = [(b, a) for a, b in forward]
    reach = rows // 2
    m = n // PARTS

    def hop_to(value, way):
        return lax.ppermute(value, ("row", "tile"), way)

    def gather(piece):
        got = [None] * rows
        got[0] = down = up = piece
        for hop in range(1, reach):
            got[hop] = down = [hop_to(part, forward) for part in down]
            got[rows - hop] = up = [hop_to(part, backward) for part in up]
        sides = [(down, forward) if c % 2 == 0 else (up, backward) for c in range(PARTS)]
        got[reach] = [hop_to(side[c], way) for c, (side, way) in enumerate(sides)]
        return got

    def spread(held, first, last, masks, step):
        down = [hop_to(part, forward) for part in first]
        up = [hop_to(part, backward) for part in last]
        if step == 0:
            down[0], masks = lax.optimization_barrier((down[0], masks))
        downs, ups = [down], [up]
        for hop in range(1, rows - 1):
            down, up = list(down), list(up)
            for c in range(PARTS):
                own = pick(masks[step], held, hop * n + c * m, down[c])
                down[c] = hop_to(own, forward)
                own = pick(masks[step], held, (rows - 1 - hop) * n + c * m, up[c])
                up[c] = hop_to(own, backward)
            downs.append(down)
            ups.append(up)
        return downs, ups, masks

    def local(right_side, diag_inverse, u_factor, v_factor, ranks, pivots):
        steps = pivots.shape[0]
        held = residual = right_side[0]
        cols, width = held.shape[1], u_factor.shape[3]
        masks, distances, kept, sides = device_facts(pivots, ranks, (m, cols), rows)
        diag_other = lax.ppermute(diag_inverse, "tile", SWAP)
        first = [held[c * m : (c + 1) * m] for c in range(PARTS)]
        final = [held[half - n + c * m : half - n + (c + 1) * m] for c in range(PARTS)]
        solved = []
        for step in range(steps):
            downs, ups, masks = spread(held, first, final, masks, step)
            take, so_far, early = diag_early(step, pivots, diag_other, held, downs[:-1], ups[:-1])
            ends = (downs[-1], ups[-1])
            other = diag_late(step, take, False, distances, so_far, early, *ends, BF16, "diag_give")
            mine = diag_late(step, diag_inverse, True, distances, so_far, None, *ends, F32, "diag_keep")
            total = mine + lax.ppermute(other, "tile", SWAP).astype(F32)
            x = [total[c * m : (c + 1) * m].astype(BF16) for c in range(PARTS)]
            solved += x
            if step == 0:
                x, v_rows = lax.optimization_barrier((x, v_factor[0]))
                v_pairs = v_rows.reshape(steps, reach, 2, n, width)
                upper = sides[None, :, :, None] == 1
                v_keep = jnp.where(upper, v_pairs[:, :, 1], v_pairs[:, :, 0])
                v_give = jnp.where(upper, v_pairs[:, :, 0], v_pairs[:, :, 1])
                v_take = lax.ppermute(v_give, "tile", SWAP)
                v_pieces = jnp.concatenate([v_keep, v_take], 1)
            got = gather(x)
            part = coef_product(v_pieces[step], [k for k in range(rows) if k != reach], got)
            part, sent = coef_product(v_pieces[step], [reach], got, part)
            taken = lax.ppermute(sent, "tile", SWAP)
            if step == steps - 1:
                out = update_last(step, kept, part, taken, residual, u_factor, n)
                continue
            *ends, coef = update_ends(step, kept, part, taken, residual, u_factor, n, PARTS)
            first, final = ends[:PARTS], ends[PARTS:]
            residual, held = update_whole(step, coef, residual, u_factor, n)
        return jnp.concatenate(solved).reshape(steps, n, cols), out[None]

    return local


def gathered_steps(right_side, diag_inverse, u_factor, v_factor, ranks, pivots):
    residual = right_side[0].astype(F32)
    half = residual.shape[0]
    heights = lax.broadcasted_iota(jnp.int32, (u_factor.shape[3], 1), 0)
    me, tile = lax.axis_index("row"), lax.axis_index("tile")
    solved = []
    for step in range(pivots.shape[0]):
        current = residual.astype(BF16)
        held = lax.psum(jnp.where(me == pivots[step], current, jnp.zeros_like(current)), "row")
        other = lax.ppermute(held, "tile", SWAP)
        pivot = jnp.where(tile == 0, jnp.concatenate([held, other]), jnp.concatenate([other, held]))
        x = jnp.dot(diag_inverse[step], pivot, preferred_element_type=F32).astype(BF16)
        solved.append(x)
        x_all = lax.all_gather(x, ("row", "tile"), axis=0, tiled=True)
        x_mine = lax.dynamic_slice_in_dim(x_all, tile * half, half, 0)
        part = lax.dot_general(
            v_factor[0, step], x_mine, (((0,), (0,)), ((), ())), preferred_element_type=F32
        )
        coef = part + lax.ppermute(part, "tile", SWAP)
        finished = jnp.any(pivots[: step + 1] == me)
        kept = jnp.where(finished, 0, ranks[0, step])
        coef = jnp.where(heights < kept, coef, F32(0.0)).astype(BF16)
        residual = residual - jnp.dot(u_factor[0, step], coef, preferred_element_type=F32)
    return jnp.stack(solved), residual[None]


def solution(mesh):
    rows = mesh.shape["row"]

    def local(right_side, diag_inverse, *others):
        half, n = right_side.shape[1], diag_inverse.shape[1]
        short = rows % 2 == 0 and rows <= MOST_HOPS and n % LANES == 0 and half == rows * n
        run = ring_steps(rows, half, n) if short else gathered_steps
        return run(right_side, diag_inverse, *others)

    in_specs = (
        P(("grp", "row"), "tile", None),
        P(None, ("row", "tile"), None),
        P("row", None, "tile", None),
        P("row", None, "tile", None),
        P("row", None),
        P(),
    )
    out_specs = (P(None, ("grp", "row", "tile"), None), P(("grp", "row"), "tile", None))
    return jax.shard_map(local, mesh=mesh, in_specs=in_specs, out_specs=out_specs, check_vma=False)
```

```python
import jax
import jax.numpy as jnp
from jax import lax
from jax.experimental import pallas as pl
from jax.experimental.pallas import tpu as pltpu
from jax.sharding import PartitionSpec as P


MOST_HOPS = 8
LANES = 128
PARTS = 2
SWAP = [(0, 1), (1, 0)]
BF16 = jnp.bfloat16
F32 = jnp.float32
VMEM_GRANT = 20 * 1024 * 1024


def ring_order(rows):
    return list(range(0, rows, 2)) + list(range(rows - 1, 0, -2))


def ring_place(index, rows):
    return jnp.where(lax.rem(index, 2) == 0, lax.div(index, 2), rows - lax.div(index + 1, 2))


def ring_row(place, rows):
    return jnp.where(place < rows // 2, 2 * place, 2 * (rows - place) - 1)


def ring_distance(holder, rows):
    return lax.rem(ring_place(lax.axis_index("row"), rows) - ring_place(holder, rows) + rows, rows)


def half_held(distance):
    return lax.rem(lax.axis_index("tile") + distance, 2)


def whole_specs(count):
    return [pl.BlockSpec(memory_space=pltpu.VMEM)] * count


def in_smem(count):
    return [pl.BlockSpec(memory_space=pltpu.SMEM)] * count


def cost(flops, moved):
    return pl.CostEstimate(flops=flops, bytes_accessed=moved, transcendentals=0)


SMALL = pltpu.CompilerParams(vmem_limit_bytes=VMEM_GRANT // 4)
PARAMS = pltpu.CompilerParams(vmem_limit_bytes=VMEM_GRANT)


def device_facts(pivots, ranks, shape, rows):
    steps = pivots.shape[0]
    reach = rows // 2
    sides_shape = (-(-reach // 8) * 8, LANES)
    small = (8, LANES)

    def kernel(pivots_ref, ranks_ref, *out_refs):
        me, tile = lax.axis_index("row"), lax.axis_index("tile")
        finished = False
        for p in range(steps):
            holds = pivots_ref[p] == me
            out_refs[p][...] = jnp.full(shape, jnp.where(holds, 1.0, 0.0), F32).astype(BF16)
            finished = jnp.logical_or(finished, holds)
            out_refs[steps + p][...] = jnp.full(small, ring_distance(pivots_ref[p], rows), jnp.int32)
            out_refs[2 * steps + p][...] = jnp.full(small, jnp.where(finished, 0, ranks_ref[0, p]), jnp.int32)
        heights = lax.broadcasted_iota(jnp.int32, sides_shape, 0)
        sides = jnp.zeros(sides_shape, jnp.int32)
        for i in range(reach):
            hops = ring_distance(tile * reach + i, rows)
            sides = jnp.where(heights == i, lax.rem(tile + hops, 2), sides)
        out_refs[3 * steps][...] = sides

    out = pl.pallas_call(
        kernel,
        out_shape=(jax.ShapeDtypeStruct(shape, BF16),) * steps
        + (jax.ShapeDtypeStruct(small, jnp.int32),) * (2 * steps)
        + (jax.ShapeDtypeStruct(sides_shape, jnp.int32),),
        in_specs=in_smem(2),
        out_specs=tuple(whole_specs(3 * steps + 1)),
        compiler_params=SMALL,
        name="device_facts",
    )(pivots, ranks)
    return out[:steps], out[steps : 2 * steps], out[2 * steps : 3 * steps], out[3 * steps][:reach, :1]


def pick(mask, held, start, received):
    n = received.shape[0]

    def kernel(mask_ref, held_ref, got_ref, out_ref):
        out_ref[...] = jnp.where(mask_ref[...] > 0, held_ref[start : start + n, :], got_ref[...])

    return pl.pallas_call(
        kernel,
        out_shape=jax.ShapeDtypeStruct(received.shape, received.dtype),
        in_specs=whole_specs(3),
        out_specs=whole_specs(1)[0],
        compiler_params=SMALL,
        name="pick",
    )(mask, held, received)


def diag_early(step, pivots, diag_other, held, downs, ups):
    hops, parts = len(downs), len(downs[0])
    rows = hops + 2
    m, cols = downs[0][0].shape
    n = m * parts
    half = rows * n

    def kernel(pivots_ref, diag_ref, held_ref, *refs):
        got_refs, (take_ref, whole_ref, part_ref, sem) = refs[: 2 * hops * parts], refs[2 * hops * parts :]
        down_refs, up_refs = got_refs[: hops * parts], got_refs[hops * parts :]
        distance = ring_distance(pivots_ref[step], rows)
        base = pl.multiple_of(half_held(distance) * half, half)
        fetch = pltpu.make_async_copy(diag_ref.at[step, :, pl.ds(base, half)], take_ref, sem)
        fetch.start()

        @pl.when(distance == 0)
        def _():
            whole_ref[...] = held_ref[...]

        @pl.when(distance > 0)
        def _():
            missing = pl.multiple_of((rows - 1 - distance) * n, n)
            whole_ref[pl.ds(missing, 2 * n), :] = jnp.zeros((2 * n, cols), BF16)

        for hop in range(1, hops + 1):
            for near, at, side in (
                (distance <= hop, hop - distance, down_refs),
                (distance >= rows - hop, 2 * rows - 1 - hop - distance, up_refs),
            ):

                @pl.when(jnp.logical_and(distance > 0, near))
                def _(at=at, side=side, hop=hop):
                    for c in range(parts):
                        rows_at = pl.multiple_of(at * n + c * m, m)
                        whole_ref[pl.ds(rows_at, m), :] = side[(hop - 1) * parts + c][...]

        fetch.wait()
        part_ref[...] = jnp.dot(take_ref[...], whole_ref[...], preferred_element_type=F32)

    flat = [part for side in (downs, ups) for hop in side for part in hop]
    return pl.pallas_call(
        kernel,
        out_shape=(
            jax.ShapeDtypeStruct((n, half), BF16),
            jax.ShapeDtypeStruct((half, cols), BF16),
            jax.ShapeDtypeStruct((n, cols), F32),
        ),
        in_specs=in_smem(1) + [pl.BlockSpec(memory_space=pl.ANY)] + whole_specs(1 + len(flat)),
        out_specs=tuple(whole_specs(3)),
        scratch_shapes=[pltpu.SemaphoreType.DMA],
        compiler_params=PARAMS,
        cost_estimate=cost(2 * n * half * cols, 8 * n * half),
        name="diag_early",
    )(pivots, diag_other, held, *flat)


def diag_late(step, diag, column, distances, so_far, part, down, up, kind, name):
    parts = len(down)
    m, cols = down[0].shape
    n = m * parts
    half = so_far.shape[0]
    rows = half // n

    def kernel(distance_ref, diag_ref, so_far_ref, *refs):
        piece_refs, refs = refs[: 2 * parts], refs[2 * parts :]
        out_ref, total_ref, pair_ref = refs[-3:]
        distance = jnp.max(distance_ref[...])
        if column:
            base = pl.multiple_of(half_held(distance) * half, half)
            total_ref[...] = jnp.dot(
                diag_ref[step, :, pl.ds(base, half)], so_far_ref[...], preferred_element_type=F32
            )
        else:
            total_ref[...] = refs[0][...]

        @pl.when(distance > 0)
        def _():
            for c in range(2 * parts):
                pair_ref[c * m : (c + 1) * m, :] = piece_refs[c][...]
            at = pl.multiple_of((rows - 1 - distance) * n, n)
            if column:
                factor = diag_ref[step, :, pl.ds(pl.multiple_of(base + at, n), 2 * n)]
            else:
                factor = diag_ref[:, pl.ds(at, 2 * n)]
            total_ref[...] += jnp.dot(factor, pair_ref[...], preferred_element_type=F32)

        out_ref[...] = total_ref[...].astype(kind)

    given = [] if column else [part]
    return pl.pallas_call(
        kernel,
        out_shape=jax.ShapeDtypeStruct((n, cols), kind),
        in_specs=whole_specs(3 + 2 * parts + len(given)),
        out_specs=whole_specs(1)[0],
        scratch_shapes=[pltpu.VMEM((n, cols), F32), pltpu.VMEM((2 * n, cols), BF16)],
        compiler_params=PARAMS,
        cost_estimate=cost(2 * n * (half if column else 2 * n) * cols, 8 * n * n),
        name=name,
    )(distances[step], diag, so_far, *down, *up, *given)


def coef_product(v_pieces, places, pieces, before=None):
    rows, n, width = v_pieces.shape
    parts = len(pieces[places[0]])
    m, cols = pieces[places[0]][0].shape
    reach = rows // 2
    flat = [part for k in places for part in pieces[k]]
    final = before is not None

    def kernel(v_ref, *refs):
        piece_refs, refs = refs[: len(flat)], refs[len(flat) :]
        out_ref = refs[1] if final else refs[0]
        place, tile = ring_place(lax.axis_index("row"), rows), lax.axis_index("tile")
        for i, k in enumerate(places):
            row = ring_row(lax.rem(place - k + rows, rows), rows)
            at = lax.rem(row + tile * reach, rows)
            for c in range(parts):
                part = lax.dot_general(
                    v_ref[at, c * m : (c + 1) * m, :],
                    piece_refs[i * parts + c][...],
                    (((0,), (0,)), ((), ())),
                    preferred_element_type=F32,
                )
                if i == 0 and c == 0:
                    out_ref[...] = refs[0][...] + part if final else part
                else:
                    out_ref[...] += part
        if final:
            refs[2][...] = out_ref[...].astype(BF16)

    full = jax.ShapeDtypeStruct((width, cols), F32)
    return pl.pallas_call(
        kernel,
        out_shape=(full, jax.ShapeDtypeStruct((width, cols), BF16)) if final else full,
        in_specs=whole_specs(1 + len(flat) + int(final)),
        out_specs=tuple(whole_specs(2)) if final else whole_specs(1)[0],
        compiler_params=PARAMS,
        cost_estimate=cost(2 * len(places) * n * width * cols, 4 * len(places) * n * width),
        name="coef_product",
    )(v_pieces, *flat, *([before] if final else []))


def masked_coef(kept_ref, part_ref, taken_ref):
    kept = jnp.max(kept_ref[...])
    heights = lax.broadcasted_iota(jnp.int32, part_ref.shape, 0)
    return jnp.where(heights < kept, part_ref[...] + taken_ref[...].astype(F32), 0.0).astype(BF16)


def update_ends(step, kept, part, taken, residual, factor, n, parts):
    half, cols = residual.shape
    m = n // parts

    def kernel(kept_ref, part_ref, taken_ref, residual_ref, u_ref, *refs):
        end_refs, coef_ref = refs[: 2 * parts], refs[2 * parts]
        coef = masked_coef(kept_ref, part_ref, taken_ref)
        coef_ref[...] = coef
        for i, start in enumerate((0, half - n)):
            span = slice(start, start + n)
            change = jnp.dot(u_ref[0, step, span, :], coef, preferred_element_type=F32)
            rounded = (residual_ref[span, :].astype(F32) - change).astype(BF16)
            for c in range(parts):
                end_refs[i * parts + c][...] = rounded[c * m : (c + 1) * m, :]

    ends = (jax.ShapeDtypeStruct((m, cols), BF16),) * (2 * parts)
    return pl.pallas_call(
        kernel,
        out_shape=ends + (jax.ShapeDtypeStruct(part.shape, BF16),),
        in_specs=whole_specs(5),
        out_specs=tuple(whole_specs(2 * parts + 1)),
        compiler_params=PARAMS,
        cost_estimate=cost(4 * n * part.shape[0] * cols, 8 * n * cols),
        name="update_ends",
    )(kept[step], part, taken, residual, factor)


def update_whole(step, coef, residual, factor, n):
    half, cols = residual.shape

    def kernel(coef_ref, residual_ref, u_ref, out_ref, rounded_ref):
        for start in range(0, half, n):
            span = slice(start, start + n)
            change = jnp.dot(u_ref[0, step, span, :], coef_ref[...], preferred_element_type=F32)
            value = residual_ref[span, :].astype(F32) - change
            out_ref[span, :] = value
            rounded_ref[span, :] = value.astype(BF16)

    return pl.pallas_call(
        kernel,
        out_shape=(jax.ShapeDtypeStruct((half, cols), F32), jax.ShapeDtypeStruct((half, cols), BF16)),
        in_specs=whole_specs(3),
        out_specs=tuple(whole_specs(2)),
        compiler_params=PARAMS,
        cost_estimate=cost(2 * half * coef.shape[0] * cols, 8 * half * cols),
        name="update_whole",
    )(coef, residual, factor)


def update_last(step, kept, part, taken, residual, factor, n):
    half, cols = residual.shape
    rows = half // n

    def kernel(kept_ref, part_ref, taken_ref, residual_ref, u_ref, out_ref, whole_ref, sems):
        coef = masked_coef(kept_ref, part_ref, taken_ref)
        copies = []
        for i in range(rows):
            span = slice(i * n, (i + 1) * n)
            change = jnp.dot(u_ref[0, step, span, :], coef, preferred_element_type=F32)
            whole_ref[span, :] = residual_ref[span, :].astype(F32) - change
            copies.append(pltpu.make_async_copy(whole_ref.at[span, :], out_ref.at[span, :], sems.at[i]))
            copies[-1].start()
        for copy in copies:
            copy.wait()

    return pl.pallas_call(
        kernel,
        out_shape=jax.ShapeDtypeStruct((half, cols), F32),
        in_specs=whole_specs(5),
        out_specs=pl.BlockSpec(memory_space=pl.ANY),
        scratch_shapes=[pltpu.VMEM((half, cols), F32), pltpu.SemaphoreType.DMA((rows,))],
        compiler_params=PARAMS,
        cost_estimate=cost(2 * half * part.shape[0] * cols, 8 * half * cols),
        name="update_last",
    )(kept[step], part, taken, residual, factor)


def ring_steps(rows, half, n):
    ring = ring_order(rows)
    links = [(ring[i], ring[(i + 1) % rows]) for i in range(rows)]
    forward = [(2 * a + tile, 2 * b + 1 - tile) for a, b in links for tile in range(2)]
    backward = [(b, a) for a, b in forward]
    reach = rows // 2
    m = n // PARTS

    def hop_to(value, way):
        return lax.ppermute(value, ("row", "tile"), way)

    def gather(piece):
        got = [None] * rows
        got[0] = down = up = piece
        for hop in range(1, reach):
            got[hop] = down = [hop_to(part, forward) for part in down]
            got[rows - hop] = up = [hop_to(part, backward) for part in up]
        sides = [(down, forward) if c % 2 == 0 else (up, backward) for c in range(PARTS)]
        got[reach] = [hop_to(side[c], way) for c, (side, way) in enumerate(sides)]
        return got

    def spread(held, first, last, masks, step):
        down = [hop_to(part, forward) for part in first]
        up = [hop_to(part, backward) for part in last]
        if step == 0:
            down[0], masks = lax.optimization_barrier((down[0], masks))
        downs, ups = [down], [up]

        def rows_of(start):
            return (held[start : start + m], 0) if step == 0 else (held, start)

        for hop in range(1, rows - 1):
            down, up = list(down), list(up)
            for c in range(PARTS):
                own = pick(masks[step], *rows_of(hop * n + c * m), down[c])
                down[c] = hop_to(own, forward)
                own = pick(masks[step], *rows_of((rows - 1 - hop) * n + c * m), up[c])
                up[c] = hop_to(own, backward)
            downs.append(down)
            ups.append(up)
        return downs, ups, masks

    def local(right_side, diag_inverse, u_factor, v_factor, ranks, pivots):
        steps = pivots.shape[0]
        held = residual = right_side[0]
        cols, width = held.shape[1], u_factor.shape[3]
        masks, distances, kept, sides = device_facts(pivots, ranks, (m, cols), rows)
        diag_other = lax.ppermute(diag_inverse, "tile", SWAP)
        first = [held[c * m : (c + 1) * m] for c in range(PARTS)]
        final = [held[half - n + c * m : half - n + (c + 1) * m] for c in range(PARTS)]
        solved = []
        for step in range(steps):
            downs, ups, masks = spread(held, first, final, masks, step)
            take, so_far, early = diag_early(step, pivots, diag_other, held, downs[:-1], ups[:-1])
            ends = (downs[-1], ups[-1])
            other = diag_late(step, take, False, distances, so_far, early, *ends, BF16, "diag_give")
            mine = diag_late(step, diag_inverse, True, distances, so_far, None, *ends, F32, "diag_keep")
            total = mine + lax.ppermute(other, "tile", SWAP).astype(F32)
            x = [total[c * m : (c + 1) * m].astype(BF16) for c in range(PARTS)]
            solved += x
            if step == 0:
                x, v_rows = lax.optimization_barrier((x, v_factor[0]))
                v_pairs = v_rows.reshape(steps, reach, 2, n, width)
                upper = sides[None, :, :, None] == 1
                v_keep = jnp.where(upper, v_pairs[:, :, 1], v_pairs[:, :, 0])
                v_give = jnp.where(upper, v_pairs[:, :, 0], v_pairs[:, :, 1])
                v_take = lax.ppermute(v_give, "tile", SWAP)
                v_pieces = jnp.concatenate([v_keep, v_take], 1)
            got = gather(x)
            part = coef_product(v_pieces[step], [k for k in range(rows) if k != reach], got)
            part, sent = coef_product(v_pieces[step], [reach], got, part)
            taken = lax.ppermute(sent, "tile", SWAP)
            if step == steps - 1:
                out = update_last(step, kept, part, taken, residual, u_factor, n)
                continue
            *ends, coef = update_ends(step, kept, part, taken, residual, u_factor, n, PARTS)
            first, final = ends[:PARTS], ends[PARTS:]
            residual, held = update_whole(step, coef, residual, u_factor, n)
        return jnp.concatenate(solved).reshape(steps, n, cols), out[None]

    return local


def gathered_steps(right_side, diag_inverse, u_factor, v_factor, ranks, pivots):
    residual = right_side[0].astype(F32)
    half = residual.shape[0]
    heights = lax.broadcasted_iota(jnp.int32, (u_factor.shape[3], 1), 0)
    me, tile = lax.axis_index("row"), lax.axis_index("tile")
    solved = []
    for step in range(pivots.shape[0]):
        current = residual.astype(BF16)
        held = lax.psum(jnp.where(me == pivots[step], current, jnp.zeros_like(current)), "row")
        other = lax.ppermute(held, "tile", SWAP)
        pivot = jnp.where(tile == 0, jnp.concatenate([held, other]), jnp.concatenate([other, held]))
        x = jnp.dot(diag_inverse[step], pivot, preferred_element_type=F32).astype(BF16)
        solved.append(x)
        x_all = lax.all_gather(x, ("row", "tile"), axis=0, tiled=True)
        x_mine = lax.dynamic_slice_in_dim(x_all, tile * half, half, 0)
        part = lax.dot_general(
            v_factor[0, step], x_mine, (((0,), (0,)), ((), ())), preferred_element_type=F32
        )
        coef = part + lax.ppermute(part, "tile", SWAP)
        finished = jnp.any(pivots[: step + 1] == me)
        kept = jnp.where(finished, 0, ranks[0, step])
        coef = jnp.where(heights < kept, coef, F32(0.0)).astype(BF16)
        residual = residual - jnp.dot(u_factor[0, step], coef, preferred_element_type=F32)
    return jnp.stack(solved), residual[None]


def solution(mesh):
    rows = mesh.shape["row"]

    def local(right_side, diag_inverse, *others):
        half, n = right_side.shape[1], diag_inverse.shape[1]
        short = rows % 2 == 0 and rows <= MOST_HOPS and n % LANES == 0 and half == rows * n
        run = ring_steps(rows, half, n) if short else gathered_steps
        return run(right_side, diag_inverse, *others)

    in_specs = (
        P(("grp", "row"), "tile", None),
        P(None, ("row", "tile"), None),
        P("row", None, "tile", None),
        P("row", None, "tile", None),
        P("row", None),
        P(),
    )
    out_specs = (P(None, ("grp", "row", "tile"), None), P(("grp", "row"), "tile", None))
    return jax.shard_map(local, mesh=mesh, in_specs=in_specs, out_specs=out_specs, check_vma=False)
```
